128 devices in a mesh: req: 8 (over x, z_hi), mlp: 16 (over y, z_lo, core).
Axes of the slice: x: 4, y: 4, z: 4 (z_hi: 2, z_lo: 2; z = z_hi * 2 + z_lo), core: 2. Of those that a mesh axis runs over, the one named last changes fastest.
Arguments:
- tokens: bfloat16 [8, 1024, 2048], P('req', None, 'mlp'), may hold values from -6 to 6
- lengths: int32 [8], replicated, may hold values from 1 to 1024, 3072 in all
- retention_gain: float32 [2048], replicated, may hold values from 0.1 to 1.9
- forward_gain: float32 [2048], replicated, may hold values from 0.1 to 1.9
- query_weight: float32 [2048, 2048], P('mlp'), may hold values from -0.125 to 0.125
- key_weight: float32 [2048, 2048], P('mlp'), may hold values from -0.125 to 0.125
- value_weight: float32 [2048, 4096], P('mlp'), may hold values from -0.125 to 0.125
- gate_weight: float32 [2048, 4096], P('mlp'), may hold values from -0.125 to 0.125
- output_weight: float32 [4096, 2048], P('mlp'), may hold values from -0.125 to 0.125
- swish_weight: float32 [2048, 4096], P('mlp'), may hold values from -0.125 to 0.125
- up_weight: float32 [2048, 4096], P('mlp'), may hold values from -0.125 to 0.125
- down_weight: float32 [4096, 2048], P('mlp'), may hold values from -0.125 to 0.125
Outputs:
- prefill_out: bfloat16 [8, 1024, 2048], P('req', None, 'mlp')
The draws below stay inside these ranges and needn't reach their ends.
Inputs may be any that keep to these rules, and one draw needn't show every extreme that they name: Request b is served by owner b of req. The lengths add up to exactly 3072; the longest is exactly 1024.
All inputs are finite; a program needn't handle non-finite values.
Results may differ from the reference program's by a relative error of at most 0.028.
Values may be sent and summed in bfloat16 or wider, within the bound.
A program may use at most 128 MiB of HBM per device.

```python
import math
import jax
import jax.numpy as jnp
import numpy as np
from jax import lax

D = 2048
H = 8
DK = 256
DV = 512
FF = 4096
SPAN = 256
LMAX = 1024
REQS = 8
TOTAL = 3072
N_MLP = 16


def strengthened(drawn, stream_key, source, target, blocks, factor):
    def block_of(axis_at):
        return (jnp.arange(drawn.shape[axis_at]) // (drawn.shape[axis_at] // blocks)).reshape((-1,) + (1,) * (drawn.ndim - 1 - axis_at))

    first = jax.random.permutation(stream_key, blocks)[block_of(target)]
    second = (block_of(target) + blocks // 2) % blocks
    return jnp.where((block_of(source) == first) | (block_of(source) == second), factor * drawn, drawn)


def levels(own_key, dims, split, least, largest):
    def one(dim, shards_of):
        heights = jax.random.uniform(jax.random.fold_in(jax.random.fold_in(own_key, 6), dim), (shards_of,), jnp.float32, least / len(split), largest / len(split))
        return jnp.repeat(jnp.exp(heights), dims[dim] // shards_of).reshape((-1,) + (1,) * (len(dims) - dim - 1))

    loudness = one(*split[0])
    for cut in split[1:]:
        loudness = loudness * one(*cut)
    return loudness


def length_profile(count, total, reach, skew):
    loads = [(1 << 20) // math.isqrt(standing ** skew) + 1 for standing in range(2, count + 1)]
    spare, counts = total - reach - (count - 1), [1] * (count - 1)
    while spare > 0:
        movable = [i for i in range(count - 1) if counts[i] < reach]
        mass, budget = sum([loads[i] for i in movable]), spare
        for i in movable:
            addition = min(reach - counts[i], max(1, budget * loads[i] // mass), spare)
            counts[i] = counts[i] + addition
            spare = spare - addition
    return np.array([reach] + counts)


def ragged_sizes(stream_key, amount, total, limit, skew):
    if amount == 2:
        one = jax.random.randint(stream_key, (), max(1, total - limit), min(limit, total - 1) + 1)
        return jnp.stack([one, total - one])
    sizes = jnp.asarray(length_profile(amount, total, limit, skew), jnp.int32)
    couples = (amount - 1) // 2
    giver, receiver = sizes[1:1 + 2 * couples:2], sizes[2:2 + 2 * couples:2]
    room = jnp.minimum(giver - 1, limit - receiver)
    moved = jax.random.randint(jax.random.fold_in(stream_key, 1), (couples,), 0, 1 << 20) % (room + 1)
    sizes = sizes.at[1:1 + 2 * couples:2].set(giver - moved).at[2:2 + 2 * couples:2].set(receiver + moved)
    return sizes[jax.random.permutation(jax.random.fold_in(stream_key, 2), amount)]


def normal_values(key, dims, scale, reach, shards=(), kind=jnp.bfloat16):
    entries = jax.random.normal(key, dims, jnp.float32) * scale
    if len(shards) > 0:
        entries = levels(key, dims, shards, -0.22, 0.18) * entries
    return jnp.clip(entries, min=-reach, max=reach).astype(kind)


def bell_draw_with(own_key, dims, spread, bound, pieces, heavy, held_as=jnp.bfloat16):
    result = spread * jax.random.normal(own_key, dims, jnp.float32)
    if pieces:
        result = result * levels(own_key, dims, pieces, -0.22, 0.18)
    return jnp.clip(strengthened(result, jax.random.fold_in(own_key, 3), *heavy), -bound, bound).astype(held_as)


def setup_inputs(seed: int = 0) -> dict:
    key_of = jax.random.split(jax.random.key(seed), 13)
    return {
        "tokens": normal_values(key_of[0], (REQS, LMAX, D), 1.0, 6.0, ((0, 8), (2, 16))),
        "lengths": ragged_sizes(key_of[1], REQS, TOTAL, LMAX, 2).astype(jnp.int32),
        "retention_gain": jnp.clip(1.0 + 0.18 * jax.random.normal(key_of[2], (D,), jnp.float32), 0.1, 1.9),
        "forward_gain": jnp.clip(1.0 + 0.18 * jax.random.normal(key_of[3], (D,), jnp.float32), 0.1, 1.9),
        "query_weight": normal_values(key_of[4], (D, H * DK), D ** -0.5, 0.125, ((0, 16),), jnp.float32),
        "key_weight": normal_values(key_of[5], (D, H * DK), D ** -0.5, 0.125, ((0, 16),), jnp.float32),
        "value_weight": normal_values(key_of[6], (D, H * DV), D ** -0.5, 0.125, ((0, 16),), jnp.float32),
        "gate_weight": normal_values(key_of[7], (D, H * DV), D ** -0.5, 0.125, ((0, 16),), jnp.float32),
        "output_weight": bell_draw_with(key_of[8], (H * DV, D), (H * DV) ** -0.5, 0.125, ((0, 16),), (0, 1, 16, 2.0), jnp.float32),
        "swish_weight": normal_values(key_of[9], (D, FF), D ** -0.5, 0.125, ((0, 16),), jnp.float32),
        "up_weight": normal_values(key_of[10], (D, FF), D ** -0.5, 0.125, ((0, 16),), jnp.float32),
        "down_weight": bell_draw_with(key_of[11], (FF, D), FF ** -0.5, 0.125, ((0, 16),), (0, 1, 16, 2.0), jnp.float32),
    }


epsilon = 1e-05
highest = lax.Precision.HIGHEST

def norm_rows(token_rows, gain_vector):
    values = token_rows.astype(jnp.float32)
    row_scale = lax.rsqrt(lax.optimization_barrier(jnp.mean(values * values, axis=-1, keepdims=True)) + epsilon)
    return (values * row_scale * gain_vector).astype(jnp.bfloat16)

def decay_rates():
    return 1.0 - jnp.exp2(-5.0 - jnp.arange(H).astype(jnp.float32))

def retain(query_rows, key_rows, value_rows):
    decay_rate = decay_rates()
    count_blocks = LMAX // SPAN
    query_blocks = query_rows.astype(jnp.float32).reshape(count_blocks, SPAN, H, DK)
    key_blocks = key_rows.astype(jnp.float32).reshape(count_blocks, SPAN, H, DK)
    value_blocks = value_rows.astype(jnp.float32).reshape(count_blocks, SPAN, H, DV)
    position = jnp.arange(SPAN)
    distance = position[:, None] - position[None, :]
    powers = jnp.power(decay_rate[:, None, None], jnp.maximum(distance, 0).astype(jnp.float32)[None])
    within_mask = jnp.where(distance[None] >= 0, powers, 0.0)
    leading = jnp.power(decay_rate[None, :], (position + 1).astype(jnp.float32)[:, None])
    trailing = jnp.power(decay_rate[None, :], (SPAN - 1 - position).astype(jnp.float32)[:, None])
    span_decay = jnp.power(decay_rate, jnp.float32(SPAN))

    def advance(memory, blocks_in):
        query_block, key_block, value_block = blocks_in
        scores = jnp.einsum('ihd,jhd->hij', query_block, key_block, precision=highest) * within_mask
        weights = lax.optimization_barrier(scores.astype(jnp.bfloat16)).astype(jnp.float32)
        within_sum = jnp.einsum('hij,jhv->ihv', weights, value_block, precision=highest)
        across_sum = jnp.einsum('ihd,hdv->ihv', query_block, memory, precision=highest) * leading[:, :, None]
        decayed = key_block * trailing[:, :, None]
        memory = memory * span_decay[:, None, None] + jnp.einsum('jhd,jhv->hdv', decayed, value_block, precision=highest)
        return (memory, within_sum + across_sum)
    start_memory = jnp.zeros((H, DK, DV), jnp.float32)
    retained = lax.scan(advance, start_memory, (query_blocks, key_blocks, value_blocks))[1]
    return retained.reshape(LMAX, H, DV)

def blocked_sum(left_rows, right_server):
    block_cols = left_rows.shape[1] // N_MLP
    left_blocks = left_rows.reshape(left_rows.shape[0], N_MLP, block_cols).transpose(1, 0, 2)
    right_blocks = right_server.reshape(N_MLP, block_cols, right_server.shape[1])

    def add_block(total, pair):
        left_block, right_block = pair
        part = jnp.dot(left_block, right_block, preferred_element_type=jnp.float32)
        rounded = lax.optimization_barrier(part.astype(jnp.bfloat16)).astype(jnp.float32)
        return (total + rounded, None)
    start = jnp.zeros((left_rows.shape[0], right_server.shape[1]), jnp.float32)
    return lax.scan(add_block, start, (left_blocks, right_blocks))[0]

def reference(tokens, lengths, retention_gain, forward_gain, query_weight, key_weight, value_weight, gate_weight, output_weight, swish_weight, up_weight, down_weight):
    query_server = query_weight.astype(jnp.bfloat16)
    key_server = key_weight.astype(jnp.bfloat16)
    value_server = value_weight.astype(jnp.bfloat16)
    gate_server = gate_weight.astype(jnp.bfloat16)
    output_server = output_weight.astype(jnp.bfloat16)
    swish_server = swish_weight.astype(jnp.bfloat16)
    up_server = up_weight.astype(jnp.bfloat16)
    down_server = down_weight.astype(jnp.bfloat16)

    def one_request(item):
        token_rows, length = item
        normed = norm_rows(token_rows, retention_gain)
        query_rows = jnp.dot(normed, query_server, preferred_element_type=jnp.float32).astype(jnp.bfloat16)
        key_rows = (jnp.dot(normed, key_server, preferred_element_type=jnp.float32) * DK ** (-0.5)).astype(jnp.bfloat16)
        value_rows = jnp.dot(normed, value_server, preferred_element_type=jnp.float32).astype(jnp.bfloat16)
        gate_rows = jnp.dot(normed, gate_server, preferred_element_type=jnp.float32).astype(jnp.bfloat16)
        retained = retain(query_rows.reshape(LMAX, H, DK), key_rows.reshape(LMAX, H, DK), value_rows.reshape(LMAX, H, DV))
        row_mean = lax.optimization_barrier(jnp.mean(retained, axis=-1, keepdims=True))
        centered = retained - row_mean
        row_var = lax.optimization_barrier(jnp.mean(centered * centered, axis=-1, keepdims=True))
        grouped = (centered * lax.rsqrt(row_var + epsilon)).reshape(LMAX, H * DV)
        gated = (jax.nn.silu(gate_rows.astype(jnp.float32)) * grouped).astype(jnp.bfloat16)
        stream = (token_rows.astype(jnp.float32) + blocked_sum(gated, output_server)).astype(jnp.bfloat16)
        normed_stream = norm_rows(stream, forward_gain)
        swish_part = jnp.dot(normed_stream, swish_server, preferred_element_type=jnp.float32)
        up_part = jnp.dot(normed_stream, up_server, preferred_element_type=jnp.float32)
        hidden = (jax.nn.silu(swish_part) * up_part).astype(jnp.bfloat16)
        finished = stream.astype(jnp.float32) + blocked_sum(hidden, down_server)
        live_rows = jnp.arange(LMAX) < length
        return jnp.where(live_rows[:, None], finished, 0.0).astype(jnp.bfloat16)
    return lax.map(one_request, (tokens, lengths))
```

```python
import functools
import jax
import jax.numpy as jnp
from jax import lax
from jax.experimental import pallas as pl
from jax.experimental.pallas import tpu as pltpu
from jax.sharding import PartitionSpec as P

H = 8
DK = 256
DV = 512
SPAN = 256
LMAX = 1024
BLK = 128
CUT = 448
LOA = (0, 224)
HIA = (224, 448)
ALLA = (0, 448)
LOB = (448, 736)
HIB = (736, 1024)
ALLB = (448, 1024)
REST = [(2, 1), (2, 0), (1, 1), (3, 1), (1, 0), (3, 0), (0, 1)]

epsilon = 1e-05
bf16 = jnp.bfloat16
f32 = jnp.float32


def rows_of(span):
    return pl.ds(span[0], span[1] - span[0])


class Place:
    def __init__(self):
        self.req = lax.axis_index("req")
        self.me = lax.axis_index("mlp")
        self.x = self.req // 2
        self.zh = self.req % 2
        self.y = self.me // 4
        self.z = (self.me // 2) % 2
        self.c = self.me % 2

    def member(self, dy, zr, cc):
        return ((self.y + dy + 4) % 4) * 4 + ((self.z + zr) % 2) * 2 + (self.c + cc) % 2

    def near(self, dy, zr, cc):
        return (self.req, self.member(dy, zr, cc))

    def across(self, dx):
        return (((self.x + dx + 4) % 4) * 2 + self.zh, self.me)


class Mover:
    def __init__(self, send, recv):
        self.send, self.recv, self.count, self.sent = send, recv, 0, []

    def plan(self, src, dst, device):
        i = self.count
        self.count += 1
        return pltpu.make_async_remote_copy(
            src_ref=src, dst_ref=dst, send_sem=self.send.at[i], recv_sem=self.recv.at[i],
            device_id=device, device_id_type=pl.DeviceIdType.MESH,
        )

    def go(self, src, dst, device):
        copy = self.plan(src, dst, device)
        copy.start()
        self.sent.append(copy)
        return copy

    def drain(self):
        for copy in self.sent:
            copy.wait_send()
        self.sent = []


def greet(devices):
    barrier = pltpu.get_barrier_semaphore()
    for device in devices:
        pl.semaphore_signal(barrier, inc=1, device_id=device, device_id_type=pl.DeviceIdType.MESH)
    pl.semaphore_wait(barrier, len(devices))


def column(member):
    return pl.ds(pl.multiple_of(member * BLK, BLK), BLK)


class Gather:
    def __init__(self, place, mover, full):
        self.p, self.m, self.full = place, mover, full
        self.pend = []

    def at(self, span, dy, zr, cc=0):
        return self.full.at[rows_of(span), column(self.p.member(dy, zr, cc))]

    def pass_on(self, span, dy, zr, targets):
        place = self.p
        ref = self.at(span, dy, zr)
        out = []
        for step in targets:
            device = {"r": place.near(1, 0, 0), "l": place.near(-1, 0, 0),
                      "z": place.near(0, 1, 0), "c": place.near(0, 0, 1)}[step]
            out.append(self.m.go(ref, ref, device))
        return out

    def start_a(self):
        self.a = self.pass_on(ALLA, 0, 0, "rlzc")

    def start_b(self):
        self.b = self.pass_on(ALLB, 0, 0, "zrlc")

    def first(self):
        ar, al, az, ac = self.a
        bz, br, bl, bc = self.b
        self.pend += [ac, bc]
        bz.wait_recv()
        self.zb = self.pass_on(ALLB, 0, 1, "rlc")
        ar.wait_recv()
        self.al1 = self.pass_on(LOA, -1, 0, "r") + self.pass_on(ALLA, -1, 0, "zc")
        al.wait_recv()
        self.ar1 = self.pass_on(HIA, 1, 0, "l") + self.pass_on(ALLA, 1, 0, "zc")
        br.wait_recv()
        self.bl1 = self.pass_on(LOB, -1, 0, "r") + self.pass_on(ALLB, -1, 0, "c")
        bl.wait_recv()
        self.br1 = self.pass_on(HIB, 1, 0, "l") + self.pass_on(ALLB, 1, 0, "c")
        az.wait_recv()
        self.pend += self.pass_on(ALLA, 0, 1, "c")

    def second(self):
        lo, az, ac = self.al1
        hi, az2, ac2 = self.ar1
        self.pend += [ac, ac2]
        lo.wait_recv()
        o1 = self.pass_on(LOA, -2, 0, "zc")
        hi.wait_recv()
        o2 = self.pass_on(HIA, 2, 0, "zc")
        zr, zl, zc = self.zb
        self.pend += [zc]
        zr.wait_recv()
        zlo = self.pass_on(LOB, -1, 1, "r")
        self.pend += self.pass_on(ALLB, -1, 1, "c")
        zl.wait_recv()
        zhi = self.pass_on(HIB, 1, 1, "l")
        self.pend += self.pass_on(ALLB, 1, 1, "c")
        az.wait_recv()
        self.pend += self.pass_on(ALLA, -1, 1, "c")
        az2.wait_recv()
        self.pend += self.pass_on(ALLA, 1, 1, "c")
        blo, bc = self.bl1
        bhi, bc2 = self.br1
        self.pend += [bc, bc2]
        blo.wait_recv()
        self.pend += self.pass_on(LOB, -2, 0, "c")
        bhi.wait_recv()
        self.pend += self.pass_on(HIB, 2, 0, "c")
        self.pend += [o1[1], o2[1]]
        o1[0].wait_recv()
        self.pend += self.pass_on(LOA, -2, 1, "c")
        o2[0].wait_recv()
        self.pend += self.pass_on(HIA, 2, 1, "c")
        zlo[0].wait_recv()
        self.pend += self.pass_on(LOB, -2, 1, "c")
        zhi[0].wait_recv()
        self.pend += self.pass_on(HIB, 2, 1, "c")

    def finish(self):
        for copy in self.pend:
            copy.wait_recv()
        self.pend = []


GATHER_COPIES = 44


def hand_kernel(tokens, query, key, value, gate, swish, up, full, first, second,
                quarter, own, pack1, pack2, mate1, mate2, local, send, recv):
    place = Place()
    mover = Mover(send, recv)
    x, me, c = place.x, place.me, place.c
    chip = me // 2
    loads = []

    def load(src, dst):
        copy = pltpu.make_async_copy(src, dst, local.at[len(loads)])
        copy.start()
        loads.append(copy)

    shares = ((query, 0), (key, 2048), (value, 4096), (gate, 8192), (swish, 12288), (up, 16384))
    part = pl.ds(pl.multiple_of(x * 32, 32), 32)
    for ref, at in shares:
        load(ref.at[part, :], quarter.at[:, pl.ds(at, ref.shape[1])])
    at = 0
    for ref, _ in shares:
        wide = ref.shape[1] // 8
        load(ref.at[:, pl.ds(pl.multiple_of(chip * wide, 128), wide)], own.at[:, pl.ds(at, wide)])
        at += wide
    load(tokens, full.at[:, column(me)])
    peers = [place.near(dy, zr, cc) for dy, zr in REST for cc in (0, 1)] + [place.near(0, 0, 1)]
    greet(peers + [place.across(1), place.across(-1)])
    for copy in loads[:6]:
        copy.wait()
    for d in range(16):
        pack1[d, :, 0:256] = quarter[:, (d % 2) * 2048 + (d // 2) * 256:][:, :256].astype(bf16)
        for t in (1, 2):
            pack1[d, :, t * 256:(t + 1) * 256] = quarter[:, t * 4096 + d * 256:][:, :256].astype(bf16)
        for t in (3, 4):
            pack2[d, :, (t - 3) * 256:(t - 2) * 256] = quarter[:, t * 4096 + d * 256:][:, :256].astype(bf16)

    def lot(member, slot, low=0, high=32):
        return pl.ds(pl.multiple_of(member * 128 + slot * 32 + low, 16), high - low)

    rel = [(dy, zr, cc) for dy, zr in REST for cc in (0, 1)]

    def hand_out(pack, out):
        return [mover.go(pack.at[place.member(*r)], out.at[lot(me, x), :], place.near(*r)) for r in rel]

    one = hand_out(pack1, first)
    for copy in loads[6:12]:
        copy.wait()
    full_own = pl.ds(pl.multiple_of(me * 128, 128), 128)

    def mine(core, t):
        base = (0, 512, 1024, 1536, 2048)[t]
        return own[:, pl.ds(pl.multiple_of(base + core * 256, 128), 256)].astype(bf16)

    for t in range(3):
        mate1[:, t * 256:(t + 1) * 256] = mine(1 - c, t)
        first[full_own, t * 256:(t + 1) * 256] = mine(c, t)
    for t in range(2):
        mate2[:, t * 256:(t + 1) * 256] = mine(1 - c, t + 3)
        second[full_own, t * 256:(t + 1) * 256] = mine(c, t + 3)
    partner = [mover.go(mate1, first.at[full_own, :], place.near(0, 0, 1)),
               mover.go(mate2, second.at[full_own, :], place.near(0, 0, 1))]
    loads[12].wait()
    gather = Gather(place, mover, full)
    gather.start_a()
    gather.start_b()
    two = hand_out(pack2, second)

    def origin(r):
        return place.member(-r[0], r[1], r[2])

    def spread(copies, out):
        got = []
        for r, copy in zip(rel, copies):
            copy.wait_recv()
            ref = out.at[lot(origin(r), x), :]
            got.append((mover.go(ref, ref, place.across(1)), mover.go(ref, ref, place.across(-1))))
        return got

    def onward(got, out):
        halves = []
        for r, (right, left) in zip(rel, got):
            right.wait_recv()
            ref = out.at[lot(origin(r), (x + 3) % 4, 0, 16), :]
            halves.append(mover.go(ref, ref, place.across(1)))
            left.wait_recv()
            ref = out.at[lot(origin(r), (x + 1) % 4, 16, 32), :]
            halves.append(mover.go(ref, ref, place.across(-1)))
        return halves

    got1 = spread(one, first)
    gather.first()
    half1 = onward(got1, first)
    gather.second()
    got2 = spread(two, second)
    half2 = onward(got2, second)
    gather.finish()
    for copy in half1 + half2 + partner:
        copy.wait_recv()
    mover.drain()


HAND_COPIES = GATHER_COPIES + 2 * 14 * 5 + 2


def hand_over(tokens, *weights):
    vmem = pl.BlockSpec(memory_space=pltpu.VMEM)
    hbm = pl.BlockSpec(memory_space=pl.ANY)
    return pl.pallas_call(
        hand_kernel,
        name="hand_over",
        out_shape=(
            jax.ShapeDtypeStruct((LMAX, 2048), bf16),
            jax.ShapeDtypeStruct((2048, 768), bf16),
            jax.ShapeDtypeStruct((2048, 512), bf16),
        ),
        in_specs=[vmem] + [hbm] * 6,
        out_specs=(vmem, vmem, vmem),
        scratch_shapes=[
            pltpu.VMEM((32, 20480), f32),
            pltpu.VMEM((128, 2560), f32),
            pltpu.VMEM((16, 32, 768), bf16),
            pltpu.VMEM((16, 32, 512), bf16),
            pltpu.VMEM((128, 768), bf16),
            pltpu.VMEM((128, 512), bf16),
            pltpu.SemaphoreType.DMA((13,)),
            pltpu.SemaphoreType.DMA((HAND_COPIES,)),
            pltpu.SemaphoreType.DMA((HAND_COPIES,)),
        ],
        compiler_params=pltpu.CompilerParams(
            collective_id=0, has_side_effects=True, vmem_limit_bytes=60 * 2**20
        ),
    )(tokens, *weights)


def sum_kernel(act, weight, base, out, wide, wpar, S, RA, RLO, RHI, RL, RR, RZ, local, send, recv):
    place = Place()
    mover = Mover(send, recv)
    loads = []

    def load(src, dst):
        copy = pltpu.make_async_copy(src, dst, local.at[len(loads)])
        copy.start()
        loads.append(copy)

    order = [(dy, zr) for zr in (0, 1) for dy in range(4)]
    load(act, wide.at[:, pl.ds(0, 256)])
    for i, (dy, zr) in enumerate(order):
        load(weight.at[:, column(place.member(dy, zr, 0))], wpar.at[pl.ds(0, 256), pl.ds(i * 128, 128)])
    mate = place.near(0, 0, 1)
    right, left, over = place.near(1, 0, 0), place.near(-1, 0, 0), place.near(0, 1, 0)
    greet([mate, right, left, over])
    given = [mover.go(act, wide.at[:, pl.ds(256, 256)], mate)]
    for i, (dy, zr) in enumerate(order):
        given.append(mover.go(weight.at[:, column(place.member(dy, zr, 1))],
                              wpar.at[pl.ds(256, 256), pl.ds(i * 128, 128)], mate))
    for copy in loads:
        copy.wait()
    for copy in given:
        copy.wait_recv()

    def multiply(span):
        def step(i, carry):
            row = pl.ds(pl.multiple_of(span[0] + i * 64, 64), 64)
            part = jnp.dot(wide[row, :], wpar[...], preferred_element_type=f32).astype(bf16)
            for j in range(8):
                S[j, row, :] = part[:, j * 128:(j + 1) * 128]
            return carry

        lax.fori_loop(0, (span[1] - span[0]) // 64, step, 0)

    def piece(zr, dy, span):
        return S.at[zr * 4 + dy, rows_of(span), :]

    def add(zr, dy, span, *others):
        total = S[zr * 4 + dy, rows_of(span), :].astype(f32)
        for other in others:
            total = total + other.astype(f32)
        S[zr * 4 + dy, rows_of(span), :] = total.astype(bf16)

    def inB(ref, span, *lead):
        return ref[lead + (pl.ds(span[0] - CUT, span[1] - span[0]), slice(None))]

    multiply(ALLA)
    za = {dy: mover.go(piece(1, dy, ALLA), RA.at[dy], over) for dy in (2, 1, 3, 0)}
    multiply(ALLB)
    lo, hi = {}, {}
    for zr in (1, 0):
        lo[zr] = mover.go(piece(zr, 2, LOB), RLO.at[zr, rows_of((224, 512)), :], right)
        hi[zr] = mover.go(piece(zr, 2, HIB), RHI.at[zr, rows_of((224, 512)), :], left)
    toR, toL = {}, {}
    for zr in (1, 0):
        lo[zr].wait_recv()
        add(zr, 1, LOB, RLO[zr, 224:512, :])
        toR[zr] = mover.go(piece(zr, 1, ALLB), RL.at[zr, rows_of(ALLB), :], right)
        hi[zr].wait_recv()
        add(zr, 3, HIB, RHI[zr, 224:512, :])
        toL[zr] = mover.go(piece(zr, 3, ALLB), RR.at[zr, rows_of(ALLB), :], left)
        if zr == 1:
            za[2].wait_recv()
            add(0, 2, ALLA, RA[2])
            loA = mover.go(piece(0, 2, LOA), RLO.at[0, rows_of((0, 224)), :], right)
            hiA = mover.go(piece(0, 2, HIA), RHI.at[0, rows_of((0, 224)), :], left)
    za[1].wait_recv()
    add(0, 1, ALLA, RA[1])
    loA.wait_recv()
    add(0, 1, LOA, RLO[0, 0:224, :])
    toRA = mover.go(piece(0, 1, ALLA), RL.at[0, rows_of(ALLA), :], right)
    za[3].wait_recv()
    add(0, 3, ALLA, RA[3])
    hiA.wait_recv()
    add(0, 3, HIA, RHI[0, 0:224, :])
    toLA = mover.go(piece(0, 3, ALLA), RR.at[0, rows_of(ALLA), :], left)
    toR[1].wait_recv()
    toL[1].wait_recv()
    add(1, 0, ALLB, RL[1, CUT:, :], RR[1, CUT:, :])
    zb = mover.go(piece(1, 0, ALLB), RZ, over)
    za[0].wait_recv()
    toRA.wait_recv()
    toLA.wait_recv()

    def final(span, extra):
        rows = rows_of(span)
        total = S[0, rows, :].astype(f32) + RL[0, rows, :].astype(f32) + RR[0, rows, :].astype(f32)
        total = total + extra.astype(f32)
        out[rows, :] = (base[rows, :].astype(f32) + total).astype(bf16)

    final(ALLA, RA[0])
    toR[0].wait_recv()
    toL[0].wait_recv()
    zb.wait_recv()
    final(ALLB, RZ[...])
    mover.drain()


SUM_COPIES = 9 + 4 + 4 + 4 + 2 + 2 + 1


def sum_up(act, weight, base):
    vmem = pl.BlockSpec(memory_space=pltpu.VMEM)
    return pl.pallas_call(
        sum_kernel,
        name="sum_up",
        out_shape=jax.ShapeDtypeStruct((LMAX, BLK), bf16),
        in_specs=[vmem] * 3,
        out_specs=vmem,
        scratch_shapes=[
            pltpu.VMEM((LMAX, 512), bf16),
            pltpu.VMEM((512, LMAX), bf16),
            pltpu.VMEM((8, LMAX, BLK), bf16),
            pltpu.VMEM((4, 448, BLK), bf16),
            pltpu.VMEM((2, 512, BLK), bf16),
            pltpu.VMEM((2, 512, BLK), bf16),
            pltpu.VMEM((2, LMAX, BLK), bf16),
            pltpu.VMEM((2, LMAX, BLK), bf16),
            pltpu.VMEM((576, BLK), bf16),
            pltpu.SemaphoreType.DMA((9,)),
            pltpu.SemaphoreType.DMA((SUM_COPIES,)),
            pltpu.SemaphoreType.DMA((SUM_COPIES,)),
        ],
        compiler_params=pltpu.CompilerParams(
            collective_id=1, has_side_effects=True, vmem_limit_bytes=60 * 2**20
        ),
    )(act, weight, base)


def gather_kernel(rows, full, local, send, recv):
    place = Place()
    mover = Mover(send, recv)
    copy = pltpu.make_async_copy(rows, full.at[:, column(place.me)], local)
    copy.start()
    greet([place.near(0, 0, 1), place.near(1, 0, 0), place.near(-1, 0, 0), place.near(0, 1, 0)])
    copy.wait()
    gather = Gather(place, mover, full)
    gather.start_a()
    gather.start_b()
    gather.first()
    gather.second()
    gather.finish()
    mover.drain()


def gather_up(rows):
    vmem = pl.BlockSpec(memory_space=pltpu.VMEM)
    return pl.pallas_call(
        gather_kernel,
        name="gather_up",
        out_shape=jax.ShapeDtypeStruct((LMAX, 2048), bf16),
        in_specs=[vmem],
        out_specs=vmem,
        scratch_shapes=[
            pltpu.SemaphoreType.DMA,
            pltpu.SemaphoreType.DMA((GATHER_COPIES,)),
            pltpu.SemaphoreType.DMA((GATHER_COPIES,)),
        ],
        compiler_params=pltpu.CompilerParams(
            collective_id=2, has_side_effects=True, vmem_limit_bytes=60 * 2**20
        ),
    )(rows)


def swap_cores(values):
    route = [(i, i ^ 1) for i in range(lax.axis_size("mlp"))]
    return lax.ppermute(values, "mlp", route)


def norm_rows(token_rows, gain_vector):
    values = token_rows.astype(f32)
    row_scale = lax.rsqrt(jnp.mean(values * values, axis=-1, keepdims=True) + epsilon)
    return (values * row_scale * gain_vector).astype(bf16)


def split_pair(values):
    upper = values.astype(bf16)
    lower = (values - upper.astype(f32)).astype(bf16)
    return (upper, lower)


def retain_local(query_rows, key_rows, value_rows, decay_rate, length):
    total_rows = query_rows.shape[0]
    value_cols = value_rows.shape[1]
    position = jnp.arange(SPAN)
    distance = position[:, None] - position[None, :]
    powers = jnp.power(decay_rate, jnp.maximum(distance, 0).astype(f32))
    within_mask = jnp.where(distance >= 0, powers, 0.0)
    leading = jnp.power(decay_rate, (position + 1).astype(f32))
    trailing = jnp.power(decay_rate, (SPAN - 1 - position).astype(f32))
    span_decay = jnp.power(decay_rate, jnp.float32(SPAN))
    live_blocks = (length + SPAN - 1) // SPAN
    contract_rows = (((0,), (0,)), ((), ()))

    def advance(span_index, loop_state):
        memory, output = loop_state
        row_start = span_index * SPAN
        query_block = lax.dynamic_slice_in_dim(query_rows, row_start, SPAN, 0)
        key_block = lax.dynamic_slice_in_dim(key_rows, row_start, SPAN, 0)
        value_block = lax.dynamic_slice_in_dim(value_rows, row_start, SPAN, 0)
        scores = lax.dot_general(
            query_block, key_block, (((1,), (1,)), ((), ())), preferred_element_type=f32
        )
        weights = (scores * within_mask).astype(bf16)
        within_sum = jnp.dot(weights, value_block, preferred_element_type=f32)
        memory_upper, memory_lower = split_pair(memory)
        across_sum = (
            jnp.dot(query_block, memory_upper, preferred_element_type=f32)
            + jnp.dot(query_block, memory_lower, preferred_element_type=f32)
        ) * leading[:, None]
        decayed_upper, decayed_lower = split_pair(key_block.astype(f32) * trailing[:, None])
        update = lax.dot_general(
            decayed_upper, value_block, contract_rows, preferred_element_type=f32
        ) + lax.dot_general(
            decayed_lower, value_block, contract_rows, preferred_element_type=f32
        )
        memory = memory * span_decay + update
        output = lax.dynamic_update_slice_in_dim(output, within_sum + across_sum, row_start, 0)
        return (memory, output)

    start_state = (
        jnp.zeros((DK, value_cols), f32),
        jnp.zeros((total_rows, value_cols), f32),
    )
    return lax.fori_loop(0, live_blocks, advance, start_state)[1]


def body(
    tokens,
    lengths,
    retention_gain,
    forward_gain,
    query_weight,
    key_weight,
    value_weight,
    gate_weight,
    output_weight,
    swish_weight,
    up_weight,
    down_weight,
):
    owner_index = lax.axis_index("req")
    member = lax.axis_index("mlp")
    length = lengths[owner_index]
    token_rows = tokens[0]
    gathered, first, second = hand_over(
        token_rows, query_weight, key_weight, value_weight, gate_weight, swish_weight, up_weight
    )
    normed = norm_rows(gathered, retention_gain)
    projected = jnp.dot(normed, first, preferred_element_type=f32)
    even = member % 2 == 0
    mine = jnp.where(even, projected[:, :DK], projected[:, :DK] * DK ** (-0.5)).astype(bf16)
    other = swap_cores(mine)
    query_rows = jnp.where(even, mine, other)
    key_rows = jnp.where(even, other, mine)
    value_rows = projected[:, DK : 2 * DK].astype(bf16)
    gate_rows = projected[:, 2 * DK :].astype(bf16)
    head_index = member // 2
    decay_rate = 1.0 - jnp.exp2(-5.0 - head_index.astype(f32))
    retained = retain_local(query_rows, key_rows, value_rows, decay_rate, length)
    sums = jnp.stack([jnp.sum(retained, axis=1), jnp.sum(retained * retained, axis=1)])
    sums = sums + swap_cores(sums)
    row_mean = sums[0] / DV
    row_var = sums[1] / DV - row_mean * row_mean
    grouped = (retained - row_mean[:, None]) * lax.rsqrt(row_var + epsilon)[:, None]
    gated = (jax.nn.silu(gate_rows.astype(f32)) * grouped).astype(bf16)
    stream = sum_up(gated, output_weight.astype(bf16), token_rows)
    normed_stream = norm_rows(gather_up(stream), forward_gain)
    projected = jnp.dot(normed_stream, second, preferred_element_type=f32)
    hidden = (jax.nn.silu(projected[:, :256]) * projected[:, 256:]).astype(bf16)
    result = sum_up(hidden, down_weight.astype(bf16), stream)
    live_rows = jnp.arange(LMAX) < length
    finished = jnp.where(live_rows[:, None], result, jnp.zeros_like(result))
    return finished[None]


def solution(mesh):
    placed = (
        P("req", None, "mlp"),
        P(),
        P(),
        P(),
        P("mlp", None),
        P("mlp", None),
        P("mlp", None),
        P("mlp", None),
        P("mlp", None),
        P("mlp", None),
        P("mlp", None),
        P("mlp", None),
    )
    return jax.shard_map(
        body, mesh=mesh, in_specs=placed, out_specs=P("req", None, "mlp"), check_vma=False
    )
```

```python
import functools
import jax
import jax.numpy as jnp
from jax import lax
from jax.experimental import pallas as pl
from jax.experimental.pallas import tpu as pltpu
from jax.sharding import PartitionSpec as P

H = 8
DK = 256
DV = 512
SPAN = 256
LMAX = 1024
BLK = 128
REST = [(2, 1), (2, 0), (1, 1), (3, 1), (1, 0), (3, 0), (0, 1)]

epsilon = 1e-05
bf16 = jnp.bfloat16
f32 = jnp.float32


class Cut:
    def __init__(self, rows, cut):
        half, rest = cut // 2, (rows + cut) // 2
        self.ALLA, self.LOA, self.HIA = (0, cut), (0, half), (half, cut)
        self.ALLB, self.LOB, self.HIB = (cut, rows), (cut, rest), (rest, rows)


WIDE_CUT = Cut(1024, 448)
DEAL = 448
DEAL_CUT = Cut(DEAL, 192)


def rows_of(span):
    return pl.ds(span[0], span[1] - span[0])


class Place:
    def __init__(self):
        self.req = lax.axis_index("req")
        self.me = lax.axis_index("mlp")
        self.x = self.req // 2
        self.zh = self.req % 2
        self.y = self.me // 4
        self.z = (self.me // 2) % 2
        self.c = self.me % 2

    def member(self, dy, zr, cc):
        return ((self.y + dy + 4) % 4) * 4 + ((self.z + zr) % 2) * 2 + (self.c + cc) % 2

    def near(self, dy, zr, cc):
        return (self.req, self.member(dy, zr, cc))

    def across(self, dx):
        return (((self.x + dx + 4) % 4) * 2 + self.zh, self.me)


class Mover:
    def __init__(self, send, recv):
        self.send, self.recv, self.count, self.sent = send, recv, 0, []

    def plan(self, src, dst, device):
        i = self.count
        self.count += 1
        return pltpu.make_async_remote_copy(
            src_ref=src, dst_ref=dst, send_sem=self.send.at[i], recv_sem=self.recv.at[i],
            device_id=device, device_id_type=pl.DeviceIdType.MESH,
        )

    def go(self, src, dst, device):
        copy = self.plan(src, dst, device)
        copy.start()
        self.sent.append(copy)
        return copy

    def drain(self):
        for copy in self.sent:
            copy.wait_send()
        self.sent = []


def greet(devices):
    barrier = pltpu.get_barrier_semaphore()
    for device in devices:
        pl.semaphore_signal(barrier, inc=1, device_id=device, device_id_type=pl.DeviceIdType.MESH)
    pl.semaphore_wait(barrier, len(devices))


def column(member):
    return pl.ds(pl.multiple_of(member * BLK, BLK), BLK)


class Gather:
    def __init__(self, place, mover, full, cut):
        self.p, self.m, self.full, self.s = place, mover, full, cut
        self.pend = []

    def at(self, span, dy, zr, cc=0):
        return self.full.at[rows_of(span), column(self.p.member(dy, zr, cc))]

    def pass_on(self, span, dy, zr, targets):
        place = self.p
        ref = self.at(span, dy, zr)
        out = []
        for step in targets:
            device = {"r": place.near(1, 0, 0), "l": place.near(-1, 0, 0),
                      "z": place.near(0, 1, 0), "c": place.near(0, 0, 1)}[step]
            out.append(self.m.go(ref, ref, device))
        return out

    def start_a(self):
        self.a = self.pass_on(self.s.ALLA, 0, 0, "rlzc")

    def start_b(self):
        self.b = self.pass_on(self.s.ALLB, 0, 0, "zrlc")

    def first(self):
        ar, al, az, ac = self.a
        bz, br, bl, bc = self.b
        self.pend += [ac, bc]
        bz.wait_recv()
        self.zb = self.pass_on(self.s.ALLB, 0, 1, "rlc")
        ar.wait_recv()
        self.al1 = self.pass_on(self.s.LOA, -1, 0, "r") + self.pass_on(self.s.ALLA, -1, 0, "zc")
        al.wait_recv()
        self.ar1 = self.pass_on(self.s.HIA, 1, 0, "l") + self.pass_on(self.s.ALLA, 1, 0, "zc")
        br.wait_recv()
        self.bl1 = self.pass_on(self.s.LOB, -1, 0, "r") + self.pass_on(self.s.ALLB, -1, 0, "c")
        bl.wait_recv()
        self.br1 = self.pass_on(self.s.HIB, 1, 0, "l") + self.pass_on(self.s.ALLB, 1, 0, "c")
        az.wait_recv()
        self.pend += self.pass_on(self.s.ALLA, 0, 1, "c")

    def second(self):
        lo, az, ac = self.al1
        hi, az2, ac2 = self.ar1
        self.pend += [ac, ac2]
        lo.wait_recv()
        o1 = self.pass_on(self.s.LOA, -2, 0, "zc")
        hi.wait_recv()
        o2 = self.pass_on(self.s.HIA, 2, 0, "zc")
        zr, zl, zc = self.zb
        self.pend += [zc]
        zr.wait_recv()
        zlo = self.pass_on(self.s.LOB, -1, 1, "r")
        self.pend += self.pass_on(self.s.ALLB, -1, 1, "c")
        zl.wait_recv()
        zhi = self.pass_on(self.s.HIB, 1, 1, "l")
        self.pend += self.pass_on(self.s.ALLB, 1, 1, "c")
        az.wait_recv()
        self.pend += self.pass_on(self.s.ALLA, -1, 1, "c")
        az2.wait_recv()
        self.pend += self.pass_on(self.s.ALLA, 1, 1, "c")
        blo, bc = self.bl1
        bhi, bc2 = self.br1
        self.pend += [bc, bc2]
        blo.wait_recv()
        self.pend += self.pass_on(self.s.LOB, -2, 0, "c")
        bhi.wait_recv()
        self.pend += self.pass_on(self.s.HIB, 2, 0, "c")
        self.pend += [o1[1], o2[1]]
        o1[0].wait_recv()
        self.pend += self.pass_on(self.s.LOA, -2, 1, "c")
        o2[0].wait_recv()
        self.pend += self.pass_on(self.s.HIA, 2, 1, "c")
        zlo[0].wait_recv()
        self.pend += self.pass_on(self.s.LOB, -2, 1, "c")
        zhi[0].wait_recv()
        self.pend += self.pass_on(self.s.HIB, 2, 1, "c")

    def finish(self):
        for copy in self.pend:
            copy.wait_recv()
        self.pend = []


GATHER_COPIES = 38


class Handout:
    def __init__(self, place, mover, refs, out, quarter, own, pack, mate, local):
        self.p, self.m, self.refs, self.out = place, mover, refs, out
        self.quarter, self.own, self.pack, self.mate, self.local = quarter, own, pack, mate, local
        self.rel = [(dy, zr, cc) for dy, zr in REST for cc in (0, 1)]
        self.cols = out.shape[1]

    def load(self):
        place = self.p
        chip = place.me // 2
        part = pl.ds(pl.multiple_of(place.x * 32, 32), 32)
        self.loads, at = [], 0
        for ref in self.refs:
            self.one(ref.at[part, :], self.quarter.at[:, pl.ds(at, ref.shape[1])])
            at += ref.shape[1]
        at = 0
        for ref in self.refs:
            wide = ref.shape[1] // 8
            self.one(ref.at[:, pl.ds(pl.multiple_of(chip * wide, 128), wide)], self.own.at[:, pl.ds(at, wide)])
            at += wide

    def one(self, src, dst):
        copy = pltpu.make_async_copy(src, dst, self.local.at[len(self.loads)])
        copy.start()
        self.loads.append(copy)


    def lot(self, member, slot, low=0, high=32):
        return pl.ds(pl.multiple_of(member * 128 + slot * 32 + low, 16), high - low)

    def share(self):
        place = self.p
        for copy in self.loads[:len(self.refs)]:
            copy.wait()
        for d in range(16):
            for i in range(self.cols // 256):
                self.pack[d, :, i * 256:(i + 1) * 256] = self.quarter[:, i * 4096 + self.spot(d, i):][:, :256].astype(bf16)
        self.first = [
            self.m.go(self.pack.at[place.member(*r)], self.out.at[self.lot(place.me, place.x), :], place.near(*r))
            for r in self.rel
        ]

    def spot(self, d, i):
        if i == 0 and len(self.refs) * 256 > self.cols:
            return (d % 2) * 2048 + (d // 2) * 256
        return d * 256

    def share_own(self):
        place = self.p
        for copy in self.loads[len(self.refs):]:
            copy.wait()
        rows = pl.ds(pl.multiple_of(place.me * 128, 128), 128)
        for i in range(self.cols // 256):
            mine = self.own[:, pl.ds(pl.multiple_of(i * 512 + place.c * 256, 128), 256)]
            self.out[rows, i * 256:(i + 1) * 256] = mine.astype(bf16)
            other = self.own[:, pl.ds(pl.multiple_of(i * 512 + (1 - place.c) * 256, 128), 256)]
            self.mate[:, i * 256:(i + 1) * 256] = other.astype(bf16)
        self.partner = self.m.go(self.mate, self.out.at[rows, :], place.near(0, 0, 1))

    def origin(self, r):
        return self.p.member(-r[0], r[1], r[2])

    def spread(self):
        place = self.p
        self.got = []
        for r, copy in zip(self.rel, self.first):
            copy.wait_recv()
            ref = self.out.at[self.lot(self.origin(r), place.x), :]
            self.got.append((self.m.go(ref, ref, place.across(1)), self.m.go(ref, ref, place.across(-1))))

    def onward(self):
        place = self.p
        self.halves = []
        for r, (right, left) in zip(self.rel, self.got):
            right.wait_recv()
            ref = self.out.at[self.lot(self.origin(r), (place.x + 3) % 4, 0, 16), :]
            self.halves.append(self.m.go(ref, ref, place.across(1)))
            left.wait_recv()
            ref = self.out.at[self.lot(self.origin(r), (place.x + 1) % 4, 16, 32), :]
            self.halves.append(self.m.go(ref, ref, place.across(-1)))

    def finish(self):
        self.partner.wait_recv()
        for copy in self.halves:
            copy.wait_recv()


HANDOUT_COPIES = 14 * 5 + 1


def group_peers(place):
    return [place.near(dy, zr, cc) for dy, zr in REST for cc in (0, 1)] + [place.near(0, 0, 1)]


def hand_kernel(tokens, query, key, value, gate, full, first, quarter, own, pack, mate, local, token_sem, send, recv):
    place = Place()
    mover = Mover(send, recv)
    handout = Handout(place, mover, (query, key, value, gate), first, quarter, own, pack, mate, local)
    handout.load()
    own_rows = pltpu.make_async_copy(tokens, full.at[:, column(place.me)], token_sem)
    own_rows.start()
    greet(group_peers(place) + [place.across(1), place.across(-1)])
    handout.share()
    own_rows.wait()
    gather = Gather(place, mover, full, WIDE_CUT)
    gather.start_a()
    gather.start_b()
    handout.share_own()
    handout.spread()
    gather.first()
    handout.onward()
    gather.second()
    gather.finish()
    handout.finish()
    mover.drain()


HAND_COPIES = GATHER_COPIES + HANDOUT_COPIES


def hand_over(tokens, *weights):
    vmem = pl.BlockSpec(memory_space=pltpu.VMEM)
    hbm = pl.BlockSpec(memory_space=pl.ANY)
    return pl.pallas_call(
        hand_kernel,
        name="hand_over",
        out_shape=(
            jax.ShapeDtypeStruct((LMAX, 2048), bf16),
            jax.ShapeDtypeStruct((2048, 768), bf16),
        ),
        in_specs=[vmem] + [hbm] * 4,
        out_specs=(vmem, vmem),
        scratch_shapes=[
            pltpu.VMEM((32, 12288), f32),
            pltpu.VMEM((128, 1536), f32),
            pltpu.VMEM((16, 32, 768), bf16),
            pltpu.VMEM((128, 768), bf16),
            pltpu.SemaphoreType.DMA((8,)),
            pltpu.SemaphoreType.DMA,
            pltpu.SemaphoreType.DMA((HAND_COPIES,)),
            pltpu.SemaphoreType.DMA((HAND_COPIES,)),
        ],
        compiler_params=pltpu.CompilerParams(
            collective_id=0, has_side_effects=True, vmem_limit_bytes=60 * 2**20
        ),
    )(tokens, *weights)


class Scatter:
    def __init__(self, place, mover, wide, wpar, bufs):
        self.p, self.m, self.wide, self.wpar = place, mover, wide, wpar
        self.S, self.RA, self.RLO, self.RHI, self.RL, self.RR, self.RZ = bufs
        self.right, self.left, self.over = place.near(1, 0, 0), place.near(-1, 0, 0), place.near(0, 1, 0)

    def multiply(self, span):
        rows = rows_of(span)
        for i in range(4):
            part = jnp.dot(self.wide[rows, :], self.wpar[:, i * 256:(i + 1) * 256], preferred_element_type=f32)
            part = part.astype(bf16)
            self.S[2 * i, rows, :] = part[:, :128]
            self.S[2 * i + 1, rows, :] = part[:, 128:]

    def piece(self, zr, dy, span):
        return self.S.at[zr * 4 + dy, rows_of(span), :]

    def add(self, zr, dy, span, *others):
        rows = rows_of(span)
        total = self.S[zr * 4 + dy, rows, :].astype(f32)
        for other in others:
            total = total + other[rows, :].astype(f32)
        self.S[zr * 4 + dy, rows, :] = total.astype(bf16)

    def start_a(self):
        s = DEAL_CUT
        self.za = {dy: self.m.go(self.piece(1, dy, s.ALLA), self.RA.at[dy, rows_of(s.ALLA), :], self.over)
                   for dy in (2, 1, 3, 0)}

    def start_b(self):
        s = DEAL_CUT
        self.lo, self.hi = {}, {}
        for zr in (1, 0):
            self.lo[zr] = self.m.go(self.piece(zr, 2, s.LOB), self.RLO.at[zr, rows_of(s.LOB), :], self.right)
            self.hi[zr] = self.m.go(self.piece(zr, 2, s.HIB), self.RHI.at[zr, rows_of(s.HIB), :], self.left)

    def middle(self):
        s, m = DEAL_CUT, self.m
        lo, hi, za = self.lo, self.hi, self.za
        right, left, over = self.right, self.left, self.over
        RA, RLO, RHI, RL, RR, RZ = self.RA, self.RLO, self.RHI, self.RL, self.RR, self.RZ
        toR, toL = {}, {}
        for zr in (1, 0):
            lo[zr].wait_recv()
            self.add(zr, 1, s.LOB, RLO.at[zr])
            toR[zr] = m.go(self.piece(zr, 1, s.ALLB), RL.at[zr, rows_of(s.ALLB), :], right)
            hi[zr].wait_recv()
            self.add(zr, 3, s.HIB, RHI.at[zr])
            toL[zr] = m.go(self.piece(zr, 3, s.ALLB), RR.at[zr, rows_of(s.ALLB), :], left)
            if zr == 1:
                za[2].wait_recv()
                self.add(0, 2, s.ALLA, RA.at[2])
                loA = m.go(self.piece(0, 2, s.LOA), RLO.at[0, rows_of(s.LOA), :], right)
                hiA = m.go(self.piece(0, 2, s.HIA), RHI.at[0, rows_of(s.HIA), :], left)
        za[1].wait_recv()
        self.add(0, 1, s.ALLA, RA.at[1])
        za[3].wait_recv()
        self.add(0, 3, s.ALLA, RA.at[3])
        loA.wait_recv()
        self.add(0, 1, s.LOA, RLO.at[0])
        toRA = m.go(self.piece(0, 1, s.ALLA), RL.at[0, rows_of(s.ALLA), :], right)
        hiA.wait_recv()
        self.add(0, 3, s.HIA, RHI.at[0])
        toLA = m.go(self.piece(0, 3, s.ALLA), RR.at[0, rows_of(s.ALLA), :], left)
        toR[1].wait_recv()
        toL[1].wait_recv()
        self.add(1, 0, s.ALLB, RL.at[1], RR.at[1])
        zb = m.go(self.piece(1, 0, s.ALLB), RZ.at[rows_of(s.ALLB), :], over)
        self.last = (za[0], toRA, toLA), (toR[0], toL[0], zb)

    def total(self, span, which, extra):
        for copy in self.last[which]:
            copy.wait_recv()
        rows = rows_of(span)
        total = self.S[0, rows, :].astype(f32) + self.RL[0, rows, :].astype(f32)
        return total + self.RR[0, rows, :].astype(f32) + extra[rows, :].astype(f32)

    def total_a(self):
        return self.total(DEAL_CUT.ALLA, 0, self.RA.at[0])

    def total_b(self):
        return self.total(DEAL_CUT.ALLB, 1, self.RZ)


SCATTER_COPIES = 4 + 4 + 4 + 2 + 2 + 1
OTHERS = [(dx, dz) for dx in (2, 1, 3, 0) for dz in (1, 0) if (dx, dz) != (0, 0)]


def feed_kernel(lengths, gated, tokens, gain, out_weight, down_weight, swish, up, out,
                stage, wpar, wmate, lots, token_lots, base, wide, full, normed, result, spare,
                second, quarter, own, pack, mate,
                S1, RA1, RLO1, RHI1, RL1, RR1, RZ1, S2, RA2, RLO2, RHI2, RL2, RR2, RZ2,
                local, load_sem, send, recv):
    place = Place()
    mover = Mover(send, recv)
    req = place.req
    cut = DEAL_CUT
    handout = Handout(place, mover, (swish, up), second, quarter, own, pack, mate, local)
    handout.load()
    loads = [pltpu.make_async_copy(out_weight, stage.at[0], load_sem.at[0]),
             pltpu.make_async_copy(down_weight, stage.at[1], load_sem.at[1])]
    for copy in loads:
        copy.start()
    mate_core = place.near(0, 0, 1)

    def group(dx, dz):
        return ((place.x + dx + 4) % 4) * 2 + (place.zh + dz) % 2

    greet(group_peers(place) + [(group(dx, dz), place.me) for dx, dz in OTHERS])
    dealt = []
    for dx, dz in OTHERS:
        target = group(dx, dz)
        turn = (target - req + 8) % 8
        dealt.append(mover.go(gated.at[:, turn], lots.at[req], (target, place.me)))
        dealt.append(mover.go(tokens.at[:, turn], token_lots.at[req], (target, place.me)))
    lots[req] = gated[:, 0]
    token_lots[req] = tokens[:, 0]
    handout.share()

    order = [(dy, zr) for zr in (0, 1) for dy in range(4)]

    def set_weight(which):
        loads[which].wait()
        for i, (dy, zr) in enumerate(order):
            wpar[which, 0:256, i * 128:(i + 1) * 128] = stage[which, :, column(place.member(dy, zr, 0))].astype(bf16)
            wmate[which, :, i * 128:(i + 1) * 128] = stage[which, :, column(place.member(dy, zr, 1))].astype(bf16)
        return mover.go(wmate.at[which], wpar.at[which, pl.ds(256, 256), :], mate_core)

    weight1 = set_weight(0)
    handout.share_own()

    starts, counts = [], []
    start = jnp.int32(0)
    for r in range(8):
        length = lengths[r]
        turn = (req - r + 8) % 8
        count = 16 * (length // 128) + jnp.clip(length % 128 - 16 * turn, 0, 16)
        starts.append(start)
        counts.append(count)
        start = start + count

    def chosen(span):
        rows = span[1] - span[0]
        row = lax.broadcasted_iota(jnp.int32, (rows, LMAX), 0) + span[0]
        slot = lax.broadcasted_iota(jnp.int32, (rows, LMAX), 1)
        want = jnp.full((rows, LMAX), -1, jnp.int32)
        for r in range(8):
            inside = (row >= starts[r]) & (row < starts[r] + counts[r])
            want = jnp.where(inside, row + (r * 128 - starts[r]), want)
        return jnp.where(slot == want, 1.0, 0.0).astype(bf16)

    for copy in dealt:
        copy.wait_recv()
    width = lots.shape[3]
    sent = []
    for span in (cut.ALLA, cut.ALLB):
        rows = rows_of(span)
        pick = chosen(span)
        part = jnp.dot(pick, lots[...].reshape(LMAX, width), preferred_element_type=f32)
        wide[0, rows, 0:256] = part.astype(bf16)
        ref = wide.at[0, rows, pl.ds(0, 256)]
        sent.append(mover.go(ref, wide.at[0, rows, pl.ds(256, 256)], mate_core))
        kept = jnp.dot(pick, token_lots[...].reshape(LMAX, BLK), preferred_element_type=f32)
        base[rows, :] = kept.astype(bf16)

    scatter = Scatter(place, mover, wide.at[0], wpar.at[0], (S1, RA1, RLO1, RHI1, RL1, RR1, RZ1))
    weight1.wait_recv()
    sent[0].wait_recv()
    scatter.multiply(cut.ALLA)
    scatter.start_a()
    sent[1].wait_recv()
    scatter.multiply(cut.ALLB)
    scatter.start_b()
    handout.spread()
    weight2 = set_weight(1)
    scatter.middle()
    mine = column(place.me)
    gather = Gather(place, mover, full, cut)
    full[rows_of(cut.ALLA), mine] = (base[rows_of(cut.ALLA), :].astype(f32) + scatter.total_a()).astype(bf16)
    gather.start_a()
    full[rows_of(cut.ALLB), mine] = (base[rows_of(cut.ALLB), :].astype(f32) + scatter.total_b()).astype(bf16)
    gather.start_b()
    handout.onward()
    gather.first()
    gather.second()
    gather.finish()
    handout.finish()

    def normalize(i, carry):
        rows = pl.ds(pl.multiple_of(i * 32, 32), 32)
        values = full[rows, :].astype(f32)
        scale = lax.rsqrt(jnp.mean(values * values, axis=-1, keepdims=True) + epsilon)
        normed[rows, :] = (values * scale * gain[...]).astype(bf16)
        return carry

    lax.fori_loop(0, DEAL // 32, normalize, 0)
    sent = []
    for span in (cut.ALLA, cut.ALLB):
        rows = rows_of(span)
        part = jnp.dot(normed[rows, :], second[...], preferred_element_type=f32)
        gate = part[:, :256]
        wide[1, rows, 0:256] = (gate / (1.0 + jnp.exp(-gate)) * part[:, 256:]).astype(bf16)
        ref = wide.at[1, rows, pl.ds(0, 256)]
        sent.append(mover.go(ref, wide.at[1, rows, pl.ds(256, 256)], mate_core))
    scatter = Scatter(place, mover, wide.at[1], wpar.at[1], (S2, RA2, RLO2, RHI2, RL2, RR2, RZ2))
    weight2.wait_recv()
    sent[0].wait_recv()
    scatter.multiply(cut.ALLA)
    scatter.start_a()
    sent[1].wait_recv()
    scatter.multiply(cut.ALLB)
    scatter.start_b()
    scatter.middle()
    for span, total in ((cut.ALLA, scatter.total_a), (cut.ALLB, scatter.total_b)):
        rows = rows_of(span)
        result[rows, :] = (full[rows, mine].astype(f32) + total()).astype(bf16)
    returned = []
    for r in range(8):
        row = lax.broadcasted_iota(jnp.int32, (128, DEAL), 0)
        at = lax.broadcasted_iota(jnp.int32, (128, DEAL), 1)
        pick = jnp.where((at == row + starts[r]) & (row < counts[r]), 1.0, 0.0).astype(bf16)
        back = jnp.dot(pick, result[...], preferred_element_type=f32).astype(bf16)
        spare[r] = back.reshape(8, 16, BLK)
    for dx, dz in OTHERS:
        target = group(dx, dz)
        returned.append(mover.go(spare.at[target], out.at[:, (req - target + 8) % 8], (target, place.me)))
    out[:, 0] = spare[req]
    for copy in returned:
        copy.wait_recv()
    mover.drain()


FEED_COPIES = HANDOUT_COPIES + GATHER_COPIES + 2 * SCATTER_COPIES + 7 * 3 + 2 + 4


def feed(lengths, gated, tokens, gain, out_weight, down_weight, swish, up):
    vmem = pl.BlockSpec(memory_space=pltpu.VMEM)
    hbm = pl.BlockSpec(memory_space=pl.ANY)
    sums = [
        pltpu.VMEM((8, DEAL, BLK), bf16),
        pltpu.VMEM((4, DEAL, BLK), bf16),
        pltpu.VMEM((2, DEAL, BLK), bf16),
        pltpu.VMEM((2, DEAL, BLK), bf16),
        pltpu.VMEM((2, DEAL, BLK), bf16),
        pltpu.VMEM((2, DEAL, BLK), bf16),
        pltpu.VMEM((DEAL, BLK), bf16),
    ]
    return pl.pallas_call(
        feed_kernel,
        name="feed",
        out_shape=jax.ShapeDtypeStruct((8, 8, 16, BLK), bf16),
        in_specs=[pl.BlockSpec(memory_space=pltpu.SMEM), vmem, vmem, vmem] + [hbm] * 4,
        out_specs=vmem,
        scratch_shapes=[
            pltpu.VMEM((2, 256, 2048), f32),
            pltpu.VMEM((2, 512, 1024), bf16),
            pltpu.VMEM((2, 256, 1024), bf16),
            pltpu.VMEM((8, 8, 16, 256), bf16),
            pltpu.VMEM((8, 8, 16, BLK), bf16),
            pltpu.VMEM((DEAL, BLK), bf16),
            pltpu.VMEM((2, DEAL, 512), bf16),
            pltpu.VMEM((DEAL, 2048), bf16),
            pltpu.VMEM((DEAL, 2048), bf16),
            pltpu.VMEM((DEAL, BLK), bf16),
            pltpu.VMEM((8, 8, 16, BLK), bf16),
            pltpu.VMEM((2048, 512), bf16),
            pltpu.VMEM((32, 8192), f32),
            pltpu.VMEM((128, 1024), f32),
            pltpu.VMEM((16, 32, 512), bf16),
            pltpu.VMEM((128, 512), bf16),
        ] + sums + sums + [
            pltpu.SemaphoreType.DMA((4,)),
            pltpu.SemaphoreType.DMA((2,)),
            pltpu.SemaphoreType.DMA((FEED_COPIES,)),
            pltpu.SemaphoreType.DMA((FEED_COPIES,)),
        ],
        compiler_params=pltpu.CompilerParams(
            collective_id=1, has_side_effects=True, vmem_limit_bytes=62 * 2**20
        ),
    )(lengths, gated, tokens, gain, out_weight, down_weight, swish, up)


def swap_cores(values):
    route = [(i, i ^ 1) for i in range(lax.axis_size("mlp"))]
    return lax.ppermute(values, "mlp", route)


def norm_rows(token_rows, gain_vector):
    values = token_rows.astype(f32)
    row_scale = lax.rsqrt(jnp.mean(values * values, axis=-1, keepdims=True) + epsilon)
    return (values * row_scale * gain_vector).astype(bf16)


def split_pair(values):
    upper = values.astype(bf16)
    lower = (values - upper.astype(f32)).astype(bf16)
    return (upper, lower)


def retain_local(query_rows, key_rows, value_rows, decay_rate, length):
    total_rows = query_rows.shape[0]
    value_cols = value_rows.shape[1]
    position = jnp.arange(SPAN)
    distance = position[:, None] - position[None, :]
    powers = jnp.power(decay_rate, jnp.maximum(distance, 0).astype(f32))
    within_mask = jnp.where(distance >= 0, powers, 0.0)
    leading = jnp.power(decay_rate, (position + 1).astype(f32))
    trailing = jnp.power(decay_rate, (SPAN - 1 - position).astype(f32))
    span_decay = jnp.power(decay_rate, jnp.float32(SPAN))
    live_blocks = (length + SPAN - 1) // SPAN
    contract_rows = (((0,), (0,)), ((), ()))

    def advance(span_index, loop_state):
        memory, output = loop_state
        row_start = span_index * SPAN
        query_block = lax.dynamic_slice_in_dim(query_rows, row_start, SPAN, 0)
        key_block = lax.dynamic_slice_in_dim(key_rows, row_start, SPAN, 0)
        value_block = lax.dynamic_slice_in_dim(value_rows, row_start, SPAN, 0)
        scores = lax.dot_general(
            query_block, key_block, (((1,), (1,)), ((), ())), preferred_element_type=f32
        )
        weights = (scores * within_mask).astype(bf16)
        within_sum = jnp.dot(weights, value_block, preferred_element_type=f32)
        memory_upper, memory_lower = split_pair(memory)
        across_sum = (
            jnp.dot(query_block, memory_upper, preferred_element_type=f32)
            + jnp.dot(query_block, memory_lower, preferred_element_type=f32)
        ) * leading[:, None]
        decayed_upper, decayed_lower = split_pair(key_block.astype(f32) * trailing[:, None])
        update = lax.dot_general(
            decayed_upper, value_block, contract_rows, preferred_element_type=f32
        ) + lax.dot_general(
            decayed_lower, value_block, contract_rows, preferred_element_type=f32
        )
        memory = memory * span_decay + update
        output = lax.dynamic_update_slice_in_dim(output, within_sum + across_sum, row_start, 0)
        return (memory, output)

    start_state = (
        jnp.zeros((DK, value_cols), f32),
        jnp.zeros((total_rows, value_cols), f32),
    )
    return lax.fori_loop(0, live_blocks, advance, start_state)[1]


def body(
    tokens,
    lengths,
    retention_gain,
    forward_gain,
    query_weight,
    key_weight,
    value_weight,
    gate_weight,
    output_weight,
    swish_weight,
    up_weight,
    down_weight,
):
    owner_index = lax.axis_index("req")
    member = lax.axis_index("mlp")
    length = lengths[owner_index]
    token_rows = tokens[0]
    gathered, first = hand_over(token_rows, query_weight, key_weight, value_weight, gate_weight)
    normed = norm_rows(gathered, retention_gain)
    projected = jnp.dot(normed, first, preferred_element_type=f32)
    even = member % 2 == 0
    mine = jnp.where(even, projected[:, :DK], projected[:, :DK] * DK ** (-0.5)).astype(bf16)
    other = swap_cores(mine)
    query_rows = jnp.where(even, mine, other)
    key_rows = jnp.where(even, other, mine)
    value_rows = projected[:, DK : 2 * DK].astype(bf16)
    gate_rows = projected[:, 2 * DK :].astype(bf16)
    head_index = member // 2
    decay_rate = 1.0 - jnp.exp2(-5.0 - head_index.astype(f32))
    retained = retain_local(query_rows, key_rows, value_rows, decay_rate, length)
    sums = jnp.stack([jnp.sum(retained, axis=1), jnp.sum(retained * retained, axis=1)])
    sums = sums + swap_cores(sums)
    row_mean = sums[0] / DV
    row_var = sums[1] / DV - row_mean * row_mean
    grouped = (retained - row_mean[:, None]) * lax.rsqrt(row_var + epsilon)[:, None]
    gated = (jax.nn.silu(gate_rows.astype(f32)) * grouped).astype(bf16)
    granules = (8, 8, 16)
    finished = feed(
        lengths, gated.reshape(granules + (256,)), token_rows.reshape(granules + (BLK,)),
        forward_gain.reshape(1, 2048), output_weight, down_weight, swish_weight, up_weight
    )
    return finished.reshape(1, LMAX, BLK)


def solution(mesh):
    placed = (
        P("req", None, "mlp"),
        P(),
        P(),
        P(),
        P("mlp", None),
        P("mlp", None),
        P("mlp", None),
        P("mlp", None),
        P("mlp", None),
        P("mlp", None),
        P("mlp", None),
        P("mlp", None),
    )
    return jax.shard_map(
        body, mesh=mesh, in_specs=placed, out_specs=P("req", None, "mlp"), check_vma=False
    )
```

```python
import math
import jax
import jax.numpy as jnp
from jax import lax
from jax.experimental import pallas as pl
from jax.experimental.pallas import tpu as pltpu
from jax.sharding import PartitionSpec as P

H = 8
DK = 256
DV = 512
SPAN = 256
LMAX = 1024
BLK = 128
REST = [(1, 0), (3, 0), (1, 1), (3, 1), (2, 0), (2, 1)]
DIRECT = [(0, 0, 1), (0, 1, 0), (0, 1, 1)]

epsilon = 1e-05
bf16 = jnp.bfloat16
f32 = jnp.float32


class Cut:
    def __init__(self, rows, cut):
        half, rest = cut // 2, (rows + cut) // 2
        self.ALLA, self.LOA, self.HIA = (0, cut), (0, half), (half, cut)
        self.ALLB, self.LOB, self.HIB = (cut, rows), (cut, rest), (rest, rows)


WIDE_CUT = Cut(1024, 384)
DEAL = 448
DEAL_CUT = Cut(DEAL, 192)


def rows_of(span):
    return pl.ds(span[0], span[1] - span[0])


class Place:
    def __init__(self):
        self.req = lax.axis_index("req")
        self.me = lax.axis_index("mlp")
        self.x = self.req // 2
        self.zh = self.req % 2
        self.y = self.me // 4
        self.z = (self.me // 2) % 2
        self.c = self.me % 2

    def member(self, dy, zr, cc):
        return ((self.y + dy + 4) % 4) * 4 + ((self.z + zr) % 2) * 2 + (self.c + cc) % 2

    def near(self, dy, zr, cc):
        return (self.req, self.member(dy, zr, cc))

    def across(self, dx):
        return (((self.x + dx + 4) % 4) * 2 + self.zh, self.me)


class Mover:
    def __init__(self, send, recv):
        self.send, self.recv, self.count, self.sent = send, recv, 0, []

    def plan(self, src, dst, device):
        i = self.count
        self.count += 1
        return pltpu.make_async_remote_copy(
            src_ref=src, dst_ref=dst, send_sem=self.send.at[i], recv_sem=self.recv.at[i],
            device_id=device, device_id_type=pl.DeviceIdType.MESH,
        )

    def go(self, src, dst, device):
        copy = self.plan(src, dst, device)
        copy.start()
        self.sent.append(copy)
        return copy

    def drain(self):
        for copy in self.sent:
            copy.wait_send()
        self.sent = []


def greet(devices):
    barrier = pltpu.get_barrier_semaphore()
    for device in devices:
        pl.semaphore_signal(barrier, inc=1, device_id=device, device_id_type=pl.DeviceIdType.MESH)
    pl.semaphore_wait(barrier, len(devices))


def column(member):
    return pl.ds(pl.multiple_of(member * BLK, BLK), BLK)


class Gather:
    def __init__(self, place, mover, full, cut):
        self.p, self.m, self.full, self.s = place, mover, full, cut
        self.pend = []

    def at(self, span, dy, zr, cc=0):
        return self.full.at[rows_of(span), column(self.p.member(dy, zr, cc))]

    def pass_on(self, span, dy, zr, targets):
        place = self.p
        ref = self.at(span, dy, zr)
        out = []
        for step in targets:
            device = {"r": place.near(1, 0, 0), "l": place.near(-1, 0, 0),
                      "z": place.near(0, 1, 0), "c": place.near(0, 0, 1)}[step]
            out.append(self.m.go(ref, ref, device))
        return out

    def start_a(self):
        self.a = self.pass_on(self.s.ALLA, 0, 0, "rlzc")

    def start_b(self):
        self.b = self.pass_on(self.s.ALLB, 0, 0, "zrlc")

    def first(self):
        ar, al, az, ac = self.a
        bz, br, bl, bc = self.b
        self.pend += [ac, bc]
        bz.wait_recv()
        self.zb = self.pass_on(self.s.ALLB, 0, 1, "rlc")
        ar.wait_recv()
        self.al1 = self.pass_on(self.s.LOA, -1, 0, "r") + self.pass_on(self.s.ALLA, -1, 0, "zc")
        al.wait_recv()
        self.ar1 = self.pass_on(self.s.HIA, 1, 0, "l") + self.pass_on(self.s.ALLA, 1, 0, "zc")
        br.wait_recv()
        self.bl1 = self.pass_on(self.s.LOB, -1, 0, "r") + self.pass_on(self.s.ALLB, -1, 0, "c")
        bl.wait_recv()
        self.br1 = self.pass_on(self.s.HIB, 1, 0, "l") + self.pass_on(self.s.ALLB, 1, 0, "c")
        az.wait_recv()
        self.pend += self.pass_on(self.s.ALLA, 0, 1, "c")

    def second(self):
        lo, az, ac = self.al1
        hi, az2, ac2 = self.ar1
        self.pend += [ac, ac2]
        lo.wait_recv()
        o1 = self.pass_on(self.s.LOA, -2, 0, "zc")
        hi.wait_recv()
        o2 = self.pass_on(self.s.HIA, 2, 0, "zc")
        zr, zl, zc = self.zb
        self.pend += [zc]
        zr.wait_recv()
        zlo = self.pass_on(self.s.LOB, -1, 1, "r")
        self.pend += self.pass_on(self.s.ALLB, -1, 1, "c")
        zl.wait_recv()
        zhi = self.pass_on(self.s.HIB, 1, 1, "l")
        self.pend += self.pass_on(self.s.ALLB, 1, 1, "c")
        az.wait_recv()
        self.pend += self.pass_on(self.s.ALLA, -1, 1, "c")
        az2.wait_recv()
        self.pend += self.pass_on(self.s.ALLA, 1, 1, "c")
        blo, bc = self.bl1
        bhi, bc2 = self.br1
        self.pend += [bc, bc2]
        blo.wait_recv()
        self.pend += self.pass_on(self.s.LOB, -2, 0, "c")
        bhi.wait_recv()
        self.pend += self.pass_on(self.s.HIB, 2, 0, "c")
        self.pend += [o1[1], o2[1]]
        o1[0].wait_recv()
        self.pend += self.pass_on(self.s.LOA, -2, 1, "c")
        o2[0].wait_recv()
        self.pend += self.pass_on(self.s.HIA, 2, 1, "c")
        zlo[0].wait_recv()
        self.pend += self.pass_on(self.s.LOB, -2, 1, "c")
        zhi[0].wait_recv()
        self.pend += self.pass_on(self.s.HIB, 2, 1, "c")

    def finish(self):
        for copy in self.pend:
            copy.wait_recv()
        self.pend = []


GATHER_COPIES = 38


class Handout:
    def __init__(self, place, mover, refs, out, quarter, whole, pack, mate, local):
        self.p, self.m, self.refs, self.out = place, mover, refs, out
        self.quarter, self.whole, self.pack, self.mate, self.local = quarter, whole, pack, mate, local
        self.rel = [(dy, zr, cc) for dy, zr in REST for cc in (0, 1)]
        self.cols = out.shape[1]

    def load(self):
        place = self.p
        part = pl.ds(pl.multiple_of(place.x * 32, 32), 32)
        self.loads, at = [], 0
        for ref in self.refs:
            self.one(ref.at[part, :], self.quarter.at[:, pl.ds(at, ref.shape[1])])
            at += ref.shape[1]
        for zr in (0, 1):
            chip = place.member(0, zr, 0) // 2
            at = 0
            for ref in self.refs:
                wide = ref.shape[1] // 8
                self.one(ref.at[:, pl.ds(pl.multiple_of(chip * wide, 128), wide)], self.whole.at[zr, :, pl.ds(at, wide)])
                at += wide

    def one(self, src, dst):
        copy = pltpu.make_async_copy(src, dst, self.local.at[len(self.loads)])
        copy.start()
        self.loads.append(copy)

    def lot(self, member, slot, low=0, high=32):
        return pl.ds(pl.multiple_of(member * 128 + slot * 32 + low, 16), high - low)

    def share(self):
        place = self.p
        for copy in self.loads[:len(self.refs)]:
            copy.wait()
        for d in range(16):
            for i in range(self.cols // 256):
                self.pack[d, :, i * 256:(i + 1) * 256] = self.quarter[:, i * 4096 + self.spot(d, i):][:, :256].astype(bf16)
        self.first = [
            self.m.go(self.pack.at[place.member(*r)], self.out.at[self.lot(place.me, place.x), :], place.near(*r))
            for r in self.rel
        ]

    def spot(self, d, i):
        if i == 0 and len(self.refs) * 256 > self.cols:
            return (d % 2) * 2048 + (d // 2) * 256
        return d * 256

    def share_whole(self):
        place = self.p
        for copy in self.loads[len(self.refs):]:
            copy.wait()
        rows = pl.ds(pl.multiple_of(place.me * 128, 128), 128)
        self.whole_sent = []
        for i in range(self.cols // 256):
            mine = self.whole[0, :, pl.ds(pl.multiple_of(i * 512 + place.c * 256, 128), 256)]
            self.out[rows, i * 256:(i + 1) * 256] = mine.astype(bf16)
        for at, (dy, zr, cc) in enumerate(DIRECT):
            core = (place.c + cc) % 2
            for i in range(self.cols // 256):
                other = self.whole[zr, :, pl.ds(pl.multiple_of(i * 512 + core * 256, 128), 256)]
                self.mate[at, :, i * 256:(i + 1) * 256] = other.astype(bf16)
            self.whole_sent.append(self.m.go(self.mate.at[at], self.out.at[rows, :], place.near(dy, zr, cc)))

    def origin(self, r):
        return self.p.member(-r[0], r[1], r[2])

    def spread(self, which):
        place = self.p
        got = []
        for i in which:
            self.first[i].wait_recv()
            ref = self.out.at[self.lot(self.origin(self.rel[i]), place.x), :]
            got.append((i, self.m.go(ref, ref, place.across(1)), self.m.go(ref, ref, place.across(-1))))
        return got

    def onward(self, got):
        place = self.p
        halves = []
        for i, right, left in got:
            origin = self.origin(self.rel[i])
            right.wait_recv()
            ref = self.out.at[self.lot(origin, (place.x + 3) % 4, 0, 16), :]
            halves.append(self.m.go(ref, ref, place.across(1)))
            left.wait_recv()
            ref = self.out.at[self.lot(origin, (place.x + 1) % 4, 16, 32), :]
            halves.append(self.m.go(ref, ref, place.across(-1)))
        return halves


HANDOUT_COPIES = 12 * 5 + 3


def group_peers(place):
    return [place.near(dy, zr, cc) for dy, zr in REST for cc in (0, 1)] + [place.near(*r) for r in DIRECT]


def await_all(copies):
    for copy in copies:
        copy.wait_recv()


class Scatter:
    def __init__(self, place, mover, wide, wpar, bufs):
        self.p, self.m, self.wide, self.wpar = place, mover, wide, wpar
        self.S, self.RA, self.RLO, self.RHI, self.RL, self.RR, self.RZ = bufs
        self.right, self.left, self.over = place.near(1, 0, 0), place.near(-1, 0, 0), place.near(0, 1, 0)

    def multiply(self, span):
        rows = rows_of(span)
        for i in range(4):
            part = jnp.dot(self.wide[rows, :], self.wpar[:, i * 256:(i + 1) * 256], preferred_element_type=f32)
            part = part.astype(bf16)
            self.S[2 * i, rows, :] = part[:, :128]
            self.S[2 * i + 1, rows, :] = part[:, 128:]

    def piece(self, zr, dy, span):
        return self.S.at[zr * 4 + dy, rows_of(span), :]

    def add(self, zr, dy, span, *others):
        rows = rows_of(span)
        total = self.S[zr * 4 + dy, rows, :].astype(f32)
        for other in others:
            total = total + other[rows, :].astype(f32)
        self.S[zr * 4 + dy, rows, :] = total.astype(bf16)

    def start_a(self):
        s = DEAL_CUT
        self.za = {dy: self.m.go(self.piece(1, dy, s.ALLA), self.RA.at[dy, rows_of(s.ALLA), :], self.over)
                   for dy in (2, 1, 3, 0)}

    def start_b(self):
        s = DEAL_CUT
        self.lo, self.hi = {}, {}
        for zr in (1, 0):
            self.lo[zr] = self.m.go(self.piece(zr, 2, s.LOB), self.RLO.at[zr, rows_of(s.LOB), :], self.right)
            self.hi[zr] = self.m.go(self.piece(zr, 2, s.HIB), self.RHI.at[zr, rows_of(s.HIB), :], self.left)

    def middle(self):
        s, m = DEAL_CUT, self.m
        lo, hi, za = self.lo, self.hi, self.za
        right, left, over = self.right, self.left, self.over
        RA, RLO, RHI, RL, RR, RZ = self.RA, self.RLO, self.RHI, self.RL, self.RR, self.RZ
        toR, toL = {}, {}
        for zr in (1, 0):
            lo[zr].wait_recv()
            self.add(zr, 1, s.LOB, RLO.at[zr])
            toR[zr] = m.go(self.piece(zr, 1, s.ALLB), RL.at[zr, rows_of(s.ALLB), :], right)
            hi[zr].wait_recv()
            self.add(zr, 3, s.HIB, RHI.at[zr])
            toL[zr] = m.go(self.piece(zr, 3, s.ALLB), RR.at[zr, rows_of(s.ALLB), :], left)
            if zr == 1:
                za[2].wait_recv()
                self.add(0, 2, s.ALLA, RA.at[2])
                loA = m.go(self.piece(0, 2, s.LOA), RLO.at[0, rows_of(s.LOA), :], right)
                hiA = m.go(self.piece(0, 2, s.HIA), RHI.at[0, rows_of(s.HIA), :], left)
        za[1].wait_recv()
        self.add(0, 1, s.ALLA, RA.at[1])
        za[3].wait_recv()
        self.add(0, 3, s.ALLA, RA.at[3])
        loA.wait_recv()
        self.add(0, 1, s.LOA, RLO.at[0])
        toRA = m.go(self.piece(0, 1, s.ALLA), RL.at[0, rows_of(s.ALLA), :], right)
        hiA.wait_recv()
        self.add(0, 3, s.HIA, RHI.at[0])
        toLA = m.go(self.piece(0, 3, s.ALLA), RR.at[0, rows_of(s.ALLA), :], left)
        toR[1].wait_recv()
        toL[1].wait_recv()
        self.add(1, 0, s.ALLB, RL.at[1], RR.at[1])
        zb = m.go(self.piece(1, 0, s.ALLB), RZ.at[rows_of(s.ALLB), :], over)
        self.last = (za[0], toRA, toLA), (toR[0], toL[0], zb)

    def total(self, span, which, extra):
        for copy in self.last[which]:
            copy.wait_recv()
        rows = rows_of(span)
        total = self.S[0, rows, :].astype(f32) + self.RL[0, rows, :].astype(f32)
        return total + self.RR[0, rows, :].astype(f32) + extra[rows, :].astype(f32)

    def total_a(self):
        return self.total(DEAL_CUT.ALLA, 0, self.RA.at[0])

    def total_b(self):
        return self.total(DEAL_CUT.ALLB, 1, self.RZ)


SCATTER_COPIES = 4 + 4 + 4 + 2 + 2 + 1
OTHERS = [(dx, dz) for dx in (2, 1, 3, 0) for dz in (1, 0) if (dx, dz) != (0, 0)]


def layer_kernel(lengths, gain1, gain2, tokens, token_lots_in, query, key, value, gate, out_weight, swish, up,
                 down_weight, out,
                 full1, normed1, first, acc, qk, vg,  retained, memory, decay, stats, gated, own_tokens,
                 quarter1, whole1, pack1, mate1, quarter2, whole2, pack2, mate2, second,
                 stage, wpar, wmate, lots, token_lots, pick, unpick, base, wide, full2, normed2, result, spare,
                 S1, RA1, RLO1, RHI1, RL1, RR1, RZ1, S2, RA2, RLO2, RHI2, RL2, RR2, RZ2,
                 local1, local2, load_sem, send, recv):
    place = Place()
    mover = Mover(send, recv)
    req = place.req
    cut = DEAL_CUT
    hand1 = Handout(place, mover, (query, key, value, gate), first, quarter1, whole1, pack1, mate1, local1)
    hand2 = Handout(place, mover, (swish, up), second, quarter2, whole2, pack2, mate2, local2)
    mine = column(place.me)
    hand1.load()
    loads = [pltpu.make_async_copy(tokens, full1.at[:, mine], load_sem.at[0]),
             pltpu.make_async_copy(token_lots_in, own_tokens, load_sem.at[1]),
             pltpu.make_async_copy(out_weight, stage.at[0], load_sem.at[2]),
             pltpu.make_async_copy(down_weight, stage.at[1], load_sem.at[3])]
    for copy in loads:
        copy.start()
    hand2.load()
    mate_core = place.near(0, 0, 1)

    def group(dx, dz):
        return ((place.x + dx + 4) % 4) * 2 + (place.zh + dz) % 2

    greet(group_peers(place) + [(group(dx, dz), place.me) for dx, dz in OTHERS])
    hand1.share()
    loads[0].wait()
    gather = Gather(place, mover, full1, WIDE_CUT)
    gather.start_a()
    gather.start_b()
    hand1.share_whole()

    head = place.me // 2
    log_decay, span_decay = jnp.float32(0.0), jnp.float32(0.0)
    for h in range(H):
        rate = 1.0 - 2.0 ** (-5 - h)
        log_decay = jnp.where(head == h, jnp.float32(math.log(rate)), log_decay)
        span_decay = jnp.where(head == h, jnp.float32(rate ** SPAN), span_decay)
    i = lax.broadcasted_iota(jnp.int32, (SPAN, SPAN), 0)
    j = lax.broadcasted_iota(jnp.int32, (SPAN, SPAN), 1)
    decay[0] = jnp.where(i >= j, jnp.exp((i - j).astype(f32) * log_decay), 0.0)
    decay[1] = jnp.exp((i + 1).astype(f32) * log_decay)
    decay[2] = jnp.exp((SPAN - 1 - i).astype(f32) * log_decay)

    got1 = hand1.spread(range(12))
    gather.first()
    gather.second()
    hand2.share()
    hand2.share_whole()
    gather.finish()

    def normalizer(full, normed, gain):
        def normalize(i, carry):
            rows = pl.ds(pl.multiple_of(i * 32, 32), 32)
            values = full[rows, :].astype(f32)
            scale = lax.rsqrt(jnp.mean(values * values, axis=-1, keepdims=True) + epsilon)
            normed[rows, :] = (values * scale * gain[...]).astype(bf16)
            return carry

        lax.fori_loop(0, full.shape[0] // 32, normalize, 0)

    normalizer(full1, normed1, gain1)
    halves1 = hand1.onward(got1)
    loads[1].wait()
    dealt_tokens = []
    for dx, dz in OTHERS:
        target = group(dx, dz)
        turn = (target - req + 8) % 8
        dealt_tokens.append(mover.go(own_tokens.at[:, turn], token_lots.at[req], (target, place.me)))
    token_lots[req] = own_tokens[:, 0]

    def product(rows, chips):
        total = None
        for chip in chips:
            depth = pl.ds(pl.multiple_of(chip * 256, 256), 256)
            part = jnp.dot(normed1[rows, depth], first[depth, :], preferred_element_type=f32)
            total = part if total is None else total + part
        return total

    def gather_product(chips, fresh):
        def step(i, carry):
            rows = pl.ds(pl.multiple_of(i * SPAN, SPAN), SPAN)
            part = product(rows, chips)
            acc[rows, :] = part if fresh else acc[rows, :] + part
            return carry

        lax.fori_loop(0, LMAX // SPAN, step, 0)

    def chip_of(dy, zr):
        return place.member(-dy, zr, 0) // 2

    await_all(hand1.whole_sent)
    gather_product([chip_of(0, 0), chip_of(0, 1)], True)

    order = [(dy, zr) for zr in (0, 1) for dy in range(4)]

    def set_weight(which):
        loads[2 + which].wait()
        for i, (dy, zr) in enumerate(order):
            wpar[which, 0:256, i * 128:(i + 1) * 128] = stage[which, :, column(place.member(dy, zr, 0))].astype(bf16)
            wmate[which, :, i * 128:(i + 1) * 128] = stage[which, :, column(place.member(dy, zr, 1))].astype(bf16)
        return mover.go(wmate.at[which], wpar.at[which, pl.ds(256, 256), :], mate_core)

    weights = [set_weight(0), set_weight(1)]

    starts, counts = [], []
    start = jnp.int32(0)
    for r in range(8):
        length = lengths[r]
        turn = (req - r + 8) % 8
        count = 16 * (length // 128) + jnp.clip(length % 128 - 16 * turn, 0, 16)
        starts.append(start)
        counts.append(count)
        start = start + count
    row = lax.broadcasted_iota(jnp.int32, (DEAL, 128), 0)
    lane = lax.broadcasted_iota(jnp.int32, (DEAL, 128), 1)
    slot = lax.broadcasted_iota(jnp.int32, (128, DEAL), 0)
    at = lax.broadcasted_iota(jnp.int32, (128, DEAL), 1)
    for r in range(8):
        chosen = (lane == row - starts[r]) & (lane < counts[r])
        pick[:, r * 128:(r + 1) * 128] = jnp.where(chosen, 1.0, 0.0).astype(bf16)
        chosen = (at == slot + starts[r]) & (slot < counts[r])
        unpick[r] = jnp.where(chosen, 1.0, 0.0).astype(bf16)

    await_all(halves1[:8])
    gather_product([chip_of(1, 0), chip_of(3, 0)], False)
    await_all(halves1[8:16])
    gather_product([chip_of(1, 1), chip_of(3, 1)], False)
    got2 = hand2.spread(range(6))
    await_all(halves1[16:])
    key_scale = jnp.where(place.c == 0, 1.0, DK ** (-0.5))
    swapped = []
    for b in range(4):
        rows = pl.ds(b * SPAN, SPAN)
        total = acc[rows, :] + product(rows, [chip_of(2, 0), chip_of(2, 1)])
        qk[place.c, rows, :] = (total[:, :256] * key_scale).astype(bf16)
        ref = qk.at[place.c, rows, :]
        swapped.append(mover.go(ref, ref, mate_core))
        vg[0, rows, :] = total[:, 256:512].astype(bf16)
        vg[1, rows, :] = total[:, 512:].astype(bf16)

    def attend(b):
        rows = pl.ds(b * SPAN, SPAN)
        swapped[b].wait_recv()
        query_block, key_block, value_block = qk[0, rows, :], qk[1, rows, :], vg[0, rows, :]
        scores = lax.dot_general(query_block, key_block, (((1,), (1,)), ((), ())), preferred_element_type=f32)
        total = jnp.dot((scores * decay[0]).astype(bf16), value_block, preferred_element_type=f32)
        if b > 0:
            before = memory[...]
            upper = before.astype(bf16)
            lower = (before - upper.astype(f32)).astype(bf16)
            across = jnp.dot(query_block, upper, preferred_element_type=f32)
            across = across + jnp.dot(query_block, lower, preferred_element_type=f32)
            total = total + across * decay[1]
        if b < 3:
            decayed = key_block.astype(f32) * decay[2]
            upper = decayed.astype(bf16)
            lower = (decayed - upper.astype(f32)).astype(bf16)
            turned = (((0,), (0,)), ((), ()))
            update = lax.dot_general(upper, value_block, turned, preferred_element_type=f32)
            update = update + lax.dot_general(lower, value_block, turned, preferred_element_type=f32)
            memory[...] = update if b == 0 else memory[...] * span_decay + update
        retained[rows, :] = total
        mean = jnp.sum(total, axis=1, keepdims=True) * (1.0 / 256)
        spread = total - mean
        square = jnp.sum(spread * spread, axis=1, keepdims=True)
        lanes = lax.broadcasted_iota(jnp.int32, (SPAN, 128), 1)
        stats[0, b] = jnp.where(lanes < 64, mean, square)
        return mover.go(stats.at[0, b], stats.at[1, b], mate_core)

    def finish(b, told):
        rows = pl.ds(b * SPAN, SPAN)
        told.wait_recv()
        mean, square = stats[0, b, :, 0:1], stats[0, b, :, 64:65]
        mean2, square2 = stats[1, b, :, 0:1], stats[1, b, :, 64:65]
        gap = (mean - mean2) * 0.5
        middle = (mean + mean2) * 0.5
        var = (square + square2) * (1.0 / DV) + gap * gap
        grouped = (retained[rows, :] - middle) * lax.rsqrt(var + epsilon)
        gates = vg[1, rows, :].astype(f32)
        done = (gates / (1.0 + jnp.exp(-gates)) * grouped).astype(bf16)
        gated[2 * b:2 * b + 2] = done.reshape(2, 8, 16, 256)
        two = pl.ds(2 * b, 2)
        sent = []
        for dx, dz in OTHERS:
            target = group(dx, dz)
            turn = (target - req + 8) % 8
            sent.append(mover.go(gated.at[two, turn], lots.at[req, two], (target, place.me)))
        lots[req, 2 * b:2 * b + 2] = gated[2 * b:2 * b + 2, 0]
        return sent

    dealt = []
    told = attend(0)
    for b in range(1, 4):
        later = attend(b)
        dealt += finish(b - 1, told)
        told = later
    dealt += finish(3, told)
    await_all(dealt)
    got2b = hand2.spread(range(6, 12))
    sent = []
    for span in (cut.ALLA, cut.ALLB):
        rows = rows_of(span)
        part = jnp.dot(pick[rows, :], lots[...].reshape(LMAX, 256), preferred_element_type=f32)
        wide[0, rows, 0:256] = part.astype(bf16)
        ref = wide.at[0, rows, pl.ds(0, 256)]
        sent.append(mover.go(ref, wide.at[0, rows, pl.ds(256, 256)], mate_core))

    scatter = Scatter(place, mover, wide.at[0], wpar.at[0], (S1, RA1, RLO1, RHI1, RL1, RR1, RZ1))
    weights[0].wait_recv()
    sent[0].wait_recv()
    scatter.multiply(cut.ALLA)
    scatter.start_a()
    sent[1].wait_recv()
    scatter.multiply(cut.ALLB)
    scatter.start_b()
    halves2 = hand2.onward(got2)
    await_all(dealt_tokens)
    base[...] = jnp.dot(pick[...], token_lots[...].reshape(LMAX, BLK), preferred_element_type=f32).astype(bf16)
    scatter.middle()
    gather = Gather(place, mover, full2, cut)
    full2[rows_of(cut.ALLA), mine] = (base[rows_of(cut.ALLA), :].astype(f32) + scatter.total_a()).astype(bf16)
    gather.start_a()
    full2[rows_of(cut.ALLB), mine] = (base[rows_of(cut.ALLB), :].astype(f32) + scatter.total_b()).astype(bf16)
    gather.start_b()
    halves2 += hand2.onward(got2b)
    gather.first()
    gather.second()
    gather.finish()
    await_all(halves2 + hand2.whole_sent)
    normalizer(full2, normed2, gain2)
    sent = []
    for span in (cut.ALLA, cut.ALLB):
        rows = rows_of(span)
        part = jnp.dot(normed2[rows, :], second[...], preferred_element_type=f32)
        swished = part[:, :256]
        wide[1, rows, 0:256] = (swished / (1.0 + jnp.exp(-swished)) * part[:, 256:]).astype(bf16)
        ref = wide.at[1, rows, pl.ds(0, 256)]
        sent.append(mover.go(ref, wide.at[1, rows, pl.ds(256, 256)], mate_core))
    scatter = Scatter(place, mover, wide.at[1], wpar.at[1], (S2, RA2, RLO2, RHI2, RL2, RR2, RZ2))
    weights[1].wait_recv()
    sent[0].wait_recv()
    scatter.multiply(cut.ALLA)
    scatter.start_a()
    sent[1].wait_recv()
    scatter.multiply(cut.ALLB)
    scatter.start_b()
    scatter.middle()
    for span, total in ((cut.ALLA, scatter.total_a), (cut.ALLB, scatter.total_b)):
        rows = rows_of(span)
        result[rows, :] = (full2[rows, mine].astype(f32) + total()).astype(bf16)
    for r in range(8):
        spare[r] = jnp.dot(unpick[r], result[...], preferred_element_type=f32).astype(bf16).reshape(8, 16, BLK)
    returned = []
    for dx, dz in OTHERS:
        target = group(dx, dz)
        returned.append(mover.go(spare.at[target], out.at[:, (req - target + 8) % 8], (target, place.me)))
    out[:, 0] = spare[req]
    await_all(returned)
    mover.drain()


LAYER_COPIES = 2 * HANDOUT_COPIES + 2 * GATHER_COPIES + 2 * SCATTER_COPIES + 7 * 6 + 2 + 4 + 4 + 4


def layer(*operands):
    vmem = pl.BlockSpec(memory_space=pltpu.VMEM)
    hbm = pl.BlockSpec(memory_space=pl.ANY)
    sums = [
        pltpu.VMEM((8, DEAL, BLK), bf16),
        pltpu.VMEM((4, DEAL, BLK), bf16),
        pltpu.VMEM((2, DEAL, BLK), bf16),
        pltpu.VMEM((2, DEAL, BLK), bf16),
        pltpu.VMEM((2, DEAL, BLK), bf16),
        pltpu.VMEM((2, DEAL, BLK), bf16),
        pltpu.VMEM((DEAL, BLK), bf16),
    ]
    return pl.pallas_call(
        layer_kernel,
        name="layer",
        out_shape=jax.ShapeDtypeStruct((8, 8, 16, BLK), bf16),
        in_specs=[pl.BlockSpec(memory_space=pltpu.SMEM), vmem, vmem] + [hbm] * 10,
        out_specs=vmem,
        scratch_shapes=[
            pltpu.VMEM((LMAX, 2048), bf16),
            pltpu.VMEM((LMAX, 2048), bf16),
            pltpu.VMEM((2048, 768), bf16),
            pltpu.VMEM((LMAX, 768), f32),
            pltpu.VMEM((2, LMAX, 256), bf16),
            pltpu.VMEM((2, LMAX, 256), bf16),

            pltpu.VMEM((LMAX, 256), f32),
            pltpu.VMEM((256, 256), f32),
            pltpu.VMEM((3, SPAN, SPAN), f32),
            pltpu.VMEM((2, 4, SPAN, 128), f32),
            pltpu.VMEM((8, 8, 16, 256), bf16),
            pltpu.VMEM((8, 8, 16, BLK), bf16),
            pltpu.VMEM((32, 12288), f32),
            pltpu.VMEM((2, 128, 1536), f32),
            pltpu.VMEM((16, 32, 768), bf16),
            pltpu.VMEM((3, 128, 768), bf16),
            pltpu.VMEM((32, 8192), f32),
            pltpu.VMEM((2, 128, 1024), f32),
            pltpu.VMEM((16, 32, 512), bf16),
            pltpu.VMEM((3, 128, 512), bf16),
            pltpu.VMEM((2048, 512), bf16),
            pltpu.VMEM((2, 256, 2048), f32),
            pltpu.VMEM((2, 512, 1024), bf16),
            pltpu.VMEM((2, 256, 1024), bf16),
            pltpu.VMEM((8, 8, 16, 256), bf16),
            pltpu.VMEM((8, 8, 16, BLK), bf16),
            pltpu.VMEM((DEAL, LMAX), bf16),
            pltpu.VMEM((8, 128, DEAL), bf16),
            pltpu.VMEM((DEAL, BLK), bf16),
            pltpu.VMEM((2, DEAL, 512), bf16),
            pltpu.VMEM((DEAL, 2048), bf16),
            pltpu.VMEM((DEAL, 2048), bf16),
            pltpu.VMEM((DEAL, BLK), bf16),
            pltpu.VMEM((8, 8, 16, BLK), bf16),
        ] + sums + sums + [
            pltpu.SemaphoreType.DMA((12,)),
            pltpu.SemaphoreType.DMA((6,)),
            pltpu.SemaphoreType.DMA((4,)),
            pltpu.SemaphoreType.DMA((LAYER_COPIES,)),
            pltpu.SemaphoreType.DMA((LAYER_COPIES,)),
        ],
        compiler_params=pltpu.CompilerParams(
            collective_id=0, has_side_effects=True, vmem_limit_bytes=63 * 2**20
        ),
    )(*operands)


def body(
    tokens,
    lengths,
    retention_gain,
    forward_gain,
    query_weight,
    key_weight,
    value_weight,
    gate_weight,
    output_weight,
    swish_weight,
    up_weight,
    down_weight,
):
    rows = tokens.reshape(8, 8, 16, BLK)
    finished = layer(
        lengths, retention_gain.reshape(1, 2048), forward_gain.reshape(1, 2048), tokens[0], rows,
        query_weight, key_weight, value_weight, gate_weight, output_weight, swish_weight, up_weight, down_weight
    )
    return finished.reshape(1, LMAX, BLK)


def solution(mesh):
    placed = (
        P("req", None, "mlp"),
        P(),
        P(),
        P(),
        P("mlp", None),
        P("mlp", None),
        P("mlp", None),
        P("mlp", None),
        P("mlp", None),
        P("mlp", None),
        P("mlp", None),
        P("mlp", None),
    )
    return jax.shard_map(
        body, mesh=mesh, in_specs=placed, out_specs=P("req", None, "mlp"), check_vma=False
    )
```

```python
import math
import jax
import jax.numpy as jnp
from jax import lax
from jax.experimental import pallas as pl
from jax.experimental.pallas import tpu as pltpu
from jax.sharding import PartitionSpec as P

H = 8
DK = 256
DV = 512
SPAN = 256
LMAX = 1024
BLK = 128
REST = [(0, 1), (1, 0), (3, 0), (1, 1), (3, 1), (2, 0), (2, 1)]
DIRECT = [(0, 0, 1)]

epsilon = 1e-05
bf16 = jnp.bfloat16
f32 = jnp.float32


class Cut:
    def __init__(self, rows, cut):
        half, rest = cut // 2, (rows + cut) // 2
        self.ALLA, self.LOA, self.HIA = (0, cut), (0, half), (half, cut)
        self.ALLB, self.LOB, self.HIB = (cut, rows), (cut, rest), (rest, rows)


WIDE_CUT = Cut(1024, 448)
DEAL = 448
DEAL_CUT = Cut(DEAL, 192)


def rows_of(span):
    return pl.ds(span[0], span[1] - span[0])


class Place:
    def __init__(self):
        self.req = lax.axis_index("req")
        self.me = lax.axis_index("mlp")
        self.x = self.req // 2
        self.zh = self.req % 2
        self.y = self.me // 4
        self.z = (self.me // 2) % 2
        self.c = self.me % 2

    def member(self, dy, zr, cc):
        return ((self.y + dy + 4) % 4) * 4 + ((self.z + zr) % 2) * 2 + (self.c + cc) % 2

    def near(self, dy, zr, cc):
        return (self.req, self.member(dy, zr, cc))

    def across(self, dx):
        return (((self.x + dx + 4) % 4) * 2 + self.zh, self.me)


class Mover:
    def __init__(self, send, recv):
        self.send, self.recv, self.count, self.sent = send, recv, 0, []

    def plan(self, src, dst, device):
        i = self.count
        self.count += 1
        return pltpu.make_async_remote_copy(
            src_ref=src, dst_ref=dst, send_sem=self.send.at[i], recv_sem=self.recv.at[i],
            device_id=device, device_id_type=pl.DeviceIdType.MESH,
        )

    def go(self, src, dst, device):
        copy = self.plan(src, dst, device)
        copy.start()
        self.sent.append(copy)
        return copy

    def drain(self):
        for copy in self.sent:
            copy.wait_send()
        self.sent = []


def greet(devices):
    barrier = pltpu.get_barrier_semaphore()
    for device in devices:
        pl.semaphore_signal(barrier, inc=1, device_id=device, device_id_type=pl.DeviceIdType.MESH)
    pl.semaphore_wait(barrier, len(devices))


def column(member):
    return pl.ds(pl.multiple_of(member * BLK, BLK), BLK)


class Gather:
    def __init__(self, place, mover, full, cut):
        self.p, self.m, self.full, self.s = place, mover, full, cut
        self.pend = []

    def at(self, span, dy, zr, cc=0):
        return self.full.at[rows_of(span), column(self.p.member(dy, zr, cc))]

    def pass_on(self, span, dy, zr, targets):
        place = self.p
        ref = self.at(span, dy, zr)
        out = []
        for step in targets:
            device = {"r": place.near(1, 0, 0), "l": place.near(-1, 0, 0),
                      "z": place.near(0, 1, 0), "c": place.near(0, 0, 1)}[step]
            out.append(self.m.go(ref, ref, device))
        return out

    def start_a(self):
        self.a = self.pass_on(self.s.ALLA, 0, 0, "rlzc")

    def start_b(self):
        self.b = self.pass_on(self.s.ALLB, 0, 0, "zrlc")

    def first(self):
        ar, al, az, ac = self.a
        bz, br, bl, bc = self.b
        self.pend += [ac, bc]
        bz.wait_recv()
        self.zb = self.pass_on(self.s.ALLB, 0, 1, "rlc")
        ar.wait_recv()
        self.al1 = self.pass_on(self.s.LOA, -1, 0, "r") + self.pass_on(self.s.ALLA, -1, 0, "zc")
        al.wait_recv()
        self.ar1 = self.pass_on(self.s.HIA, 1, 0, "l") + self.pass_on(self.s.ALLA, 1, 0, "zc")
        br.wait_recv()
        self.bl1 = self.pass_on(self.s.LOB, -1, 0, "r") + self.pass_on(self.s.ALLB, -1, 0, "c")
        bl.wait_recv()
        self.br1 = self.pass_on(self.s.HIB, 1, 0, "l") + self.pass_on(self.s.ALLB, 1, 0, "c")
        az.wait_recv()
        self.pend += self.pass_on(self.s.ALLA, 0, 1, "c")

    def second(self):
        lo, az, ac = self.al1
        hi, az2, ac2 = self.ar1
        self.pend += [ac, ac2]
        lo.wait_recv()
        o1 = self.pass_on(self.s.LOA, -2, 0, "zc")
        hi.wait_recv()
        o2 = self.pass_on(self.s.HIA, 2, 0, "zc")
        zr, zl, zc = self.zb
        self.pend += [zc]
        zr.wait_recv()
        zlo = self.pass_on(self.s.LOB, -1, 1, "r")
        self.pend += self.pass_on(self.s.ALLB, -1, 1, "c")
        zl.wait_recv()
        zhi = self.pass_on(self.s.HIB, 1, 1, "l")
        self.pend += self.pass_on(self.s.ALLB, 1, 1, "c")
        az.wait_recv()
        self.pend += self.pass_on(self.s.ALLA, -1, 1, "c")
        az2.wait_recv()
        self.pend += self.pass_on(self.s.ALLA, 1, 1, "c")
        blo, bc = self.bl1
        bhi, bc2 = self.br1
        self.pend += [bc, bc2]
        blo.wait_recv()
        self.pend += self.pass_on(self.s.LOB, -2, 0, "c")
        bhi.wait_recv()
        self.pend += self.pass_on(self.s.HIB, 2, 0, "c")
        self.pend += [o1[1], o2[1]]
        o1[0].wait_recv()
        self.pend += self.pass_on(self.s.LOA, -2, 1, "c")
        o2[0].wait_recv()
        self.pend += self.pass_on(self.s.HIA, 2, 1, "c")
        zlo[0].wait_recv()
        self.pend += self.pass_on(self.s.LOB, -2, 1, "c")
        zhi[0].wait_recv()
        self.pend += self.pass_on(self.s.HIB, 2, 1, "c")

    def finish(self):
        for copy in self.pend:
            copy.wait_recv()
        self.pend = []


GATHER_COPIES = 38


class Handout:
    def __init__(self, place, mover, refs, out, quarter, whole, pack, mate, local):
        self.p, self.m, self.refs, self.out = place, mover, refs, out
        self.quarter, self.whole, self.pack, self.mate, self.local = quarter, whole, pack, mate, local
        self.rel = [(dy, zr, cc) for dy, zr in REST for cc in (0, 1)]
        self.cols = out.shape[1]

    def load(self):
        place = self.p
        part = pl.ds(pl.multiple_of(place.x * 32, 32), 32)
        self.loads, at = [], 0
        for ref in self.refs:
            self.one(ref.at[part, :], self.quarter.at[:, pl.ds(at, ref.shape[1])])
            at += ref.shape[1]
        for zr in (0,):
            chip = place.member(0, zr, 0) // 2
            at = 0
            for ref in self.refs:
                wide = ref.shape[1] // 8
                self.one(ref.at[:, pl.ds(pl.multiple_of(chip * wide, 128), wide)], self.whole.at[zr, :, pl.ds(at, wide)])
                at += wide

    def one(self, src, dst):
        copy = pltpu.make_async_copy(src, dst, self.local.at[len(self.loads)])
        copy.start()
        self.loads.append(copy)

    def lot(self, member, slot, low=0, high=32):
        return pl.ds(pl.multiple_of(member * 128 + slot * 32 + low, 16), high - low)

    def share(self):
        place = self.p
        for copy in self.loads[:len(self.refs)]:
            copy.wait()
        for d in range(16):
            for i in range(self.cols // 256):
                self.pack[d, :, i * 256:(i + 1) * 256] = self.quarter[:, i * 4096 + self.spot(d, i):][:, :256].astype(bf16)
        self.first = [
            self.m.go(self.pack.at[place.member(*r)], self.out.at[self.lot(place.me, place.x), :], place.near(*r))
            for r in self.rel
        ]

    def spot(self, d, i):
        if i == 0 and len(self.refs) * 256 > self.cols:
            return (d % 2) * 2048 + (d // 2) * 256
        return d * 256

    def share_whole(self):
        place = self.p
        for copy in self.loads[len(self.refs):]:
            copy.wait()
        rows = pl.ds(pl.multiple_of(place.me * 128, 128), 128)
        self.whole_sent = []
        for i in range(self.cols // 256):
            mine = self.whole[0, :, pl.ds(pl.multiple_of(i * 512 + place.c * 256, 128), 256)]
            self.out[rows, i * 256:(i + 1) * 256] = mine.astype(bf16)
        for at, (dy, zr, cc) in enumerate(DIRECT):
            core = (place.c + cc) % 2
            for i in range(self.cols // 256):
                other = self.whole[zr, :, pl.ds(pl.multiple_of(i * 512 + core * 256, 128), 256)]
                self.mate[at, :, i * 256:(i + 1) * 256] = other.astype(bf16)
            self.whole_sent.append(self.m.go(self.mate.at[at], self.out.at[rows, :], place.near(dy, zr, cc)))

    def origin(self, r):
        return self.p.member(-r[0], r[1], r[2])

    def spread(self, which):
        place = self.p
        got = []
        for i in which:
            self.first[i].wait_recv()
            ref = self.out.at[self.lot(self.origin(self.rel[i]), place.x), :]
            got.append((i, self.m.go(ref, ref, place.across(1)), self.m.go(ref, ref, place.across(-1))))
        return got

    def onward(self, got):
        place = self.p
        halves = []
        for i, right, left in got:
            origin = self.origin(self.rel[i])
            right.wait_recv()
            ref = self.out.at[self.lot(origin, (place.x + 3) % 4, 0, 16), :]
            halves.append(self.m.go(ref, ref, place.across(1)))
            left.wait_recv()
            ref = self.out.at[self.lot(origin, (place.x + 1) % 4, 16, 32), :]
            halves.append(self.m.go(ref, ref, place.across(-1)))
        return halves


HANDOUT_COPIES = 14 * 5 + 1


def group_peers(place):
    return [place.near(dy, zr, cc) for dy, zr in REST for cc in (0, 1)] + [place.near(*r) for r in DIRECT]


def await_all(copies):
    for copy in copies:
        copy.wait_recv()


class Scatter:
    def __init__(self, place, mover, wide, wpar, bufs):
        self.p, self.m, self.wide, self.wpar = place, mover, wide, wpar
        self.S, self.RA, self.RLO, self.RHI, self.RL, self.RR, self.RZ = bufs
        self.right, self.left, self.over = place.near(1, 0, 0), place.near(-1, 0, 0), place.near(0, 1, 0)

    def multiply(self, span):
        rows = rows_of(span)
        for i in range(4):
            part = jnp.dot(self.wide[rows, :], self.wpar[:, i * 256:(i + 1) * 256], preferred_element_type=f32)
            part = part.astype(bf16)
            self.S[2 * i, rows, :] = part[:, :128]
            self.S[2 * i + 1, rows, :] = part[:, 128:]

    def piece(self, zr, dy, span):
        return self.S.at[zr * 4 + dy, rows_of(span), :]

    def add(self, zr, dy, span, *others):
        rows = rows_of(span)
        total = self.S[zr * 4 + dy, rows, :].astype(f32)
        for other in others:
            total = total + other[rows, :].astype(f32)
        self.S[zr * 4 + dy, rows, :] = total.astype(bf16)

    def start_a(self):
        s = DEAL_CUT
        self.za = {dy: self.m.go(self.piece(1, dy, s.ALLA), self.RA.at[dy, rows_of(s.ALLA), :], self.over)
                   for dy in (2, 1, 3, 0)}

    def start_b(self):
        s = DEAL_CUT
        self.lo, self.hi = {}, {}
        for zr in (1, 0):
            self.lo[zr] = self.m.go(self.piece(zr, 2, s.LOB), self.RLO.at[zr, rows_of(s.LOB), :], self.right)
            self.hi[zr] = self.m.go(self.piece(zr, 2, s.HIB), self.RHI.at[zr, rows_of(s.HIB), :], self.left)

    def middle(self):
        s, m = DEAL_CUT, self.m
        lo, hi, za = self.lo, self.hi, self.za
        right, left, over = self.right, self.left, self.over
        RA, RLO, RHI, RL, RR, RZ = self.RA, self.RLO, self.RHI, self.RL, self.RR, self.RZ
        toR, toL = {}, {}
        for zr in (1, 0):
            lo[zr].wait_recv()
            self.add(zr, 1, s.LOB, RLO.at[zr])
            toR[zr] = m.go(self.piece(zr, 1, s.ALLB), RL.at[zr, rows_of(s.ALLB), :], right)
            hi[zr].wait_recv()
            self.add(zr, 3, s.HIB, RHI.at[zr])
            toL[zr] = m.go(self.piece(zr, 3, s.ALLB), RR.at[zr, rows_of(s.ALLB), :], left)
            if zr == 1:
                za[2].wait_recv()
                self.add(0, 2, s.ALLA, RA.at[2])
                loA = m.go(self.piece(0, 2, s.LOA), RLO.at[0, rows_of(s.LOA), :], right)
                hiA = m.go(self.piece(0, 2, s.HIA), RHI.at[0, rows_of(s.HIA), :], left)
        za[1].wait_recv()
        self.add(0, 1, s.ALLA, RA.at[1])
        za[3].wait_recv()
        self.add(0, 3, s.ALLA, RA.at[3])
        loA.wait_recv()
        self.add(0, 1, s.LOA, RLO.at[0])
        toRA = m.go(self.piece(0, 1, s.ALLA), RL.at[0, rows_of(s.ALLA), :], right)
        hiA.wait_recv()
        self.add(0, 3, s.HIA, RHI.at[0])
        toLA = m.go(self.piece(0, 3, s.ALLA), RR.at[0, rows_of(s.ALLA), :], left)
        toR[1].wait_recv()
        toL[1].wait_recv()
        self.add(1, 0, s.ALLB, RL.at[1], RR.at[1])
        zb = m.go(self.piece(1, 0, s.ALLB), RZ.at[rows_of(s.ALLB), :], over)
        self.last = (za[0], toRA, toLA), (toR[0], toL[0], zb)

    def total(self, span, which, extra):
        for copy in self.last[which]:
            copy.wait_recv()
        rows = rows_of(span)
        total = self.S[0, rows, :].astype(f32) + self.RL[0, rows, :].astype(f32)
        return total + self.RR[0, rows, :].astype(f32) + extra[rows, :].astype(f32)

    def total_a(self):
        return self.total(DEAL_CUT.ALLA, 0, self.RA.at[0])

    def total_b(self):
        return self.total(DEAL_CUT.ALLB, 1, self.RZ)


SCATTER_COPIES = 4 + 4 + 4 + 2 + 2 + 1
OTHERS = [(dx, dz) for dx in (2, 1, 3, 0) for dz in (1, 0) if (dx, dz) != (0, 0)]


def layer_kernel(lengths, gain1, gain2, tokens, token_lots_in, query, key, value, gate, out_weight, swish, up,
                 down_weight, out,
                 full1, normed1, first, acc, qk, vg,  retained, memory, decay, stats, gated, own_tokens,
                 quarter1, whole1, pack1, mate1, quarter2, whole2, pack2, mate2, second,
                 stage, wpar, wmate, lots, token_lots, pick, unpick, base, wide, full2, normed2, result, spare,
                 S1, RA1, RLO1, RHI1, RL1, RR1, RZ1, S2, RA2, RLO2, RHI2, RL2, RR2, RZ2,
                 local1, local2, load_sem, send, recv):
    place = Place()
    mover = Mover(send, recv)
    req = place.req
    cut = DEAL_CUT
    hand1 = Handout(place, mover, (query, key, value, gate), first, quarter1, whole1, pack1, mate1, local1)
    hand2 = Handout(place, mover, (swish, up), second, quarter2, whole2, pack2, mate2, local2)
    mine = column(place.me)
    hand1.load()
    loads = [pltpu.make_async_copy(tokens, full1.at[:, mine], load_sem.at[0]),
             pltpu.make_async_copy(token_lots_in, own_tokens, load_sem.at[1]),
             pltpu.make_async_copy(out_weight, stage.at[0], load_sem.at[2]),
             pltpu.make_async_copy(down_weight, stage.at[1], load_sem.at[3])]
    for copy in loads:
        copy.start()
    hand2.load()
    mate_core = place.near(0, 0, 1)

    def group(dx, dz):
        return ((place.x + dx + 4) % 4) * 2 + (place.zh + dz) % 2

    greet(group_peers(place) + [(group(dx, dz), place.me) for dx, dz in OTHERS])
    hand1.share()
    loads[0].wait()
    gather = Gather(place, mover, full1, WIDE_CUT)
    gather.start_a()
    gather.start_b()
    hand1.share_whole()

    head = place.me // 2
    log_decay, span_decay = jnp.float32(0.0), jnp.float32(0.0)
    for h in range(H):
        rate = 1.0 - 2.0 ** (-5 - h)
        log_decay = jnp.where(head == h, jnp.float32(math.log(rate)), log_decay)
        span_decay = jnp.where(head == h, jnp.float32(rate ** SPAN), span_decay)
    i = lax.broadcasted_iota(jnp.int32, (SPAN, SPAN), 0)
    j = lax.broadcasted_iota(jnp.int32, (SPAN, SPAN), 1)
    decay[0] = jnp.where(i >= j, jnp.exp((i - j).astype(f32) * log_decay), 0.0)
    decay[1] = jnp.exp((i + 1).astype(f32) * log_decay)
    decay[2] = jnp.exp((SPAN - 1 - i).astype(f32) * log_decay)

    got1 = hand1.spread(range(14))
    gather.first()
    halves1 = hand1.onward(got1[:8])
    gather.second()
    halves1 += hand1.onward(got1[8:])
    gather.finish()

    def normalizer(full, normed, gain):
        def normalize(i, carry):
            rows = pl.ds(pl.multiple_of(i * 32, 32), 32)
            values = full[rows, :].astype(f32)
            scale = lax.rsqrt(jnp.mean(values * values, axis=-1, keepdims=True) + epsilon)
            normed[rows, :] = (values * scale * gain[...]).astype(bf16)
            return carry

        lax.fori_loop(0, full.shape[0] // 32, normalize, 0)

    normalizer(full1, normed1, gain1)
    hand2.share()
    hand2.share_whole()
    loads[1].wait()
    dealt_tokens = []
    for dx, dz in OTHERS:
        target = group(dx, dz)
        turn = (target - req + 8) % 8
        dealt_tokens.append(mover.go(own_tokens.at[:, turn], token_lots.at[req], (target, place.me)))
    token_lots[req] = own_tokens[:, 0]

    def product(rows, chips):
        total = None
        for chip in chips:
            depth = pl.ds(pl.multiple_of(chip * 256, 256), 256)
            part = jnp.dot(normed1[rows, depth], first[depth, :], preferred_element_type=f32)
            total = part if total is None else total + part
        return total

    def gather_product(chips, fresh):
        def step(i, carry):
            rows = pl.ds(pl.multiple_of(i * SPAN, SPAN), SPAN)
            part = product(rows, chips)
            acc[rows, :] = part if fresh else acc[rows, :] + part
            return carry

        lax.fori_loop(0, LMAX // SPAN, step, 0)

    def chip_of(dy, zr):
        return place.member(-dy, zr, 0) // 2

    await_all(hand1.whole_sent + halves1[:8])
    gather_product([chip_of(0, 0), chip_of(0, 1), chip_of(1, 0)], True)

    order = [(dy, zr) for zr in (0, 1) for dy in range(4)]

    def set_weight(which):
        loads[2 + which].wait()
        for i, (dy, zr) in enumerate(order):
            wpar[which, 0:256, i * 128:(i + 1) * 128] = stage[which, :, column(place.member(dy, zr, 0))].astype(bf16)
            wmate[which, :, i * 128:(i + 1) * 128] = stage[which, :, column(place.member(dy, zr, 1))].astype(bf16)
        return mover.go(wmate.at[which], wpar.at[which, pl.ds(256, 256), :], mate_core)

    weights = [set_weight(0), set_weight(1)]

    starts, counts = [], []
    start = jnp.int32(0)
    for r in range(8):
        length = lengths[r]
        turn = (req - r + 8) % 8
        count = 16 * (length // 128) + jnp.clip(length % 128 - 16 * turn, 0, 16)
        starts.append(start)
        counts.append(count)
        start = start + count
    row = lax.broadcasted_iota(jnp.int32, (DEAL, 128), 0)
    lane = lax.broadcasted_iota(jnp.int32, (DEAL, 128), 1)
    slot = lax.broadcasted_iota(jnp.int32, (128, DEAL), 0)
    at = lax.broadcasted_iota(jnp.int32, (128, DEAL), 1)
    for r in range(8):
        chosen = (lane == row - starts[r]) & (lane < counts[r])
        pick[:, r * 128:(r + 1) * 128] = jnp.where(chosen, 1.0, 0.0).astype(bf16)
        chosen = (at == slot + starts[r]) & (slot < counts[r])
        unpick[r] = jnp.where(chosen, 1.0, 0.0).astype(bf16)

    await_all(halves1[8:16])
    gather_product([chip_of(3, 0), chip_of(1, 1)], False)
    await_all(halves1[16:24])
    gather_product([chip_of(3, 1), chip_of(2, 0)], False)
    got2 = hand2.spread(range(7))
    await_all(halves1[24:])
    key_scale = jnp.where(place.c == 0, 1.0, DK ** (-0.5))
    swapped = []

    def project(b):
        rows = pl.ds(b * SPAN, SPAN)
        total = acc[rows, :] + product(rows, [chip_of(2, 1)])
        qk[place.c, rows, :] = (total[:, :256] * key_scale).astype(bf16)
        ref = qk.at[place.c, rows, :]
        swapped.append(mover.go(ref, ref, mate_core))
        vg[0, rows, :] = total[:, 256:512].astype(bf16)
        vg[1, rows, :] = total[:, 512:].astype(bf16)

    def attend(b):
        rows = pl.ds(b * SPAN, SPAN)
        swapped[b].wait_recv()
        query_block, key_block, value_block = qk[0, rows, :], qk[1, rows, :], vg[0, rows, :]
        scores = lax.dot_general(query_block, key_block, (((1,), (1,)), ((), ())), preferred_element_type=f32)
        total = jnp.dot((scores * decay[0]).astype(bf16), value_block, preferred_element_type=f32)
        if b > 0:
            before = memory[...]
            upper = before.astype(bf16)
            lower = (before - upper.astype(f32)).astype(bf16)
            across = jnp.dot(query_block, upper, preferred_element_type=f32)
            across = across + jnp.dot(query_block, lower, preferred_element_type=f32)
            total = total + across * decay[1]
        if b < 3:
            decayed = key_block.astype(f32) * decay[2]
            upper = decayed.astype(bf16)
            lower = (decayed - upper.astype(f32)).astype(bf16)
            turned = (((0,), (0,)), ((), ()))
            update = lax.dot_general(upper, value_block, turned, preferred_element_type=f32)
            update = update + lax.dot_general(lower, value_block, turned, preferred_element_type=f32)
            memory[...] = update if b == 0 else memory[...] * span_decay + update
        retained[rows, :] = total
        mean = jnp.sum(total, axis=1, keepdims=True) * (1.0 / 256)
        spread = total - mean
        square = jnp.sum(spread * spread, axis=1, keepdims=True)
        lanes = lax.broadcasted_iota(jnp.int32, (SPAN, 128), 1)
        stats[0, b] = jnp.where(lanes < 64, mean, square)
        return mover.go(stats.at[0, b], stats.at[1, b], mate_core)

    def finish(b, told):
        rows = pl.ds(b * SPAN, SPAN)
        told.wait_recv()
        mean, square = stats[0, b, :, 0:1], stats[0, b, :, 64:65]
        mean2, square2 = stats[1, b, :, 0:1], stats[1, b, :, 64:65]
        gap = (mean - mean2) * 0.5
        middle = (mean + mean2) * 0.5
        var = (square + square2) * (1.0 / DV) + gap * gap
        grouped = (retained[rows, :] - middle) * lax.rsqrt(var + epsilon)
        gates = vg[1, rows, :].astype(f32)
        done = (gates / (1.0 + jnp.exp(-gates)) * grouped).astype(bf16)
        gated[2 * b:2 * b + 2] = done.reshape(2, 8, 16, 256)
        two = pl.ds(2 * b, 2)
        sent = []
        for dx, dz in OTHERS:
            target = group(dx, dz)
            turn = (target - req + 8) % 8
            sent.append(mover.go(gated.at[two, turn], lots.at[req, two], (target, place.me)))
        lots[req, 2 * b:2 * b + 2] = gated[2 * b:2 * b + 2, 0]
        return sent

    dealt, told = [], []
    project(0)
    for b in range(4):
        if b < 3:
            project(b + 1)
        told.append(attend(b))
        if b > 0:
            dealt += finish(b - 1, told[b - 1])
    dealt += finish(3, told[3])
    await_all(dealt)
    got2b = hand2.spread(range(7, 14))
    sent = []
    for span in (cut.ALLA, cut.ALLB):
        rows = rows_of(span)
        part = jnp.dot(pick[rows, :], lots[...].reshape(LMAX, 256), preferred_element_type=f32)
        wide[0, rows, 0:256] = part.astype(bf16)
        ref = wide.at[0, rows, pl.ds(0, 256)]
        sent.append(mover.go(ref, wide.at[0, rows, pl.ds(256, 256)], mate_core))

    scatter = Scatter(place, mover, wide.at[0], wpar.at[0], (S1, RA1, RLO1, RHI1, RL1, RR1, RZ1))
    weights[0].wait_recv()
    sent[0].wait_recv()
    scatter.multiply(cut.ALLA)
    scatter.start_a()
    sent[1].wait_recv()
    scatter.multiply(cut.ALLB)
    scatter.start_b()
    halves2 = hand2.onward(got2)
    await_all(dealt_tokens)
    base[...] = jnp.dot(pick[...], token_lots[...].reshape(LMAX, BLK), preferred_element_type=f32).astype(bf16)
    scatter.middle()
    gather = Gather(place, mover, full2, cut)
    full2[rows_of(cut.ALLA), mine] = (base[rows_of(cut.ALLA), :].astype(f32) + scatter.total_a()).astype(bf16)
    gather.start_a()
    full2[rows_of(cut.ALLB), mine] = (base[rows_of(cut.ALLB), :].astype(f32) + scatter.total_b()).astype(bf16)
    gather.start_b()
    halves2 += hand2.onward(got2b)
    gather.first()
    gather.second()
    gather.finish()
    await_all(halves2 + hand2.whole_sent)
    normalizer(full2, normed2, gain2)
    sent = []
    for span in (cut.ALLA, cut.ALLB):
        rows = rows_of(span)
        part = jnp.dot(normed2[rows, :], second[...], preferred_element_type=f32)
        swished = part[:, :256]
        wide[1, rows, 0:256] = (swished / (1.0 + jnp.exp(-swished)) * part[:, 256:]).astype(bf16)
        ref = wide.at[1, rows, pl.ds(0, 256)]
        sent.append(mover.go(ref, wide.at[1, rows, pl.ds(256, 256)], mate_core))
    scatter = Scatter(place, mover, wide.at[1], wpar.at[1], (S2, RA2, RLO2, RHI2, RL2, RR2, RZ2))
    weights[1].wait_recv()
    sent[0].wait_recv()
    scatter.multiply(cut.ALLA)
    scatter.start_a()
    sent[1].wait_recv()
    scatter.multiply(cut.ALLB)
    scatter.start_b()
    scatter.middle()
    for span, total in ((cut.ALLA, scatter.total_a), (cut.ALLB, scatter.total_b)):
        rows = rows_of(span)
        result[rows, :] = (full2[rows, mine].astype(f32) + total()).astype(bf16)
    for r in range(8):
        spare[r] = jnp.dot(unpick[r], result[...], preferred_element_type=f32).astype(bf16).reshape(8, 16, BLK)
    returned = []
    for dx, dz in OTHERS:
        target = group(dx, dz)
        returned.append(mover.go(spare.at[target], out.at[:, (req - target + 8) % 8], (target, place.me)))
    out[:, 0] = spare[req]
    await_all(returned)
    mover.drain()


LAYER_COPIES = 2 * HANDOUT_COPIES + 2 * GATHER_COPIES + 2 * SCATTER_COPIES + 7 * 6 + 2 + 4 + 4 + 4


def layer(*operands):
    vmem = pl.BlockSpec(memory_space=pltpu.VMEM)
    hbm = pl.BlockSpec(memory_space=pl.ANY)
    sums = [
        pltpu.VMEM((8, DEAL, BLK), bf16),
        pltpu.VMEM((4, DEAL, BLK), bf16),
        pltpu.VMEM((2, DEAL, BLK), bf16),
        pltpu.VMEM((2, DEAL, BLK), bf16),
        pltpu.VMEM((2, DEAL, BLK), bf16),
        pltpu.VMEM((2, DEAL, BLK), bf16),
        pltpu.VMEM((DEAL, BLK), bf16),
    ]
    return pl.pallas_call(
        layer_kernel,
        name="layer",
        out_shape=jax.ShapeDtypeStruct((8, 8, 16, BLK), bf16),
        in_specs=[pl.BlockSpec(memory_space=pltpu.SMEM), vmem, vmem] + [hbm] * 10,
        out_specs=vmem,
        scratch_shapes=[
            pltpu.VMEM((LMAX, 2048), bf16),
            pltpu.VMEM((LMAX, 2048), bf16),
            pltpu.VMEM((2048, 768), bf16),
            pltpu.VMEM((LMAX, 768), f32),
            pltpu.VMEM((2, LMAX, 256), bf16),
            pltpu.VMEM((2, LMAX, 256), bf16),

            pltpu.VMEM((LMAX, 256), f32),
            pltpu.VMEM((256, 256), f32),
            pltpu.VMEM((3, SPAN, SPAN), f32),
            pltpu.VMEM((2, 4, SPAN, 128), f32),
            pltpu.VMEM((8, 8, 16, 256), bf16),
            pltpu.VMEM((8, 8, 16, BLK), bf16),
            pltpu.VMEM((32, 12288), f32),
            pltpu.VMEM((1, 128, 1536), f32),
            pltpu.VMEM((16, 32, 768), bf16),
            pltpu.VMEM((1, 128, 768), bf16),
            pltpu.VMEM((32, 8192), f32),
            pltpu.VMEM((1, 128, 1024), f32),
            pltpu.VMEM((16, 32, 512), bf16),
            pltpu.VMEM((1, 128, 512), bf16),
            pltpu.VMEM((2048, 512), bf16),
            pltpu.VMEM((2, 256, 2048), f32),
            pltpu.VMEM((2, 512, 1024), bf16),
            pltpu.VMEM((2, 256, 1024), bf16),
            pltpu.VMEM((8, 8, 16, 256), bf16),
            pltpu.VMEM((8, 8, 16, BLK), bf16),
            pltpu.VMEM((DEAL, LMAX), bf16),
            pltpu.VMEM((8, 128, DEAL), bf16),
            pltpu.VMEM((DEAL, BLK), bf16),
            pltpu.VMEM((2, DEAL, 512), bf16),
            pltpu.VMEM((DEAL, 2048), bf16),
            pltpu.VMEM((DEAL, 2048), bf16),
            pltpu.VMEM((DEAL, BLK), bf16),
            pltpu.VMEM((8, 8, 16, BLK), bf16),
        ] + sums + sums + [
            pltpu.SemaphoreType.DMA((8,)),
            pltpu.SemaphoreType.DMA((4,)),
            pltpu.SemaphoreType.DMA((4,)),
            pltpu.SemaphoreType.DMA((LAYER_COPIES,)),
            pltpu.SemaphoreType.DMA((LAYER_COPIES,)),
        ],
        compiler_params=pltpu.CompilerParams(
            collective_id=0, has_side_effects=True, vmem_limit_bytes=63 * 2**20
        ),
    )(*operands)


def body(
    tokens,
    lengths,
    retention_gain,
    forward_gain,
    query_weight,
    key_weight,
    value_weight,
    gate_weight,
    output_weight,
    swish_weight,
    up_weight,
    down_weight,
):
    rows = tokens.reshape(8, 8, 16, BLK)
    finished = layer(
        lengths, retention_gain.reshape(1, 2048), forward_gain.reshape(1, 2048), tokens[0], rows,
        query_weight, key_weight, value_weight, gate_weight, output_weight, swish_weight, up_weight, down_weight
    )
    return finished.reshape(1, LMAX, BLK)


def solution(mesh):
    placed = (
        P("req", None, "mlp"),
        P(),
        P(),
        P(),
        P("mlp", None),
        P("mlp", None),
        P("mlp", None),
        P("mlp", None),
        P("mlp", None),
        P("mlp", None),
        P("mlp", None),
        P("mlp", None),
    )
    return jax.shard_map(
        body, mesh=mesh, in_specs=placed, out_specs=P("req", None, "mlp"), check_vma=False
    )
```

```python
import math
import jax
import jax.numpy as jnp
from jax import lax
from jax.experimental import pallas as pl
from jax.experimental.pallas import tpu as pltpu
from jax.sharding import PartitionSpec as P

H = 8
DK = 256
DV = 512
SPAN = 256
LMAX = 1024
BLK = 128
REST = [(0, 1), (1, 0), (3, 0), (1, 1), (3, 1), (2, 0), (2, 1)]
DIRECT = [(0, 0, 1)]

epsilon = 1e-05
bf16 = jnp.bfloat16
f32 = jnp.float32


class Cut:
    def __init__(self, rows, cut):
        half, rest = cut // 2, (rows + cut) // 2
        self.ALLA, self.LOA, self.HIA = (0, cut), (0, half), (half, cut)
        self.ALLB, self.LOB, self.HIB = (cut, rows), (cut, rest), (rest, rows)


WIDE_CUT = Cut(1024, 416)
DEAL = 448
DEAL_CUT = Cut(DEAL, 192)


def rows_of(span):
    return pl.ds(span[0], span[1] - span[0])


class Place:
    def __init__(self):
        self.req = lax.axis_index("req")
        self.me = lax.axis_index("mlp")
        self.x = self.req // 2
        self.zh = self.req % 2
        self.y = self.me // 4
        self.z = (self.me // 2) % 2
        self.c = self.me % 2

    def member(self, dy, zr, cc):
        return ((self.y + dy + 4) % 4) * 4 + ((self.z + zr) % 2) * 2 + (self.c + cc) % 2

    def near(self, dy, zr, cc):
        return (self.req, self.member(dy, zr, cc))

    def across(self, dx):
        return (((self.x + dx + 4) % 4) * 2 + self.zh, self.me)


class Mover:
    def __init__(self, send, recv):
        self.send, self.recv, self.count, self.sent = send, recv, 0, []

    def plan(self, src, dst, device):
        i = self.count
        self.count += 1
        return pltpu.make_async_remote_copy(
            src_ref=src, dst_ref=dst, send_sem=self.send.at[i], recv_sem=self.recv.at[i],
            device_id=device, device_id_type=pl.DeviceIdType.MESH,
        )

    def go(self, src, dst, device):
        copy = self.plan(src, dst, device)
        copy.start()
        self.sent.append(copy)
        return copy

    def drain(self):
        for copy in self.sent:
            copy.wait_send()
        self.sent = []


def greet(devices):
    barrier = pltpu.get_barrier_semaphore()
    for device in devices:
        pl.semaphore_signal(barrier, inc=1, device_id=device, device_id_type=pl.DeviceIdType.MESH)
    pl.semaphore_wait(barrier, len(devices))


def column(member):
    return pl.ds(pl.multiple_of(member * BLK, BLK), BLK)


class Gather:
    def __init__(self, place, mover, full, cut):
        self.p, self.m, self.full, self.s = place, mover, full, cut
        self.need = {}

    def at(self, span, dy, zr):
        return self.full.at[rows_of(span), column(self.p.member(dy, zr, 0))]

    def pass_on(self, span, dy, zr, targets):
        place = self.p
        ref = self.at(span, dy, zr)
        out = []
        for step in targets:
            device = {"r": place.near(1, 0, 0), "l": place.near(-1, 0, 0),
                      "z": place.near(0, 1, 0), "c": place.near(0, 0, 1)}[step]
            copy = self.m.go(ref, ref, device)
            if step == "c":
                self.need.setdefault((dy % 4, zr), []).append(copy)
            else:
                out.append(copy)
        return out

    def start_a(self):
        self.a = self.pass_on(self.s.ALLA, 0, 0, "rlzc")

    def start_b(self):
        self.b = self.pass_on(self.s.ALLB, 0, 0, "zrlc")

    def first(self):
        ar, al, az = self.a
        bz, br, bl = self.b
        bz.wait_recv()
        self.zb = self.pass_on(self.s.ALLB, 0, 1, "rlc")
        ar.wait_recv()
        self.al1 = self.pass_on(self.s.LOA, -1, 0, "r") + self.pass_on(self.s.ALLA, -1, 0, "zc")
        al.wait_recv()
        self.ar1 = self.pass_on(self.s.HIA, 1, 0, "l") + self.pass_on(self.s.ALLA, 1, 0, "zc")
        br.wait_recv()
        self.bl1 = self.pass_on(self.s.LOB, -1, 0, "r") + self.pass_on(self.s.ALLB, -1, 0, "c")
        bl.wait_recv()
        self.br1 = self.pass_on(self.s.HIB, 1, 0, "l") + self.pass_on(self.s.ALLB, 1, 0, "c")
        az.wait_recv()
        self.pass_on(self.s.ALLA, 0, 1, "c")

    def second(self):
        lo, az = self.al1
        hi, az2 = self.ar1
        lo.wait_recv()
        self.o1 = self.pass_on(self.s.LOA, -2, 0, "zc")
        hi.wait_recv()
        self.o2 = self.pass_on(self.s.HIA, 2, 0, "zc")
        zr, zl = self.zb
        zr.wait_recv()
        self.zlo = self.pass_on(self.s.LOB, -1, 1, "r") + self.pass_on(self.s.ALLB, -1, 1, "c")
        zl.wait_recv()
        self.zhi = self.pass_on(self.s.HIB, 1, 1, "l") + self.pass_on(self.s.ALLB, 1, 1, "c")
        az.wait_recv()
        self.pass_on(self.s.ALLA, -1, 1, "c")
        az2.wait_recv()
        self.pass_on(self.s.ALLA, 1, 1, "c")

    def third(self):
        self.bl1[0].wait_recv()
        self.pass_on(self.s.LOB, -2, 0, "c")
        self.br1[0].wait_recv()
        self.pass_on(self.s.HIB, 2, 0, "c")
        self.o1[0].wait_recv()
        self.pass_on(self.s.LOA, -2, 1, "c")
        self.o2[0].wait_recv()
        self.pass_on(self.s.HIA, 2, 1, "c")
        self.zlo[0].wait_recv()
        self.pass_on(self.s.LOB, -2, 1, "c")
        self.zhi[0].wait_recv()
        self.pass_on(self.s.HIB, 2, 1, "c")

    def ready(self, dy, zr):
        for copy in self.need.pop((dy % 4, zr), ()):
            copy.wait_recv()

    def finish(self):
        for key in list(self.need):
            self.ready(*key)


GATHER_COPIES = 38


class Handout:
    def __init__(self, place, mover, refs, out, quarter, whole, pack, mate, local):
        self.p, self.m, self.refs, self.out = place, mover, refs, out
        self.quarter, self.whole, self.pack, self.mate, self.local = quarter, whole, pack, mate, local
        self.rel = [(dy, zr, cc) for dy, zr in REST for cc in (0, 1)]
        self.cols = out.shape[1]

    def load(self):
        place = self.p
        part = pl.ds(pl.multiple_of(place.x * 32, 32), 32)
        self.loads, at = [], 0
        for ref in self.refs:
            self.one(ref.at[part, :], self.quarter.at[:, pl.ds(at, ref.shape[1])])
            at += ref.shape[1]
        for zr in (0,):
            chip = place.member(0, zr, 0) // 2
            at = 0
            for ref in self.refs:
                wide = ref.shape[1] // 8
                self.one(ref.at[:, pl.ds(pl.multiple_of(chip * wide, 128), wide)], self.whole.at[zr, :, pl.ds(at, wide)])
                at += wide

    def one(self, src, dst):
        copy = pltpu.make_async_copy(src, dst, self.local.at[len(self.loads)])
        copy.start()
        self.loads.append(copy)

    def lot(self, member, slot, low=0, high=32):
        return pl.ds(pl.multiple_of(member * 128 + slot * 32 + low, 16), high - low)

    def prepare(self):
        for copy in self.loads[:len(self.refs)]:
            copy.wait()
        for d in range(16):
            for i in range(self.cols // 256):
                self.pack[d, :, i * 256:(i + 1) * 256] = self.quarter[:, i * 4096 + self.spot(d, i):][:, :256].astype(bf16)

    def share(self):
        place = self.p
        self.first = [
            self.m.go(self.pack.at[place.member(*r)], self.out.at[self.lot(place.me, place.x), :], place.near(*r))
            for r in self.rel
        ]

    def spot(self, d, i):
        if i == 0 and len(self.refs) * 256 > self.cols:
            return (d % 2) * 2048 + (d // 2) * 256
        return d * 256

    def share_whole(self):
        place = self.p
        for copy in self.loads[len(self.refs):]:
            copy.wait()
        rows = pl.ds(pl.multiple_of(place.me * 128, 128), 128)
        self.whole_sent = []
        for i in range(self.cols // 256):
            mine = self.whole[0, :, pl.ds(pl.multiple_of(i * 512 + place.c * 256, 128), 256)]
            self.out[rows, i * 256:(i + 1) * 256] = mine.astype(bf16)
        for at, (dy, zr, cc) in enumerate(DIRECT):
            core = (place.c + cc) % 2
            for i in range(self.cols // 256):
                other = self.whole[zr, :, pl.ds(pl.multiple_of(i * 512 + core * 256, 128), 256)]
                self.mate[at, :, i * 256:(i + 1) * 256] = other.astype(bf16)
            self.whole_sent.append(self.m.go(self.mate.at[at], self.out.at[rows, :], place.near(dy, zr, cc)))

    def origin(self, r):
        return self.p.member(-r[0], r[1], r[2])

    def spread(self, which):
        place = self.p
        got = []
        for i in which:
            self.first[i].wait_recv()
            ref = self.out.at[self.lot(self.origin(self.rel[i]), place.x), :]
            got.append((i, self.m.go(ref, ref, place.across(1)), self.m.go(ref, ref, place.across(-1))))
        return got

    def onward(self, got):
        place = self.p
        halves = []
        for i, right, left in got:
            origin = self.origin(self.rel[i])
            right.wait_recv()
            ref = self.out.at[self.lot(origin, (place.x + 3) % 4, 0, 16), :]
            halves.append(self.m.go(ref, ref, place.across(1)))
            left.wait_recv()
            ref = self.out.at[self.lot(origin, (place.x + 1) % 4, 16, 32), :]
            halves.append(self.m.go(ref, ref, place.across(-1)))
        return halves


HANDOUT_COPIES = 14 * 5 + 1


def group_peers(place):
    return [place.near(dy, zr, cc) for dy, zr in REST for cc in (0, 1)] + [place.near(*r) for r in DIRECT]


def await_all(copies):
    for copy in copies:
        copy.wait_recv()


class Scatter:
    def __init__(self, place, mover, wide, wpar, bufs):
        self.p, self.m, self.wide, self.wpar = place, mover, wide, wpar
        self.S, self.RA, self.RLO, self.RHI, self.RL, self.RR, self.RZ = bufs
        self.right, self.left, self.over = place.near(1, 0, 0), place.near(-1, 0, 0), place.near(0, 1, 0)

    def multiply(self, span):
        rows = rows_of(span)
        for i in range(4):
            part = jnp.dot(self.wide[rows, :], self.wpar[:, i * 256:(i + 1) * 256], preferred_element_type=f32)
            part = part.astype(bf16)
            self.S[2 * i, rows, :] = part[:, :128]
            self.S[2 * i + 1, rows, :] = part[:, 128:]

    def piece(self, zr, dy, span):
        return self.S.at[zr * 4 + dy, rows_of(span), :]

    def add(self, zr, dy, span, *others):
        rows = rows_of(span)
        total = self.S[zr * 4 + dy, rows, :].astype(f32)
        for other in others:
            total = total + other[rows, :].astype(f32)
        self.S[zr * 4 + dy, rows, :] = total.astype(bf16)

    def start_a(self):
        s = DEAL_CUT
        self.za = {dy: self.m.go(self.piece(1, dy, s.ALLA), self.RA.at[dy, rows_of(s.ALLA), :], self.over)
                   for dy in (2, 1, 3, 0)}

    def start_b(self):
        s = DEAL_CUT
        self.lo, self.hi = {}, {}
        for zr in (1, 0):
            self.lo[zr] = self.m.go(self.piece(zr, 2, s.LOB), self.RLO.at[zr, rows_of(s.LOB), :], self.right)
            self.hi[zr] = self.m.go(self.piece(zr, 2, s.HIB), self.RHI.at[zr, rows_of(s.HIB), :], self.left)

    def middle(self):
        s, m = DEAL_CUT, self.m
        lo, hi, za = self.lo, self.hi, self.za
        right, left, over = self.right, self.left, self.over
        RA, RLO, RHI, RL, RR, RZ = self.RA, self.RLO, self.RHI, self.RL, self.RR, self.RZ
        toR, toL = {}, {}
        for zr in (1, 0):
            lo[zr].wait_recv()
            self.add(zr, 1, s.LOB, RLO.at[zr])
            toR[zr] = m.go(self.piece(zr, 1, s.ALLB), RL.at[zr, rows_of(s.ALLB), :], right)
            hi[zr].wait_recv()
            self.add(zr, 3, s.HIB, RHI.at[zr])
            toL[zr] = m.go(self.piece(zr, 3, s.ALLB), RR.at[zr, rows_of(s.ALLB), :], left)
            if zr == 1:
                za[2].wait_recv()
                self.add(0, 2, s.ALLA, RA.at[2])
                loA = m.go(self.piece(0, 2, s.LOA), RLO.at[0, rows_of(s.LOA), :], right)
                hiA = m.go(self.piece(0, 2, s.HIA), RHI.at[0, rows_of(s.HIA), :], left)
        za[1].wait_recv()
        self.add(0, 1, s.ALLA, RA.at[1])
        za[3].wait_recv()
        self.add(0, 3, s.ALLA, RA.at[3])
        loA.wait_recv()
        self.add(0, 1, s.LOA, RLO.at[0])
        toRA = m.go(self.piece(0, 1, s.ALLA), RL.at[0, rows_of(s.ALLA), :], right)
        hiA.wait_recv()
        self.add(0, 3, s.HIA, RHI.at[0])
        toLA = m.go(self.piece(0, 3, s.ALLA), RR.at[0, rows_of(s.ALLA), :], left)
        toR[1].wait_recv()
        toL[1].wait_recv()
        self.add(1, 0, s.ALLB, RL.at[1], RR.at[1])
        zb = m.go(self.piece(1, 0, s.ALLB), RZ.at[rows_of(s.ALLB), :], over)
        self.last = (za[0], toRA, toLA), (toR[0], toL[0], zb)

    def total(self, span, which, extra):
        for copy in self.last[which]:
            copy.wait_recv()
        rows = rows_of(span)
        total = self.S[0, rows, :].astype(f32) + self.RL[0, rows, :].astype(f32)
        return total + self.RR[0, rows, :].astype(f32) + extra[rows, :].astype(f32)

    def total_a(self):
        return self.total(DEAL_CUT.ALLA, 0, self.RA.at[0])

    def total_b(self):
        return self.total(DEAL_CUT.ALLB, 1, self.RZ)


SCATTER_COPIES = 4 + 4 + 4 + 2 + 2 + 1
OTHERS = [(dx, dz) for dx in (2, 1, 3, 0) for dz in (1, 0) if (dx, dz) != (0, 0)]


def layer_kernel(lengths, gain1, gain2, tokens, token_lots_in, query, key, value, gate, out_weight, swish, up,
                 down_weight, out,
                 full1, squares, first, acc, qk, vg,  retained, memory, decay, stats, gated,
                 quarter1, whole1, pack1, mate1, quarter2, whole2, pack2, mate2, second,
                 stage, wpar, wmate, lots, token_lots, pick, unpick, base, wide, full2, normed2, result, spare,
                 S1, RA1, RLO1, RHI1, RL1, RR1, RZ1, S2, RA2, RLO2, RHI2, RL2, RR2, RZ2,
                 local1, local2, load_sem, send, recv):
    place = Place()
    mover = Mover(send, recv)
    req = place.req
    cut = DEAL_CUT
    hand1 = Handout(place, mover, (query, key, value, gate), first, quarter1, whole1, pack1, mate1, local1)
    hand2 = Handout(place, mover, (swish, up), second, quarter2, whole2, pack2, mate2, local2)
    mine = column(place.me)
    hand1.load()
    loads = [pltpu.make_async_copy(tokens, full1.at[:, mine], load_sem.at[0]),
             pltpu.make_async_copy(out_weight, stage.at[0], load_sem.at[1]),
             pltpu.make_async_copy(down_weight, stage.at[1], load_sem.at[2]),
             pltpu.make_async_copy(token_lots_in.at[:, 0], token_lots.at[req], load_sem.at[3])]
    for copy in loads:
        copy.start()
    hand2.load()
    mate_core = place.near(0, 0, 1)

    def group(dx, dz):
        return ((place.x + dx + 4) % 4) * 2 + (place.zh + dz) % 2

    hand1.prepare()
    greet(group_peers(place) + [(group(dx, dz), place.me) for dx, dz in OTHERS])
    hand1.share()
    loads[0].wait()
    gather = Gather(place, mover, full1, WIDE_CUT)
    gather.start_a()
    gather.start_b()
    dealt_tokens = []
    for dx, dz in OTHERS:
        target = group(dx, dz)
        turn = (target - req + 8) % 8
        dealt_tokens.append(mover.go(token_lots_in.at[:, turn], token_lots.at[req], (target, place.me)))
    hand1.share_whole()

    head = place.me // 2
    log_decay, span_decay = jnp.float32(0.0), jnp.float32(0.0)
    for h in range(H):
        rate = 1.0 - 2.0 ** (-5 - h)
        log_decay = jnp.where(head == h, jnp.float32(math.log(rate)), log_decay)
        span_decay = jnp.where(head == h, jnp.float32(rate ** SPAN), span_decay)
    i = lax.broadcasted_iota(jnp.int32, (SPAN, SPAN), 0)
    j = lax.broadcasted_iota(jnp.int32, (SPAN, SPAN), 1)
    decay[0] = jnp.where(i >= j, jnp.exp((i - j).astype(f32) * log_decay), 0.0)
    decay[1] = jnp.exp((i + 1).astype(f32) * log_decay)
    decay[2] = jnp.exp((SPAN - 1 - i).astype(f32) * log_decay)

    order = [(dy, zr) for zr in (0, 1) for dy in range(4)]

    def set_weight(which):
        loads[1 + which].wait()
        for i, (dy, zr) in enumerate(order):
            wpar[which, 0:256, i * 128:(i + 1) * 128] = stage[which, :, column(place.member(dy, zr, 0))].astype(bf16)
            wmate[which, :, i * 128:(i + 1) * 128] = stage[which, :, column(place.member(dy, zr, 1))].astype(bf16)
        return mover.go(wmate.at[which], wpar.at[which, pl.ds(256, 256), :], mate_core)

    starts, counts = [], []
    start = jnp.int32(0)
    for r in range(8):
        length = lengths[r]
        turn = (req - r + 8) % 8
        count = 16 * (length // 128) + jnp.clip(length % 128 - 16 * turn, 0, 16)
        starts.append(start)
        counts.append(count)
        start = start + count

    def select():
        row = lax.broadcasted_iota(jnp.int32, (DEAL, 128), 0)
        lane = lax.broadcasted_iota(jnp.int32, (DEAL, 128), 1)
        slot = lax.broadcasted_iota(jnp.int32, (128, DEAL), 0)
        at = lax.broadcasted_iota(jnp.int32, (128, DEAL), 1)
        for r in range(8):
            chosen = (lane == row - starts[r]) & (lane < counts[r])
            pick[:, r * 128:(r + 1) * 128] = jnp.where(chosen, 1.0, 0.0).astype(bf16)
            chosen = (at == slot + starts[r]) & (slot < counts[r])
            unpick[r] = jnp.where(chosen, 1.0, 0.0).astype(bf16)

    def gained(rows, chips):
        total, square = None, None
        for chip in chips:
            depth = pl.ds(pl.multiple_of(chip * 256, 256), 256)
            values = full1[rows, depth].astype(f32)
            part = jnp.dot((values * gain1[:, depth]).astype(bf16), first[depth, :], preferred_element_type=f32)
            values = values * values
            values = values[:, :128] + values[:, 128:]
            total = part if total is None else total + part
            square = values if square is None else square + values
        return total, square

    def gather_product(rels, fresh=False):
        chips = [place.member(-dy, zr, 0) // 2 for dy, zr in rels]
        for dy, zr in rels:
            gather.ready(-dy, zr)

        def step(i, carry):
            rows = pl.ds(pl.multiple_of(i * SPAN, SPAN), SPAN)
            part, square = gained(rows, chips)
            acc[rows, :] = part if fresh else acc[rows, :] + part
            squares[rows, :] = square if fresh else squares[rows, :] + square
            return carry

        lax.fori_loop(0, LMAX // SPAN, step, 0)

    got1 = hand1.spread(range(14))
    weights = [set_weight(0)]
    gather.first()
    halves1 = hand1.onward(got1[:6])
    await_all(hand1.whole_sent)
    gather_product([(0, 0)], True)
    weights.append(set_weight(1))
    gather.second()
    halves1 += hand1.onward(got1[6:10])
    gather.third()
    halves1 += hand1.onward(got1[10:])
    hand2.prepare()
    hand2.share()
    hand2.share_whole()
    await_all(halves1[:8])
    gather_product([(0, 1), (1, 0)])
    await_all(halves1[8:16])
    gather_product([(3, 0), (1, 1)])
    await_all(halves1[16:24])
    gather_product([(3, 1), (2, 0)])
    gather.finish()
    await_all(halves1[24:])
    last_chip = [place.member(-2, 1, 0) // 2]
    key_scale = jnp.where(place.c == 0, 1.0, DK ** (-0.5))
    swapped = []

    def project(b):
        rows = pl.ds(b * SPAN, SPAN)
        total, square = gained(rows, last_chip)
        square = jnp.sum(squares[rows, :] + square, axis=1, keepdims=True)
        total = (acc[rows, :] + total) * lax.rsqrt(square * (1.0 / 2048) + epsilon)
        qk[place.c, rows, :] = (total[:, :256] * key_scale).astype(bf16)
        ref = qk.at[place.c, rows, :]
        swapped.append(mover.go(ref, ref, mate_core))
        vg[0, rows, :] = total[:, 256:512].astype(bf16)
        vg[1, rows, :] = total[:, 512:].astype(bf16)

    def attend(b):
        rows = pl.ds(b * SPAN, SPAN)
        swapped[b].wait_recv()
        query_block, key_block, value_block = qk[0, rows, :], qk[1, rows, :], vg[0, rows, :]
        scores = lax.dot_general(query_block, key_block, (((1,), (1,)), ((), ())), preferred_element_type=f32)
        total = jnp.dot((scores * decay[0]).astype(bf16), value_block, preferred_element_type=f32)
        if b > 0:
            before = memory[...]
            upper = before.astype(bf16)
            lower = (before - upper.astype(f32)).astype(bf16)
            across = jnp.dot(query_block, upper, preferred_element_type=f32)
            across = across + jnp.dot(query_block, lower, preferred_element_type=f32)
            total = total + across * decay[1]
        if b < 3:
            decayed = key_block.astype(f32) * decay[2]
            upper = decayed.astype(bf16)
            lower = (decayed - upper.astype(f32)).astype(bf16)
            turned = (((0,), (0,)), ((), ()))
            update = lax.dot_general(upper, value_block, turned, preferred_element_type=f32)
            update = update + lax.dot_general(lower, value_block, turned, preferred_element_type=f32)
            memory[...] = update if b == 0 else memory[...] * span_decay + update
        retained[rows, :] = total
        mean = jnp.sum(total, axis=1, keepdims=True) * (1.0 / 256)
        spread = total - mean
        square = jnp.sum(spread * spread, axis=1, keepdims=True)
        lanes = lax.broadcasted_iota(jnp.int32, (SPAN, 128), 1)
        stats[0, b] = jnp.where(lanes < 64, mean, square)
        return mover.go(stats.at[0, b], stats.at[1, b], mate_core)

    def finish(b, told):
        rows = pl.ds(b * SPAN, SPAN)
        told.wait_recv()
        mean, square = stats[0, b, :, 0:1], stats[0, b, :, 64:65]
        mean2, square2 = stats[1, b, :, 0:1], stats[1, b, :, 64:65]
        gap = (mean - mean2) * 0.5
        middle = (mean + mean2) * 0.5
        var = (square + square2) * (1.0 / DV) + gap * gap
        grouped = (retained[rows, :] - middle) * lax.rsqrt(var + epsilon)
        gates = vg[1, rows, :].astype(f32)
        done = (gates / (1.0 + jnp.exp(-gates)) * grouped).astype(bf16)
        gated[2 * b:2 * b + 2] = done.reshape(2, 8, 16, 256)
        two = pl.ds(2 * b, 2)
        sent = []
        for dx, dz in OTHERS:
            target = group(dx, dz)
            turn = (target - req + 8) % 8
            sent.append(mover.go(gated.at[two, turn], lots.at[req, two], (target, place.me)))
        lots[req, 2 * b:2 * b + 2] = gated[2 * b:2 * b + 2, 0]
        return sent

    dealt, told = [], []
    project(0)
    got2 = hand2.spread(range(7))
    for b in range(4):
        if b < 3:
            project(b + 1)
        told.append(attend(b))
        if b > 0:
            dealt += finish(b - 1, told[b - 1])
    dealt += finish(3, told[3])
    loads[3].wait()
    select()
    await_all(dealt)
    got2b = hand2.spread(range(7, 14))
    sent = []
    for span in (cut.ALLA, cut.ALLB):
        rows = rows_of(span)
        part = jnp.dot(pick[rows, :], lots[...].reshape(LMAX, 256), preferred_element_type=f32)
        wide[0, rows, 0:256] = part.astype(bf16)
        ref = wide.at[0, rows, pl.ds(0, 256)]
        sent.append(mover.go(ref, wide.at[0, rows, pl.ds(256, 256)], mate_core))

    scatter = Scatter(place, mover, wide.at[0], wpar.at[0], (S1, RA1, RLO1, RHI1, RL1, RR1, RZ1))
    weights[0].wait_recv()
    sent[0].wait_recv()
    scatter.multiply(cut.ALLA)
    scatter.start_a()
    sent[1].wait_recv()
    scatter.multiply(cut.ALLB)
    scatter.start_b()
    halves2 = hand2.onward(got2)
    await_all(dealt_tokens)
    base[...] = jnp.dot(pick[...], token_lots[...].reshape(LMAX, BLK), preferred_element_type=f32).astype(bf16)
    scatter.middle()
    gather = Gather(place, mover, full2, cut)
    full2[rows_of(cut.ALLA), mine] = (base[rows_of(cut.ALLA), :].astype(f32) + scatter.total_a()).astype(bf16)
    gather.start_a()
    full2[rows_of(cut.ALLB), mine] = (base[rows_of(cut.ALLB), :].astype(f32) + scatter.total_b()).astype(bf16)
    gather.start_b()
    halves2 += hand2.onward(got2b)
    gather.first()
    gather.second()
    gather.third()
    gather.finish()
    await_all(halves2 + hand2.whole_sent)
    def normalize(i, carry):
        rows = pl.ds(pl.multiple_of(i * 32, 32), 32)
        values = full2[rows, :].astype(f32)
        scale = lax.rsqrt(jnp.mean(values * values, axis=-1, keepdims=True) + epsilon)
        normed2[rows, :] = (values * scale * gain2[...]).astype(bf16)
        return carry

    lax.fori_loop(0, DEAL // 32, normalize, 0)
    sent = []
    for span in (cut.ALLA, cut.ALLB):
        rows = rows_of(span)
        part = jnp.dot(normed2[rows, :], second[...], preferred_element_type=f32)
        swished = part[:, :256]
        wide[1, rows, 0:256] = (swished / (1.0 + jnp.exp(-swished)) * part[:, 256:]).astype(bf16)
        ref = wide.at[1, rows, pl.ds(0, 256)]
        sent.append(mover.go(ref, wide.at[1, rows, pl.ds(256, 256)], mate_core))
    scatter = Scatter(place, mover, wide.at[1], wpar.at[1], (S2, RA2, RLO2, RHI2, RL2, RR2, RZ2))
    weights[1].wait_recv()
    sent[0].wait_recv()
    scatter.multiply(cut.ALLA)
    scatter.start_a()
    sent[1].wait_recv()
    scatter.multiply(cut.ALLB)
    scatter.start_b()
    scatter.middle()
    for span, total in ((cut.ALLA, scatter.total_a), (cut.ALLB, scatter.total_b)):
        rows = rows_of(span)
        result[rows, :] = (full2[rows, mine].astype(f32) + total()).astype(bf16)
    for r in range(8):
        spare[r] = jnp.dot(unpick[r], result[...], preferred_element_type=f32).astype(bf16).reshape(8, 16, BLK)
    returned = []
    for dx, dz in OTHERS:
        target = group(dx, dz)
        returned.append(mover.go(spare.at[target], out.at[:, (req - target + 8) % 8], (target, place.me)))
    out[:, 0] = spare[req]
    await_all(returned)
    mover.drain()


LAYER_COPIES = 2 * HANDOUT_COPIES + 2 * GATHER_COPIES + 2 * SCATTER_COPIES + 7 * 6 + 2 + 4 + 4 + 4


def layer(*operands):
    vmem = pl.BlockSpec(memory_space=pltpu.VMEM)
    hbm = pl.BlockSpec(memory_space=pl.ANY)
    sums = [
        pltpu.VMEM((8, DEAL, BLK), bf16),
        pltpu.VMEM((4, DEAL, BLK), bf16),
        pltpu.VMEM((2, DEAL, BLK), bf16),
        pltpu.VMEM((2, DEAL, BLK), bf16),
        pltpu.VMEM((2, DEAL, BLK), bf16),
        pltpu.VMEM((2, DEAL, BLK), bf16),
        pltpu.VMEM((DEAL, BLK), bf16),
    ]
    return pl.pallas_call(
        layer_kernel,
        name="layer",
        out_shape=jax.ShapeDtypeStruct((8, 8, 16, BLK), bf16),
        in_specs=[pl.BlockSpec(memory_space=pltpu.SMEM), vmem, vmem] + [hbm] * 10,
        out_specs=vmem,
        scratch_shapes=[
            pltpu.VMEM((LMAX, 2048), bf16),
            pltpu.VMEM((LMAX, 128), f32),
            pltpu.VMEM((2048, 768), bf16),
            pltpu.VMEM((LMAX, 768), f32),
            pltpu.VMEM((2, LMAX, 256), bf16),
            pltpu.VMEM((2, LMAX, 256), bf16),

            pltpu.VMEM((LMAX, 256), f32),
            pltpu.VMEM((256, 256), f32),
            pltpu.VMEM((3, SPAN, SPAN), f32),
            pltpu.VMEM((2, 4, SPAN, 128), f32),
            pltpu.VMEM((8, 8, 16, 256), bf16),
            pltpu.VMEM((32, 12288), f32),
            pltpu.VMEM((1, 128, 1536), f32),
            pltpu.VMEM((16, 32, 768), bf16),
            pltpu.VMEM((1, 128, 768), bf16),
            pltpu.VMEM((32, 8192), f32),
            pltpu.VMEM((1, 128, 1024), f32),
            pltpu.VMEM((16, 32, 512), bf16),
            pltpu.VMEM((1, 128, 512), bf16),
            pltpu.VMEM((2048, 512), bf16),
            pltpu.VMEM((2, 256, 2048), f32),
            pltpu.VMEM((2, 512, 1024), bf16),
            pltpu.VMEM((2, 256, 1024), bf16),
            pltpu.VMEM((8, 8, 16, 256), bf16),
            pltpu.VMEM((8, 8, 16, BLK), bf16),
            pltpu.VMEM((DEAL, LMAX), bf16),
            pltpu.VMEM((8, 128, DEAL), bf16),
            pltpu.VMEM((DEAL, BLK), bf16),
            pltpu.VMEM((2, DEAL, 512), bf16),
            pltpu.VMEM((DEAL, 2048), bf16),
            pltpu.VMEM((DEAL, 2048), bf16),
            pltpu.VMEM((DEAL, BLK), bf16),
            pltpu.VMEM((8, 8, 16, BLK), bf16),
        ] + sums + sums + [
            pltpu.SemaphoreType.DMA((8,)),
            pltpu.SemaphoreType.DMA((4,)),
            pltpu.SemaphoreType.DMA((4,)),
            pltpu.SemaphoreType.DMA((LAYER_COPIES,)),
            pltpu.SemaphoreType.DMA((LAYER_COPIES,)),
        ],
        compiler_params=pltpu.CompilerParams(
            collective_id=0, has_side_effects=True, vmem_limit_bytes=63 * 2**20
        ),
    )(*operands)


def body(
    tokens,
    lengths,
    retention_gain,
    forward_gain,
    query_weight,
    key_weight,
    value_weight,
    gate_weight,
    output_weight,
    swish_weight,
    up_weight,
    down_weight,
):
    rows = tokens.reshape(8, 8, 16, BLK)
    finished = layer(
        lengths, retention_gain.reshape(1, 2048), forward_gain.reshape(1, 2048), tokens[0], rows,
        query_weight, key_weight, value_weight, gate_weight, output_weight, swish_weight, up_weight, down_weight
    )
    return finished.reshape(1, LMAX, BLK)


def solution(mesh):
    placed = (
        P("req", None, "mlp"),
        P(),
        P(),
        P(),
        P("mlp", None),
        P("mlp", None),
        P("mlp", None),
        P("mlp", None),
        P("mlp", None),
        P("mlp", None),
        P("mlp", None),
        P("mlp", None),
    )
    return jax.shard_map(
        body, mesh=mesh, in_specs=placed, out_specs=P("req", None, "mlp"), check_vma=False
    )
```

```python
import math
import jax
import jax.numpy as jnp
from jax import lax
from jax.experimental import pallas as pl
from jax.experimental.pallas import tpu as pltpu
from jax.sharding import PartitionSpec as P

H = 8
DK = 256
DV = 512
SPAN = 256
LMAX = 1024
BLK = 128
REST = [(0, 1), (1, 0), (3, 0), (1, 1), (3, 1), (2, 0), (2, 1)]
DIRECT = [(0, 0, 1)]

epsilon = 1e-05
bf16 = jnp.bfloat16
f32 = jnp.float32


class Cut:
    def __init__(self, rows, cut):
        half, rest = cut // 2, (rows + cut) // 2
        self.ALLA, self.LOA, self.HIA = (0, cut), (0, half), (half, cut)
        self.ALLB, self.LOB, self.HIB = (cut, rows), (cut, rest), (rest, rows)


WIDE_CUT = Cut(1024, 416)
DEAL = 448
DEAL_CUT = Cut(DEAL, 192)


def rows_of(span):
    return pl.ds(span[0], span[1] - span[0])


class Place:
    def __init__(self):
        self.req = lax.axis_index("req")
        self.me = lax.axis_index("mlp")
        self.x = self.req // 2
        self.zh = self.req % 2
        self.y = self.me // 4
        self.z = (self.me // 2) % 2
        self.c = self.me % 2

    def member(self, dy, zr, cc):
        return ((self.y + dy + 4) % 4) * 4 + ((self.z + zr) % 2) * 2 + (self.c + cc) % 2

    def near(self, dy, zr, cc):
        return (self.req, self.member(dy, zr, cc))

    def across(self, dx):
        return (((self.x + dx + 4) % 4) * 2 + self.zh, self.me)


class Mover:
    def __init__(self, send, recv):
        self.send, self.recv, self.count, self.sent = send, recv, 0, []

    def plan(self, src, dst, device):
        i = self.count
        self.count += 1
        return pltpu.make_async_remote_copy(
            src_ref=src, dst_ref=dst, send_sem=self.send.at[i], recv_sem=self.recv.at[i],
            device_id=device, device_id_type=pl.DeviceIdType.MESH,
        )

    def go(self, src, dst, device):
        copy = self.plan(src, dst, device)
        copy.start()
        self.sent.append(copy)
        return copy

    def drain(self):
        for copy in self.sent:
            copy.wait_send()
        self.sent = []


def greet(devices):
    barrier = pltpu.get_barrier_semaphore()
    for device in devices:
        pl.semaphore_signal(barrier, inc=1, device_id=device, device_id_type=pl.DeviceIdType.MESH)
    pl.semaphore_wait(barrier, len(devices))


def column(member):
    return pl.ds(pl.multiple_of(member * BLK, BLK), BLK)


class Gather:
    def __init__(self, place, mover, full, cut):
        self.p, self.m, self.full, self.s = place, mover, full, cut
        self.need = {}

    def at(self, span, dy, zr):
        return self.full.at[rows_of(span), column(self.p.member(dy, zr, 0))]

    def pass_on(self, span, dy, zr, targets):
        place = self.p
        ref = self.at(span, dy, zr)
        out = []
        for step in targets:
            device = {"r": place.near(1, 0, 0), "l": place.near(-1, 0, 0),
                      "z": place.near(0, 1, 0), "c": place.near(0, 0, 1)}[step]
            copy = self.m.go(ref, ref, device)
            if step == "c":
                self.need.setdefault((dy % 4, zr), []).append(copy)
            else:
                out.append(copy)
        return out

    def start_a(self):
        self.a = self.pass_on(self.s.ALLA, 0, 0, "rlzc")

    def start_b(self):
        self.b = self.pass_on(self.s.ALLB, 0, 0, "zrlc")

    def first(self):
        ar, al, az = self.a
        bz, br, bl = self.b
        bz.wait_recv()
        self.zb = self.pass_on(self.s.ALLB, 0, 1, "rlc")
        ar.wait_recv()
        self.al1 = self.pass_on(self.s.LOA, -1, 0, "r") + self.pass_on(self.s.ALLA, -1, 0, "zc")
        al.wait_recv()
        self.ar1 = self.pass_on(self.s.HIA, 1, 0, "l") + self.pass_on(self.s.ALLA, 1, 0, "zc")
        br.wait_recv()
        self.bl1 = self.pass_on(self.s.LOB, -1, 0, "r") + self.pass_on(self.s.ALLB, -1, 0, "c")
        bl.wait_recv()
        self.br1 = self.pass_on(self.s.HIB, 1, 0, "l") + self.pass_on(self.s.ALLB, 1, 0, "c")
        az.wait_recv()
        self.pass_on(self.s.ALLA, 0, 1, "c")

    def second(self):
        lo, az = self.al1
        hi, az2 = self.ar1
        lo.wait_recv()
        self.o1 = self.pass_on(self.s.LOA, -2, 0, "zc")
        hi.wait_recv()
        self.o2 = self.pass_on(self.s.HIA, 2, 0, "zc")
        zr, zl = self.zb
        zr.wait_recv()
        self.zlo = self.pass_on(self.s.LOB, -1, 1, "r") + self.pass_on(self.s.ALLB, -1, 1, "c")
        zl.wait_recv()
        self.zhi = self.pass_on(self.s.HIB, 1, 1, "l") + self.pass_on(self.s.ALLB, 1, 1, "c")
        az.wait_recv()
        self.pass_on(self.s.ALLA, -1, 1, "c")
        az2.wait_recv()
        self.pass_on(self.s.ALLA, 1, 1, "c")

    def third(self):
        self.bl1[0].wait_recv()
        self.pass_on(self.s.LOB, -2, 0, "c")
        self.br1[0].wait_recv()
        self.pass_on(self.s.HIB, 2, 0, "c")
        self.o1[0].wait_recv()
        self.pass_on(self.s.LOA, -2, 1, "c")
        self.o2[0].wait_recv()
        self.pass_on(self.s.HIA, 2, 1, "c")
        self.zlo[0].wait_recv()
        self.pass_on(self.s.LOB, -2, 1, "c")
        self.zhi[0].wait_recv()
        self.pass_on(self.s.HIB, 2, 1, "c")

    def ready(self, dy, zr):
        for copy in self.need.pop((dy % 4, zr), ()):
            copy.wait_recv()

    def finish(self):
        for key in list(self.need):
            self.ready(*key)


GATHER_COPIES = 38


class Handout:
    def __init__(self, place, mover, refs, out, quarter, whole, pack, mate, local):
        self.p, self.m, self.refs, self.out = place, mover, refs, out
        self.quarter, self.whole, self.pack, self.mate, self.local = quarter, whole, pack, mate, local
        self.rel = [(dy, zr, cc) for dy, zr in REST for cc in (0, 1)]
        self.cols = out.shape[1]

    def load(self):
        place = self.p
        part = pl.ds(pl.multiple_of(place.x * 32, 32), 32)
        self.loads, at = [], 0
        for ref in self.refs:
            self.one(ref.at[part, :], self.quarter.at[:, pl.ds(at, ref.shape[1])])
            at += ref.shape[1]
        for zr in (0,):
            chip = place.member(0, zr, 0) // 2
            at = 0
            for ref in self.refs:
                wide = ref.shape[1] // 8
                self.one(ref.at[:, pl.ds(pl.multiple_of(chip * wide, 128), wide)], self.whole.at[zr, :, pl.ds(at, wide)])
                at += wide

    def one(self, src, dst):
        copy = pltpu.make_async_copy(src, dst, self.local.at[len(self.loads)])
        copy.start()
        self.loads.append(copy)

    def lot(self, member, slot, low=0, high=32):
        return pl.ds(pl.multiple_of(member * 128 + slot * 32 + low, 16), high - low)

    def prepare(self):
        for copy in self.loads[:len(self.refs)]:
            copy.wait()
        for d in range(16):
            for i in range(self.cols // 256):
                self.pack[d, :, i * 256:(i + 1) * 256] = self.quarter[:, i * 4096 + self.spot(d, i):][:, :256].astype(bf16)

    def share(self):
        place = self.p
        self.first = [
            self.m.go(self.pack.at[place.member(*r)], self.out.at[self.lot(place.me, place.x), :], place.near(*r))
            for r in self.rel
        ]

    def spot(self, d, i):
        if i == 0 and len(self.refs) * 256 > self.cols:
            return (d % 2) * 2048 + (d // 2) * 256
        return d * 256

    def share_whole(self):
        place = self.p
        for copy in self.loads[len(self.refs):]:
            copy.wait()
        rows = pl.ds(pl.multiple_of(place.me * 128, 128), 128)
        self.whole_sent = []
        for i in range(self.cols // 256):
            mine = self.whole[0, :, pl.ds(pl.multiple_of(i * 512 + place.c * 256, 128), 256)]
            self.out[rows, i * 256:(i + 1) * 256] = mine.astype(bf16)
        for at, (dy, zr, cc) in enumerate(DIRECT):
            core = (place.c + cc) % 2
            for i in range(self.cols // 256):
                other = self.whole[zr, :, pl.ds(pl.multiple_of(i * 512 + core * 256, 128), 256)]
                self.mate[at, :, i * 256:(i + 1) * 256] = other.astype(bf16)
            self.whole_sent.append(self.m.go(self.mate.at[at], self.out.at[rows, :], place.near(dy, zr, cc)))

    def origin(self, r):
        return self.p.member(-r[0], r[1], r[2])

    def spread(self, which):
        place = self.p
        got = []
        for i in which:
            self.first[i].wait_recv()
            ref = self.out.at[self.lot(self.origin(self.rel[i]), place.x), :]
            got.append((i, self.m.go(ref, ref, place.across(1)), self.m.go(ref, ref, place.across(-1))))
        return got

    def onward(self, got):
        place = self.p
        halves = []
        for i, right, left in got:
            origin = self.origin(self.rel[i])
            right.wait_recv()
            ref = self.out.at[self.lot(origin, (place.x + 3) % 4, 0, 16), :]
            halves.append(self.m.go(ref, ref, place.across(1)))
            left.wait_recv()
            ref = self.out.at[self.lot(origin, (place.x + 1) % 4, 16, 32), :]
            halves.append(self.m.go(ref, ref, place.across(-1)))
        return halves


HANDOUT_COPIES = 14 * 5 + 1


def group_peers(place):
    return [place.near(dy, zr, cc) for dy, zr in REST for cc in (0, 1)] + [place.near(*r) for r in DIRECT]


def await_all(copies):
    for copy in copies:
        copy.wait_recv()


class Scatter:
    def __init__(self, place, mover, wide, wpar, bufs):
        self.p, self.m, self.wide, self.wpar = place, mover, wide, wpar
        self.S, self.RA, self.RLO, self.RHI, self.RL, self.RR, self.RZ = bufs
        self.right, self.left, self.over = place.near(1, 0, 0), place.near(-1, 0, 0), place.near(0, 1, 0)

    def multiply(self, span):
        rows = rows_of(span)
        for i in range(4):
            part = jnp.dot(self.wide[rows, :], self.wpar[:, i * 256:(i + 1) * 256], preferred_element_type=f32)
            part = part.astype(bf16)
            self.S[2 * i, rows, :] = part[:, :128]
            self.S[2 * i + 1, rows, :] = part[:, 128:]

    def piece(self, zr, dy, span):
        return self.S.at[zr * 4 + dy, rows_of(span), :]

    def add(self, zr, dy, span, *others):
        rows = rows_of(span)
        total = self.S[zr * 4 + dy, rows, :].astype(f32)
        for other in others:
            total = total + other[rows, :].astype(f32)
        self.S[zr * 4 + dy, rows, :] = total.astype(bf16)

    def start_a(self):
        s = DEAL_CUT
        self.za = {dy: self.m.go(self.piece(1, dy, s.ALLA), self.RA.at[dy, rows_of(s.ALLA), :], self.over)
                   for dy in (2, 1, 3, 0)}

    def start_b(self):
        s = DEAL_CUT
        self.lo, self.hi = {}, {}
        for zr in (1, 0):
            self.lo[zr] = self.m.go(self.piece(zr, 2, s.LOB), self.RLO.at[zr, rows_of(s.LOB), :], self.right)
            self.hi[zr] = self.m.go(self.piece(zr, 2, s.HIB), self.RHI.at[zr, rows_of(s.HIB), :], self.left)

    def middle(self):
        s, m = DEAL_CUT, self.m
        lo, hi, za = self.lo, self.hi, self.za
        right, left, over = self.right, self.left, self.over
        RA, RLO, RHI, RL, RR, RZ = self.RA, self.RLO, self.RHI, self.RL, self.RR, self.RZ
        toR, toL = {}, {}
        for zr in (1, 0):
            lo[zr].wait_recv()
            self.add(zr, 1, s.LOB, RLO.at[zr])
            toR[zr] = m.go(self.piece(zr, 1, s.ALLB), RL.at[zr, rows_of(s.ALLB), :], right)
            hi[zr].wait_recv()
            self.add(zr, 3, s.HIB, RHI.at[zr])
            toL[zr] = m.go(self.piece(zr, 3, s.ALLB), RR.at[zr, rows_of(s.ALLB), :], left)
            if zr == 1:
                za[2].wait_recv()
                self.add(0, 2, s.ALLA, RA.at[2])
                loA = m.go(self.piece(0, 2, s.LOA), RLO.at[0, rows_of(s.LOA), :], right)
                hiA = m.go(self.piece(0, 2, s.HIA), RHI.at[0, rows_of(s.HIA), :], left)
        za[1].wait_recv()
        self.add(0, 1, s.ALLA, RA.at[1])
        za[3].wait_recv()
        self.add(0, 3, s.ALLA, RA.at[3])
        loA.wait_recv()
        self.add(0, 1, s.LOA, RLO.at[0])
        toRA = m.go(self.piece(0, 1, s.ALLA), RL.at[0, rows_of(s.ALLA), :], right)
        hiA.wait_recv()
        self.add(0, 3, s.HIA, RHI.at[0])
        toLA = m.go(self.piece(0, 3, s.ALLA), RR.at[0, rows_of(s.ALLA), :], left)
        toR[1].wait_recv()
        toL[1].wait_recv()
        self.add(1, 0, s.ALLB, RL.at[1], RR.at[1])
        zb = m.go(self.piece(1, 0, s.ALLB), RZ.at[rows_of(s.ALLB), :], over)
        self.last = (za[0], toRA, toLA), (toR[0], toL[0], zb)

    def total(self, span, which, extra):
        for copy in self.last[which]:
            copy.wait_recv()
        rows = rows_of(span)
        total = self.S[0, rows, :].astype(f32) + self.RL[0, rows, :].astype(f32)
        return total + self.RR[0, rows, :].astype(f32) + extra[rows, :].astype(f32)

    def total_a(self):
        return self.total(DEAL_CUT.ALLA, 0, self.RA.at[0])

    def total_b(self):
        return self.total(DEAL_CUT.ALLB, 1, self.RZ)


SCATTER_COPIES = 4 + 4 + 4 + 2 + 2 + 1
OTHERS = [(dx, dz) for dx in (2, 1, 3, 0) for dz in (1, 0) if (dx, dz) != (0, 0)]


def layer_kernel(lengths, gain1, gain2, tokens, token_lots_in, query, key, value, gate, out_weight, swish, up,
                 down_weight, out,
                 full1, squares, first, acc, qk, vg,  retained, memory, decay, stats, gated,
                 quarter1, whole1, pack1, mate1, quarter2, whole2, pack2, mate2, second,
                 stage, wpar, wmate, lots, token_lots, pick, unpick, base, wide, full2, normed2, result, spare,
                 S1, RA1, RLO1, RHI1, RL1, RR1, RZ1, S2, RA2, RLO2, RHI2, RL2, RR2, RZ2,
                 local1, local2, load_sem, send, recv):
    place = Place()
    mover = Mover(send, recv)
    req = place.req
    cut = DEAL_CUT
    hand1 = Handout(place, mover, (query, key, value, gate), first, quarter1, whole1, pack1, mate1, local1)
    hand2 = Handout(place, mover, (swish, up), second, quarter2, whole2, pack2, mate2, local2)
    mine = column(place.me)
    hand1.load()
    loads = [pltpu.make_async_copy(tokens, full1.at[:, mine], load_sem.at[0]),
             pltpu.make_async_copy(out_weight, stage.at[0], load_sem.at[1]),
             pltpu.make_async_copy(down_weight, stage.at[1], load_sem.at[2]),
             pltpu.make_async_copy(token_lots_in.at[:, 0], token_lots.at[req], load_sem.at[3])]
    for copy in loads:
        copy.start()
    hand2.load()
    mate_core = place.near(0, 0, 1)

    def group(dx, dz):
        return ((place.x + dx + 4) % 4) * 2 + (place.zh + dz) % 2

    hand1.prepare()
    greet(group_peers(place) + [(group(dx, dz), place.me) for dx, dz in OTHERS])
    hand1.share()
    loads[0].wait()
    gather = Gather(place, mover, full1, WIDE_CUT)
    hand1.share_whole()

    head = place.me // 2
    log_decay, span_decay = jnp.float32(0.0), jnp.float32(0.0)
    for h in range(H):
        rate = 1.0 - 2.0 ** (-5 - h)
        log_decay = jnp.where(head == h, jnp.float32(math.log(rate)), log_decay)
        span_decay = jnp.where(head == h, jnp.float32(rate ** SPAN), span_decay)
    i = lax.broadcasted_iota(jnp.int32, (SPAN, SPAN), 0)
    j = lax.broadcasted_iota(jnp.int32, (SPAN, SPAN), 1)
    decay[0] = jnp.where(i >= j, jnp.exp((i - j).astype(f32) * log_decay), 0.0)
    decay[1] = jnp.exp((i + 1).astype(f32) * log_decay)
    decay[2] = jnp.exp((SPAN - 1 - i).astype(f32) * log_decay)

    order = [(dy, zr) for zr in (0, 1) for dy in range(4)]

    def set_weight(which):
        loads[1 + which].wait()
        for i, (dy, zr) in enumerate(order):
            wpar[which, 0:256, i * 128:(i + 1) * 128] = stage[which, :, column(place.member(dy, zr, 0))].astype(bf16)
            wmate[which, :, i * 128:(i + 1) * 128] = stage[which, :, column(place.member(dy, zr, 1))].astype(bf16)
        return mover.go(wmate.at[which], wpar.at[which, pl.ds(256, 256), :], mate_core)

    starts, counts = [], []
    start = jnp.int32(0)
    for r in range(8):
        length = lengths[r]
        turn = (req - r + 8) % 8
        count = 16 * (length // 128) + jnp.clip(length % 128 - 16 * turn, 0, 16)
        starts.append(start)
        counts.append(count)
        start = start + count

    def select():
        row = lax.broadcasted_iota(jnp.int32, (DEAL, 128), 0)
        lane = lax.broadcasted_iota(jnp.int32, (DEAL, 128), 1)
        slot = lax.broadcasted_iota(jnp.int32, (128, DEAL), 0)
        at = lax.broadcasted_iota(jnp.int32, (128, DEAL), 1)
        for r in range(8):
            chosen = (lane == row - starts[r]) & (lane < counts[r])
            pick[:, r * 128:(r + 1) * 128] = jnp.where(chosen, 1.0, 0.0).astype(bf16)
            chosen = (at == slot + starts[r]) & (slot < counts[r])
            unpick[r] = jnp.where(chosen, 1.0, 0.0).astype(bf16)

    def gained(rows, chips):
        total, square = None, None
        for chip in chips:
            depth = pl.ds(pl.multiple_of(chip * 256, 256), 256)
            values = full1[rows, depth].astype(f32)
            part = jnp.dot((values * gain1[:, depth]).astype(bf16), first[depth, :], preferred_element_type=f32)
            values = values * values
            values = values[:, :128] + values[:, 128:]
            total = part if total is None else total + part
            square = values if square is None else square + values
        return total, square

    def gather_product(rels, fresh=False):
        chips = [place.member(-dy, zr, 0) // 2 for dy, zr in rels]
        for dy, zr in rels:
            gather.ready(-dy, zr)

        def step(i, carry):
            rows = pl.ds(pl.multiple_of(i * SPAN, SPAN), SPAN)
            part, square = gained(rows, chips)
            acc[rows, :] = part if fresh else acc[rows, :] + part
            squares[rows, :] = square if fresh else squares[rows, :] + square
            return carry

        lax.fori_loop(0, LMAX // SPAN, step, 0)

    got1 = hand1.spread(range(6))
    gather.start_a()
    gather.start_b()
    got1 += hand1.spread(range(6, 14))
    weights = [set_weight(0)]
    gather.first()
    halves1 = hand1.onward(got1[:6])
    await_all(hand1.whole_sent)
    gather_product([(0, 0)], True)
    weights.append(set_weight(1))
    gather.second()
    halves1 += hand1.onward(got1[6:10])
    gather.third()
    halves1 += hand1.onward(got1[10:])
    hand2.prepare()
    hand2.share()
    hand2.share_whole()
    await_all(halves1[:8])
    gather_product([(0, 1), (1, 0)])
    await_all(halves1[8:16])
    gather_product([(3, 0), (1, 1)])
    await_all(halves1[16:24])
    gather_product([(3, 1), (2, 0)])
    gather.finish()
    await_all(halves1[24:])
    dealt_tokens = []
    for dx, dz in OTHERS:
        target = group(dx, dz)
        turn = (target - req + 8) % 8
        dealt_tokens.append(mover.go(token_lots_in.at[:, turn], token_lots.at[req], (target, place.me)))
    last_chip = [place.member(-2, 1, 0) // 2]
    key_scale = jnp.where(place.c == 0, 1.0, DK ** (-0.5))
    swapped = []

    def project(b):
        rows = pl.ds(b * SPAN, SPAN)
        total, square = gained(rows, last_chip)
        square = jnp.sum(squares[rows, :] + square, axis=1, keepdims=True)
        total = (acc[rows, :] + total) * lax.rsqrt(square * (1.0 / 2048) + epsilon)
        qk[place.c, rows, :] = (total[:, :256] * key_scale).astype(bf16)
        ref = qk.at[place.c, rows, :]
        swapped.append(mover.go(ref, ref, mate_core))
        vg[0, rows, :] = total[:, 256:512].astype(bf16)
        vg[1, rows, :] = total[:, 512:].astype(bf16)

    def attend(b):
        rows = pl.ds(b * SPAN, SPAN)
        swapped[b].wait_recv()
        query_block, key_block, value_block = qk[0, rows, :], qk[1, rows, :], vg[0, rows, :]
        scores = lax.dot_general(query_block, key_block, (((1,), (1,)), ((), ())), preferred_element_type=f32)
        total = jnp.dot((scores * decay[0]).astype(bf16), value_block, preferred_element_type=f32)
        if b > 0:
            before = memory[...]
            upper = before.astype(bf16)
            lower = (before - upper.astype(f32)).astype(bf16)
            across = jnp.dot(query_block, upper, preferred_element_type=f32)
            across = across + jnp.dot(query_block, lower, preferred_element_type=f32)
            total = total + across * decay[1]
        if b < 3:
            decayed = key_block.astype(f32) * decay[2]
            upper = decayed.astype(bf16)
            lower = (decayed - upper.astype(f32)).astype(bf16)
            turned = (((0,), (0,)), ((), ()))
            update = lax.dot_general(upper, value_block, turned, preferred_element_type=f32)
            update = update + lax.dot_general(lower, value_block, turned, preferred_element_type=f32)
            memory[...] = update if b == 0 else memory[...] * span_decay + update
        retained[rows, :] = total
        mean = jnp.sum(total, axis=1, keepdims=True) * (1.0 / 256)
        spread = total - mean
        square = jnp.sum(spread * spread, axis=1, keepdims=True)
        lanes = lax.broadcasted_iota(jnp.int32, (SPAN, 128), 1)
        stats[0, b] = jnp.where(lanes < 64, mean, square)
        return mover.go(stats.at[0, b], stats.at[1, b], mate_core)

    def finish(b, told):
        rows = pl.ds(b * SPAN, SPAN)
        told.wait_recv()
        mean, square = stats[0, b, :, 0:1], stats[0, b, :, 64:65]
        mean2, square2 = stats[1, b, :, 0:1], stats[1, b, :, 64:65]
        gap = (mean - mean2) * 0.5
        middle = (mean + mean2) * 0.5
        var = (square + square2) * (1.0 / DV) + gap * gap
        grouped = (retained[rows, :] - middle) * lax.rsqrt(var + epsilon)
        gates = vg[1, rows, :].astype(f32)
        done = (gates / (1.0 + jnp.exp(-gates)) * grouped).astype(bf16)
        gated[2 * b:2 * b + 2] = done.reshape(2, 8, 16, 256)
        two = pl.ds(2 * b, 2)
        sent = []
        for dx, dz in OTHERS:
            target = group(dx, dz)
            turn = (target - req + 8) % 8
            sent.append(mover.go(gated.at[two, turn], lots.at[req, two], (target, place.me)))
        lots[req, 2 * b:2 * b + 2] = gated[2 * b:2 * b + 2, 0]
        return sent

    dealt, told = [], []
    project(0)
    for b in range(4):
        if b < 3:
            project(b + 1)
        told.append(attend(b))
        if b > 0:
            dealt += finish(b - 1, told[b - 1])
    dealt += finish(3, told[3])
    loads[3].wait()
    select()
    await_all(dealt)
    got2 = hand2.spread(range(14))
    sent = []
    for span in (cut.ALLA, cut.ALLB):
        rows = rows_of(span)
        part = jnp.dot(pick[rows, :], lots[...].reshape(LMAX, 256), preferred_element_type=f32)
        wide[0, rows, 0:256] = part.astype(bf16)
        ref = wide.at[0, rows, pl.ds(0, 256)]
        sent.append(mover.go(ref, wide.at[0, rows, pl.ds(256, 256)], mate_core))

    scatter = Scatter(place, mover, wide.at[0], wpar.at[0], (S1, RA1, RLO1, RHI1, RL1, RR1, RZ1))
    weights[0].wait_recv()
    sent[0].wait_recv()
    scatter.multiply(cut.ALLA)
    scatter.start_a()
    sent[1].wait_recv()
    scatter.multiply(cut.ALLB)
    scatter.start_b()
    await_all(dealt_tokens)
    base[...] = jnp.dot(pick[...], token_lots[...].reshape(LMAX, BLK), preferred_element_type=f32).astype(bf16)
    scatter.middle()
    gather = Gather(place, mover, full2, cut)
    full2[rows_of(cut.ALLA), mine] = (base[rows_of(cut.ALLA), :].astype(f32) + scatter.total_a()).astype(bf16)
    gather.start_a()
    full2[rows_of(cut.ALLB), mine] = (base[rows_of(cut.ALLB), :].astype(f32) + scatter.total_b()).astype(bf16)
    gather.start_b()
    halves2 = hand2.onward(got2[:8])
    gather.first()
    gather.second()
    halves2 += hand2.onward(got2[8:])
    gather.third()
    gather.finish()
    await_all(halves2 + hand2.whole_sent)
    def normalize(i, carry):
        rows = pl.ds(pl.multiple_of(i * 32, 32), 32)
        values = full2[rows, :].astype(f32)
        scale = lax.rsqrt(jnp.mean(values * values, axis=-1, keepdims=True) + epsilon)
        normed2[rows, :] = (values * scale * gain2[...]).astype(bf16)
        return carry

    lax.fori_loop(0, DEAL // 32, normalize, 0)
    sent = []
    for span in (cut.ALLA, cut.ALLB):
        rows = rows_of(span)
        part = jnp.dot(normed2[rows, :], second[...], preferred_element_type=f32)
        swished = part[:, :256]
        wide[1, rows, 0:256] = (swished / (1.0 + jnp.exp(-swished)) * part[:, 256:]).astype(bf16)
        ref = wide.at[1, rows, pl.ds(0, 256)]
        sent.append(mover.go(ref, wide.at[1, rows, pl.ds(256, 256)], mate_core))
    scatter = Scatter(place, mover, wide.at[1], wpar.at[1], (S2, RA2, RLO2, RHI2, RL2, RR2, RZ2))
    weights[1].wait_recv()
    sent[0].wait_recv()
    scatter.multiply(cut.ALLA)
    scatter.start_a()
    sent[1].wait_recv()
    scatter.multiply(cut.ALLB)
    scatter.start_b()
    scatter.middle()
    for span, total in ((cut.ALLA, scatter.total_a), (cut.ALLB, scatter.total_b)):
        rows = rows_of(span)
        result[rows, :] = (full2[rows, mine].astype(f32) + total()).astype(bf16)
    for r in range(8):
        spare[r] = jnp.dot(unpick[r], result[...], preferred_element_type=f32).astype(bf16).reshape(8, 16, BLK)
    returned = []
    for dx, dz in OTHERS:
        target = group(dx, dz)
        returned.append(mover.go(spare.at[target], out.at[:, (req - target + 8) % 8], (target, place.me)))
    out[:, 0] = spare[req]
    await_all(returned)
    mover.drain()


LAYER_COPIES = 2 * HANDOUT_COPIES + 2 * GATHER_COPIES + 2 * SCATTER_COPIES + 7 * 6 + 2 + 4 + 4 + 4


def layer(*operands):
    vmem = pl.BlockSpec(memory_space=pltpu.VMEM)
    hbm = pl.BlockSpec(memory_space=pl.ANY)
    sums = [
        pltpu.VMEM((8, DEAL, BLK), bf16),
        pltpu.VMEM((4, DEAL, BLK), bf16),
        pltpu.VMEM((2, DEAL, BLK), bf16),
        pltpu.VMEM((2, DEAL, BLK), bf16),
        pltpu.VMEM((2, DEAL, BLK), bf16),
        pltpu.VMEM((2, DEAL, BLK), bf16),
        pltpu.VMEM((DEAL, BLK), bf16),
    ]
    return pl.pallas_call(
        layer_kernel,
        name="layer",
        out_shape=jax.ShapeDtypeStruct((8, 8, 16, BLK), bf16),
        in_specs=[pl.BlockSpec(memory_space=pltpu.SMEM), vmem, vmem] + [hbm] * 10,
        out_specs=vmem,
        scratch_shapes=[
            pltpu.VMEM((LMAX, 2048), bf16),
            pltpu.VMEM((LMAX, 128), f32),
            pltpu.VMEM((2048, 768), bf16),
            pltpu.VMEM((LMAX, 768), f32),
            pltpu.VMEM((2, LMAX, 256), bf16),
            pltpu.VMEM((2, LMAX, 256), bf16),

            pltpu.VMEM((LMAX, 256), f32),
            pltpu.VMEM((256, 256), f32),
            pltpu.VMEM((3, SPAN, SPAN), f32),
            pltpu.VMEM((2, 4, SPAN, 128), f32),
            pltpu.VMEM((8, 8, 16, 256), bf16),
            pltpu.VMEM((32, 12288), f32),
            pltpu.VMEM((1, 128, 1536), f32),
            pltpu.VMEM((16, 32, 768), bf16),
            pltpu.VMEM((1, 128, 768), bf16),
            pltpu.VMEM((32, 8192), f32),
            pltpu.VMEM((1, 128, 1024), f32),
            pltpu.VMEM((16, 32, 512), bf16),
            pltpu.VMEM((1, 128, 512), bf16),
            pltpu.VMEM((2048, 512), bf16),
            pltpu.VMEM((2, 256, 2048), f32),
            pltpu.VMEM((2, 512, 1024), bf16),
            pltpu.VMEM((2, 256, 1024), bf16),
            pltpu.VMEM((8, 8, 16, 256), bf16),
            pltpu.VMEM((8, 8, 16, BLK), bf16),
            pltpu.VMEM((DEAL, LMAX), bf16),
            pltpu.VMEM((8, 128, DEAL), bf16),
            pltpu.VMEM((DEAL, BLK), bf16),
            pltpu.VMEM((2, DEAL, 512), bf16),
            pltpu.VMEM((DEAL, 2048), bf16),
            pltpu.VMEM((DEAL, 2048), bf16),
            pltpu.VMEM((DEAL, BLK), bf16),
            pltpu.VMEM((8, 8, 16, BLK), bf16),
        ] + sums + sums + [
            pltpu.SemaphoreType.DMA((8,)),
            pltpu.SemaphoreType.DMA((4,)),
            pltpu.SemaphoreType.DMA((4,)),
            pltpu.SemaphoreType.DMA((LAYER_COPIES,)),
            pltpu.SemaphoreType.DMA((LAYER_COPIES,)),
        ],
        compiler_params=pltpu.CompilerParams(
            collective_id=0, has_side_effects=True, vmem_limit_bytes=63 * 2**20
        ),
    )(*operands)


def body(
    tokens,
    lengths,
    retention_gain,
    forward_gain,
    query_weight,
    key_weight,
    value_weight,
    gate_weight,
    output_weight,
    swish_weight,
    up_weight,
    down_weight,
):
    rows = tokens.reshape(8, 8, 16, BLK)
    finished = layer(
        lengths, retention_gain.reshape(1, 2048), forward_gain.reshape(1, 2048), tokens[0], rows,
        query_weight, key_weight, value_weight, gate_weight, output_weight, swish_weight, up_weight, down_weight
    )
    return finished.reshape(1, LMAX, BLK)


def solution(mesh):
    placed = (
        P("req", None, "mlp"),
        P(),
        P(),
        P(),
        P("mlp", None),
        P("mlp", None),
        P("mlp", None),
        P("mlp", None),
        P("mlp", None),
        P("mlp", None),
        P("mlp", None),
        P("mlp", None),
    )
    return jax.shard_map(
        body, mesh=mesh, in_specs=placed, out_specs=P("req", None, "mlp"), check_vma=False
    )
```

```python
import math
import jax
import jax.numpy as jnp
from jax import lax
from jax.experimental import pallas as pl
from jax.experimental.pallas import tpu as pltpu
from jax.sharding import PartitionSpec as P

H = 8
DK = 256
DV = 512
SPAN = 256
LMAX = 1024
BLK = 128
REST = [(1, 0), (3, 0), (1, 1), (3, 1), (2, 0), (2, 1)]
DIRECT = [(0, 0, 1), (0, 1, 0), (0, 1, 1)]

epsilon = 1e-05
bf16 = jnp.bfloat16
f32 = jnp.float32


class Cut:
    def __init__(self, rows, cut):
        half, rest = cut // 2, (rows + cut) // 2
        self.ALLA, self.LOA, self.HIA = (0, cut), (0, half), (half, cut)
        self.ALLB, self.LOB, self.HIB = (cut, rows), (cut, rest), (rest, rows)


WIDE_CUT = Cut(1024, 480)
DEAL = 448
DEAL_CUT = Cut(DEAL, 192)


def rows_of(span):
    return pl.ds(span[0], span[1] - span[0])


class Place:
    def __init__(self):
        self.req = lax.axis_index("req")
        self.me = lax.axis_index("mlp")
        self.x = self.req // 2
        self.zh = self.req % 2
        self.y = self.me // 4
        self.z = (self.me // 2) % 2
        self.c = self.me % 2

    def member(self, dy, zr, cc):
        return ((self.y + dy + 4) % 4) * 4 + ((self.z + zr) % 2) * 2 + (self.c + cc) % 2

    def near(self, dy, zr, cc):
        return (self.req, self.member(dy, zr, cc))

    def beside(self, zr, cc):
        return (self.x * 2 + (self.zh + zr) % 2, self.member(0, zr, cc))

    def across(self, dx):
        return (((self.x + dx + 4) % 4) * 2 + self.zh, self.me)


class Mover:
    def __init__(self, send, recv):
        self.send, self.recv, self.count, self.sent = send, recv, 0, []

    def plan(self, src, dst, device):
        i = self.count
        self.count += 1
        return pltpu.make_async_remote_copy(
            src_ref=src, dst_ref=dst, send_sem=self.send.at[i], recv_sem=self.recv.at[i],
            device_id=device, device_id_type=pl.DeviceIdType.MESH,
        )

    def go(self, src, dst, device):
        copy = self.plan(src, dst, device)
        copy.start()
        self.sent.append(copy)
        return copy

    def drain(self):
        for copy in self.sent:
            copy.wait_send()
        self.sent = []


def greet(devices):
    barrier = pltpu.get_barrier_semaphore()
    for device in devices:
        pl.semaphore_signal(barrier, inc=1, device_id=device, device_id_type=pl.DeviceIdType.MESH)


def await_greetings(devices):
    pl.semaphore_wait(pltpu.get_barrier_semaphore(), len(devices))


def column(member):
    return pl.ds(pl.multiple_of(member * BLK, BLK), BLK)


class Gather:
    def __init__(self, place, mover, full, cut):
        self.p, self.m, self.full, self.s = place, mover, full, cut
        self.need = {}

    def at(self, span, dy, zr):
        return self.full.at[rows_of(span), column(self.p.member(dy, zr, 0))]

    def pass_on(self, span, dy, zr, targets):
        place = self.p
        ref = self.at(span, dy, zr)
        out = []
        for step in targets:
            device = {"r": place.near(1, 0, 0), "l": place.near(-1, 0, 0),
                      "z": place.near(0, 1, 0), "c": place.near(0, 0, 1)}[step]
            copy = self.m.go(ref, ref, device)
            if step == "c":
                self.need.setdefault((dy % 4, zr), []).append(copy)
            else:
                out.append(copy)
        return out

    def start_a(self):
        self.a = self.pass_on(self.s.ALLA, 0, 0, "rlzc")

    def start_b(self):
        self.b = self.pass_on(self.s.ALLB, 0, 0, "zrlc")

    def first(self):
        ar, al, az = self.a
        bz, br, bl = self.b
        bz.wait_recv()
        self.zb = self.pass_on(self.s.ALLB, 0, 1, "rlc")
        ar.wait_recv()
        self.al1 = self.pass_on(self.s.LOA, -1, 0, "r") + self.pass_on(self.s.ALLA, -1, 0, "zc")
        al.wait_recv()
        self.ar1 = self.pass_on(self.s.HIA, 1, 0, "l") + self.pass_on(self.s.ALLA, 1, 0, "zc")
        br.wait_recv()
        self.bl1 = self.pass_on(self.s.LOB, -1, 0, "r") + self.pass_on(self.s.ALLB, -1, 0, "c")
        bl.wait_recv()
        self.br1 = self.pass_on(self.s.HIB, 1, 0, "l") + self.pass_on(self.s.ALLB, 1, 0, "c")
        az.wait_recv()
        self.pass_on(self.s.ALLA, 0, 1, "c")

    def second(self):
        lo, az = self.al1
        hi, az2 = self.ar1
        lo.wait_recv()
        self.o1 = self.pass_on(self.s.LOA, -2, 0, "zc")
        hi.wait_recv()
        self.o2 = self.pass_on(self.s.HIA, 2, 0, "zc")
        zr, zl = self.zb
        zr.wait_recv()
        self.zlo = self.pass_on(self.s.LOB, -1, 1, "r") + self.pass_on(self.s.ALLB, -1, 1, "c")
        zl.wait_recv()
        self.zhi = self.pass_on(self.s.HIB, 1, 1, "l") + self.pass_on(self.s.ALLB, 1, 1, "c")
        az.wait_recv()
        self.pass_on(self.s.ALLA, -1, 1, "c")
        az2.wait_recv()
        self.pass_on(self.s.ALLA, 1, 1, "c")

    def third(self):
        self.bl1[0].wait_recv()
        self.pass_on(self.s.LOB, -2, 0, "c")
        self.br1[0].wait_recv()
        self.pass_on(self.s.HIB, 2, 0, "c")
        self.o1[0].wait_recv()
        self.pass_on(self.s.LOA, -2, 1, "c")
        self.o2[0].wait_recv()
        self.pass_on(self.s.HIA, 2, 1, "c")
        self.zlo[0].wait_recv()
        self.pass_on(self.s.LOB, -2, 1, "c")
        self.zhi[0].wait_recv()
        self.pass_on(self.s.HIB, 2, 1, "c")

    def ready(self, dy, zr):
        for copy in self.need.pop((dy % 4, zr), ()):
            copy.wait_recv()

    def finish(self):
        for key in list(self.need):
            self.ready(*key)


GATHER_COPIES = 38


class Handout:
    def __init__(self, place, mover, refs, out, quarter, whole, pack, mate, local):
        self.p, self.m, self.refs, self.out = place, mover, refs, out
        self.quarter, self.whole, self.pack, self.mate, self.local = quarter, whole, pack, mate, local
        self.rel = [(dy, zr, cc) for dy, zr in REST for cc in (0, 1)]
        self.cols = out.shape[1]

    def load(self):
        place = self.p
        part = pl.ds(pl.multiple_of(place.x * 32, 32), 32)
        self.loads, at = [], 0
        for ref in self.refs:
            self.one(ref.at[part, :], self.quarter.at[:, pl.ds(at, ref.shape[1])])
            at += ref.shape[1]
        for zr in (0, 1):
            chip = place.member(0, zr, 0) // 2
            at = 0
            for ref in self.refs:
                wide = ref.shape[1] // 8
                self.one(ref.at[:, pl.ds(pl.multiple_of(chip * wide, 128), wide)], self.whole.at[zr, :, pl.ds(at, wide)])
                at += wide

    def one(self, src, dst):
        copy = pltpu.make_async_copy(src, dst, self.local.at[len(self.loads)])
        copy.start()
        self.loads.append(copy)

    def lot(self, member, slot, low=0, high=32):
        return pl.ds(pl.multiple_of(member * 128 + slot * 32 + low, 16), high - low)

    def prepare(self):
        for copy in self.loads[:len(self.refs)]:
            copy.wait()
        for d in range(16):
            for i in range(self.cols // 256):
                self.pack[d, :, i * 256:(i + 1) * 256] = self.quarter[:, i * 4096 + self.spot(d, i):][:, :256].astype(bf16)

    def share(self):
        place = self.p
        self.first = [
            self.m.go(self.pack.at[place.member(*r)], self.out.at[self.lot(place.me, place.x), :], place.near(*r))
            for r in self.rel
        ]

    def spot(self, d, i):
        if i == 0 and len(self.refs) * 256 > self.cols:
            return (d % 2) * 2048 + (d // 2) * 256
        return d * 256

    def share_whole(self):
        place = self.p
        for copy in self.loads[len(self.refs):]:
            copy.wait()
        rows = pl.ds(pl.multiple_of(place.me * 128, 128), 128)
        self.whole_sent = []
        for i in range(self.cols // 256):
            mine = self.whole[0, :, pl.ds(pl.multiple_of(i * 512 + place.c * 256, 128), 256)]
            self.out[rows, i * 256:(i + 1) * 256] = mine.astype(bf16)
        for at, (dy, zr, cc) in enumerate(DIRECT):
            core = (place.c + cc) % 2
            for i in range(self.cols // 256):
                other = self.whole[zr, :, pl.ds(pl.multiple_of(i * 512 + core * 256, 128), 256)]
                self.mate[at, :, i * 256:(i + 1) * 256] = other.astype(bf16)
            self.whole_sent.append(self.m.go(self.mate.at[at], self.out.at[rows, :], place.beside(zr, cc)))

    def origin(self, r):
        return self.p.member(-r[0], r[1], r[2])

    def spread(self, which):
        place = self.p
        got = []
        for i in which:
            self.first[i].wait_recv()
            ref = self.out.at[self.lot(self.origin(self.rel[i]), place.x), :]
            got.append((i, self.m.go(ref, ref, place.across(1)), self.m.go(ref, ref, place.across(-1))))
        return got

    def onward(self, got):
        place = self.p
        halves = []
        for i, right, left in got:
            origin = self.origin(self.rel[i])
            right.wait_recv()
            ref = self.out.at[self.lot(origin, (place.x + 3) % 4, 0, 16), :]
            halves.append(self.m.go(ref, ref, place.across(1)))
            left.wait_recv()
            ref = self.out.at[self.lot(origin, (place.x + 1) % 4, 16, 32), :]
            halves.append(self.m.go(ref, ref, place.across(-1)))
        return halves


HANDOUT_COPIES = 12 * 5 + 3


def group_peers(place):
    return [place.near(dy, zr, cc) for dy, zr in REST for cc in (0, 1)] + [place.near(*r) for r in DIRECT] + [
        place.beside(1, 0), place.beside(1, 1)]


def await_all(copies):
    for copy in copies:
        copy.wait_recv()


class Scatter:
    def __init__(self, place, mover, wide, wpar, bufs):
        self.p, self.m, self.wide, self.wpar = place, mover, wide, wpar
        self.S, self.RA, self.RLO, self.RHI, self.RL, self.RR, self.RZ = bufs
        self.right, self.left, self.over = place.near(1, 0, 0), place.near(-1, 0, 0), place.near(0, 1, 0)

    def multiply(self, span):
        rows = rows_of(span)
        for i in range(4):
            part = jnp.dot(self.wide[rows, :], self.wpar[:, i * 256:(i + 1) * 256], preferred_element_type=f32)
            part = part.astype(bf16)
            self.S[2 * i, rows, :] = part[:, :128]
            self.S[2 * i + 1, rows, :] = part[:, 128:]

    def piece(self, zr, dy, span):
        return self.S.at[zr * 4 + dy, rows_of(span), :]

    def add(self, zr, dy, span, *others):
        rows = rows_of(span)
        total = self.S[zr * 4 + dy, rows, :].astype(f32)
        for other in others:
            total = total + other[rows, :].astype(f32)
        self.S[zr * 4 + dy, rows, :] = total.astype(bf16)

    def start_a(self):
        s = DEAL_CUT
        self.za = {dy: self.m.go(self.piece(1, dy, s.ALLA), self.RA.at[dy, rows_of(s.ALLA), :], self.over)
                   for dy in (2, 1, 3, 0)}

    def start_b(self):
        s = DEAL_CUT
        self.lo, self.hi = {}, {}
        for zr in (1, 0):
            self.lo[zr] = self.m.go(self.piece(zr, 2, s.LOB), self.RLO.at[zr, rows_of(s.LOB), :], self.right)
            self.hi[zr] = self.m.go(self.piece(zr, 2, s.HIB), self.RHI.at[zr, rows_of(s.HIB), :], self.left)

    def middle(self):
        s, m = DEAL_CUT, self.m
        lo, hi, za = self.lo, self.hi, self.za
        right, left, over = self.right, self.left, self.over
        RA, RLO, RHI, RL, RR, RZ = self.RA, self.RLO, self.RHI, self.RL, self.RR, self.RZ
        toR, toL = {}, {}
        for zr in (1, 0):
            lo[zr].wait_recv()
            self.add(zr, 1, s.LOB, RLO.at[zr])
            toR[zr] = m.go(self.piece(zr, 1, s.ALLB), RL.at[zr, rows_of(s.ALLB), :], right)
            hi[zr].wait_recv()
            self.add(zr, 3, s.HIB, RHI.at[zr])
            toL[zr] = m.go(self.piece(zr, 3, s.ALLB), RR.at[zr, rows_of(s.ALLB), :], left)
            if zr == 1:
                za[2].wait_recv()
                self.add(0, 2, s.ALLA, RA.at[2])
                loA = m.go(self.piece(0, 2, s.LOA), RLO.at[0, rows_of(s.LOA), :], right)
                hiA = m.go(self.piece(0, 2, s.HIA), RHI.at[0, rows_of(s.HIA), :], left)
        za[1].wait_recv()
        self.add(0, 1, s.ALLA, RA.at[1])
        za[3].wait_recv()
        self.add(0, 3, s.ALLA, RA.at[3])
        loA.wait_recv()
        self.add(0, 1, s.LOA, RLO.at[0])
        toRA = m.go(self.piece(0, 1, s.ALLA), RL.at[0, rows_of(s.ALLA), :], right)
        hiA.wait_recv()
        self.add(0, 3, s.HIA, RHI.at[0])
        toLA = m.go(self.piece(0, 3, s.ALLA), RR.at[0, rows_of(s.ALLA), :], left)
        toR[1].wait_recv()
        toL[1].wait_recv()
        self.add(1, 0, s.ALLB, RL.at[1], RR.at[1])
        zb = m.go(self.piece(1, 0, s.ALLB), RZ.at[rows_of(s.ALLB), :], over)
        self.last = (za[0], toRA, toLA), (toR[0], toL[0], zb)

    def total(self, span, which, extra):
        for copy in self.last[which]:
            copy.wait_recv()
        rows = rows_of(span)
        total = self.S[0, rows, :].astype(f32) + self.RL[0, rows, :].astype(f32)
        return total + self.RR[0, rows, :].astype(f32) + extra[rows, :].astype(f32)

    def total_a(self):
        return self.total(DEAL_CUT.ALLA, 0, self.RA.at[0])

    def total_b(self):
        return self.total(DEAL_CUT.ALLB, 1, self.RZ)


SCATTER_COPIES = 4 + 4 + 4 + 2 + 2 + 1
OTHERS = [(dx, dz) for dx in (2, 1, 3, 0) for dz in (1, 0) if (dx, dz) != (0, 0)]


def layer_kernel(lengths, gain1, gain2, tokens, token_lots_in, query, key, value, gate, out_weight, swish, up,
                 down_weight, out,
                 full1, squares, first, acc, qk, vg, retained, memory, decay, stats, gated,
                 quarter1, whole1, pack1, mate1, quarter2, whole2, pack2, mate2, second,
                 stage, wpar, wmate, lots, token_lots, pick, unpick, base, wide, full2, normed2, result, spare,
                 S1, RA1, RLO1, RHI1, RL1, RR1, RZ1, S2, RA2, RLO2, RHI2, RL2, RR2, RZ2,
                 local1, local2, load_sem, send, recv):
    place = Place()
    mover = Mover(send, recv)
    req = place.req
    cut = DEAL_CUT
    hand1 = Handout(place, mover, (query, key, value, gate), first, quarter1, whole1, pack1, mate1, local1)
    hand2 = Handout(place, mover, (swish, up), second, quarter2, whole2, pack2, mate2, local2)
    mine = column(place.me)

    def group(dx, dz):
        return ((place.x + dx + 4) % 4) * 2 + (place.zh + dz) % 2

    peers = group_peers(place) + [(group(dx, dz), place.me) for dx, dz in OTHERS]
    greet(peers)
    hand1.load()
    loads = [pltpu.make_async_copy(tokens, full1.at[:, mine], load_sem.at[0]),
             pltpu.make_async_copy(out_weight, stage.at[0], load_sem.at[1]),
             pltpu.make_async_copy(down_weight, stage.at[1], load_sem.at[2]),
             pltpu.make_async_copy(token_lots_in.at[:, 0], token_lots.at[req], load_sem.at[3])]
    for copy in loads:
        copy.start()
    hand2.load()
    mate_core = place.near(0, 0, 1)
    hand1.prepare()
    await_greetings(peers)
    hand1.share()
    loads[0].wait()
    gather = Gather(place, mover, full1, WIDE_CUT)
    hand1.share_whole()

    head = place.me // 2
    log_decay, span_decay = jnp.float32(0.0), jnp.float32(0.0)
    for h in range(H):
        rate = 1.0 - 2.0 ** (-5 - h)
        log_decay = jnp.where(head == h, jnp.float32(math.log(rate)), log_decay)
        span_decay = jnp.where(head == h, jnp.float32(rate ** SPAN), span_decay)
    i = lax.broadcasted_iota(jnp.int32, (SPAN, SPAN), 0)
    j = lax.broadcasted_iota(jnp.int32, (SPAN, SPAN), 1)
    decay[0] = jnp.where(i >= j, jnp.exp((i - j).astype(f32) * log_decay), 0.0)
    decay[1] = jnp.exp((i + 1).astype(f32) * log_decay)
    decay[2] = jnp.exp((SPAN - 1 - i).astype(f32) * log_decay)

    order = [(dy, zr) for zr in (0, 1) for dy in range(4)]

    def set_weight(which):
        loads[1 + which].wait()
        for i, (dy, zr) in enumerate(order):
            wpar[which, 0:256, i * 128:(i + 1) * 128] = stage[which, :, column(place.member(dy, zr, 0))].astype(bf16)
            wmate[which, :, i * 128:(i + 1) * 128] = stage[which, :, column(place.member(dy, zr, 1))].astype(bf16)
        return mover.go(wmate.at[which], wpar.at[which, pl.ds(256, 256), :], mate_core)

    starts, counts = [], []
    start = jnp.int32(0)
    for r in range(8):
        length = lengths[r]
        turn = (req - r + 8) % 8
        count = 16 * (length // 128) + jnp.clip(length % 128 - 16 * turn, 0, 16)
        starts.append(start)
        counts.append(count)
        start = start + count

    def select():
        row = lax.broadcasted_iota(jnp.int32, (DEAL, 128), 0)
        lane = lax.broadcasted_iota(jnp.int32, (DEAL, 128), 1)
        slot = lax.broadcasted_iota(jnp.int32, (128, DEAL), 0)
        at = lax.broadcasted_iota(jnp.int32, (128, DEAL), 1)
        for r in range(8):
            chosen = (lane == row - starts[r]) & (lane < counts[r])
            pick[:, r * 128:(r + 1) * 128] = jnp.where(chosen, 1.0, 0.0).astype(bf16)
            chosen = (at == slot + starts[r]) & (slot < counts[r])
            unpick[r] = jnp.where(chosen, 1.0, 0.0).astype(bf16)

    def gained(rows, chips):
        total, square = None, None
        for chip in chips:
            depth = pl.ds(pl.multiple_of(chip * 256, 256), 256)
            values = full1[rows, depth].astype(f32)
            part = jnp.dot((values * gain1[:, depth]).astype(bf16), first[depth, :], preferred_element_type=f32)
            values = values * values
            values = values[:, :128] + values[:, 128:]
            total = part if total is None else total + part
            square = values if square is None else square + values
        return total, square

    def gather_product(rels, fresh=False):
        chips = [place.member(-dy, zr, 0) // 2 for dy, zr in rels]
        for dy, zr in rels:
            gather.ready(-dy, zr)

        def step(i, carry):
            rows = pl.ds(pl.multiple_of(i * SPAN, SPAN), SPAN)
            part, square = gained(rows, chips)
            acc[rows, :] = part if fresh else acc[rows, :] + part
            squares[rows, :] = square if fresh else squares[rows, :] + square
            return carry

        lax.fori_loop(0, LMAX // SPAN, step, 0)

    got1 = hand1.spread(range(4))
    gather.start_a()
    gather.start_b()
    got1 += hand1.spread(range(4, 12))
    weights = [set_weight(0)]
    gather.first()
    halves1 = hand1.onward(got1[:4])
    await_all(hand1.whole_sent[:1])
    gather_product([(0, 0)], True)
    weights.append(set_weight(1))
    gather.second()
    halves1 += hand1.onward(got1[4:8])
    gather.third()
    halves1 += hand1.onward(got1[8:])
    hand2.prepare()
    hand2.share()
    hand2.share_whole()
    await_all(hand1.whole_sent[1:])
    gather_product([(0, 1)])
    await_all(halves1[:8])
    gather_product([(1, 0), (3, 0)])
    await_all(halves1[8:16])
    gather_product([(1, 1), (3, 1)])
    await_all(halves1[16:20])
    gather_product([(2, 0)])
    gather.finish()
    await_all(halves1[20:])
    dealt_tokens = []
    for dx, dz in OTHERS:
        target = group(dx, dz)
        turn = (target - req + 8) % 8
        dealt_tokens.append(mover.go(token_lots_in.at[:, turn], token_lots.at[req], (target, place.me)))
    last_chip = [place.member(-2, 1, 0) // 2]
    key_scale = jnp.where(place.c == 0, 1.0, DK ** (-0.5))
    swapped = []

    def project(b):
        rows = pl.ds(b * SPAN, SPAN)
        total, square = gained(rows, last_chip)
        square = jnp.sum(squares[rows, :] + square, axis=1, keepdims=True)
        total = (acc[rows, :] + total) * lax.rsqrt(square * (1.0 / 2048) + epsilon)
        qk[place.c, rows, :] = (total[:, :256] * key_scale).astype(bf16)
        ref = qk.at[place.c, rows, :]
        swapped.append(mover.go(ref, ref, mate_core))
        vg[0, rows, :] = total[:, 256:512].astype(bf16)
        vg[1, rows, :] = total[:, 512:].astype(bf16)

    def attend(b):
        rows = pl.ds(b * SPAN, SPAN)
        swapped[b].wait_recv()
        query_block, key_block, value_block = qk[0, rows, :], qk[1, rows, :], vg[0, rows, :]
        scores = lax.dot_general(query_block, key_block, (((1,), (1,)), ((), ())), preferred_element_type=f32)
        total = jnp.dot((scores * decay[0]).astype(bf16), value_block, preferred_element_type=f32)
        if b > 0:
            across = jnp.dot(query_block, memory[...].astype(bf16), preferred_element_type=f32)
            total = total + across * decay[1]
        if b < 3:
            decayed = (key_block.astype(f32) * decay[2]).astype(bf16)
            update = lax.dot_general(decayed, value_block, (((0,), (0,)), ((), ())), preferred_element_type=f32)
            memory[...] = update if b == 0 else memory[...] * span_decay + update
        retained[rows, :] = total
        mean = jnp.sum(total, axis=1, keepdims=True) * (1.0 / 256)
        spread = total - mean
        square = jnp.sum(spread * spread, axis=1, keepdims=True)
        lanes = lax.broadcasted_iota(jnp.int32, (SPAN, 128), 1)
        stats[0, b] = jnp.where(lanes < 64, mean, square)
        return mover.go(stats.at[0, b], stats.at[1, b], mate_core)

    def finish(b, told):
        rows = pl.ds(b * SPAN, SPAN)
        told.wait_recv()
        mean, square = stats[0, b, :, 0:1], stats[0, b, :, 64:65]
        mean2, square2 = stats[1, b, :, 0:1], stats[1, b, :, 64:65]
        gap = (mean - mean2) * 0.5
        middle = (mean + mean2) * 0.5
        var = (square + square2) * (1.0 / DV) + gap * gap
        grouped = (retained[rows, :] - middle) * lax.rsqrt(var + epsilon)
        gates = vg[1, rows, :].astype(f32)
        done = (gates / (1.0 + jnp.exp(-gates)) * grouped).astype(bf16)
        gated[2 * b:2 * b + 2] = done.reshape(2, 8, 16, 256)
        two = pl.ds(2 * b, 2)
        sent = []
        for dx, dz in OTHERS:
            target = group(dx, dz)
            turn = (target - req + 8) % 8
            sent.append(mover.go(gated.at[two, turn], lots.at[req, two], (target, place.me)))
        lots[req, 2 * b:2 * b + 2] = gated[2 * b:2 * b + 2, 0]
        return sent

    dealt, told = [], []
    project(0)
    for b in range(4):
        if b < 3:
            project(b + 1)
        told.append(attend(b))
        if b > 0:
            dealt += finish(b - 1, told[b - 1])
    dealt += finish(3, told[3])
    loads[3].wait()
    select()
    await_all(dealt)
    got2 = hand2.spread(range(12))
    sent = []
    for span in (cut.ALLA, cut.ALLB):
        rows = rows_of(span)
        part = jnp.dot(pick[rows, :], lots[...].reshape(LMAX, 256), preferred_element_type=f32)
        wide[0, rows, 0:256] = part.astype(bf16)
        ref = wide.at[0, rows, pl.ds(0, 256)]
        sent.append(mover.go(ref, wide.at[0, rows, pl.ds(256, 256)], mate_core))

    scatter = Scatter(place, mover, wide.at[0], wpar.at[0], (S1, RA1, RLO1, RHI1, RL1, RR1, RZ1))
    weights[0].wait_recv()
    sent[0].wait_recv()
    scatter.multiply(cut.ALLA)
    scatter.start_a()
    sent[1].wait_recv()
    scatter.multiply(cut.ALLB)
    scatter.start_b()
    await_all(dealt_tokens)
    base[...] = jnp.dot(pick[...], token_lots[...].reshape(LMAX, BLK), preferred_element_type=f32).astype(bf16)
    scatter.middle()
    gather = Gather(place, mover, full2, cut)
    full2[rows_of(cut.ALLA), mine] = (base[rows_of(cut.ALLA), :].astype(f32) + scatter.total_a()).astype(bf16)
    gather.start_a()
    full2[rows_of(cut.ALLB), mine] = (base[rows_of(cut.ALLB), :].astype(f32) + scatter.total_b()).astype(bf16)
    gather.start_b()
    halves2 = hand2.onward(got2[:6])
    gather.first()
    gather.second()
    halves2 += hand2.onward(got2[6:])
    gather.third()
    gather.finish()
    await_all(halves2 + hand2.whole_sent)
    def normalize(i, carry):
        rows = pl.ds(pl.multiple_of(i * 32, 32), 32)
        values = full2[rows, :].astype(f32)
        scale = lax.rsqrt(jnp.mean(values * values, axis=-1, keepdims=True) + epsilon)
        normed2[rows, :] = (values * scale * gain2[...]).astype(bf16)
        return carry

    lax.fori_loop(0, DEAL // 32, normalize, 0)
    sent = []
    for span in (cut.ALLA, cut.ALLB):
        rows = rows_of(span)
        part = jnp.dot(normed2[rows, :], second[...], preferred_element_type=f32)
        swished = part[:, :256]
        wide[1, rows, 0:256] = (swished / (1.0 + jnp.exp(-swished)) * part[:, 256:]).astype(bf16)
        ref = wide.at[1, rows, pl.ds(0, 256)]
        sent.append(mover.go(ref, wide.at[1, rows, pl.ds(256, 256)], mate_core))
    scatter = Scatter(place, mover, wide.at[1], wpar.at[1], (S2, RA2, RLO2, RHI2, RL2, RR2, RZ2))
    weights[1].wait_recv()
    sent[0].wait_recv()
    scatter.multiply(cut.ALLA)
    scatter.start_a()
    sent[1].wait_recv()
    scatter.multiply(cut.ALLB)
    scatter.start_b()
    scatter.middle()
    for span, total in ((cut.ALLA, scatter.total_a), (cut.ALLB, scatter.total_b)):
        rows = rows_of(span)
        result[rows, :] = (full2[rows, mine].astype(f32) + total()).astype(bf16)
    for r in range(8):
        spare[r] = jnp.dot(unpick[r], result[...], preferred_element_type=f32).astype(bf16).reshape(8, 16, BLK)
    returned = []
    for dx, dz in OTHERS:
        target = group(dx, dz)
        returned.append(mover.go(spare.at[target], out.at[:, (req - target + 8) % 8], (target, place.me)))
    out[:, 0] = spare[req]
    await_all(returned)
    mover.drain()


LAYER_COPIES = 2 * HANDOUT_COPIES + 2 * GATHER_COPIES + 2 * SCATTER_COPIES + 7 * 6 + 2 + 4 + 4 + 4


def layer(*operands):
    vmem = pl.BlockSpec(memory_space=pltpu.VMEM)
    hbm = pl.BlockSpec(memory_space=pl.ANY)
    sums = [
        pltpu.VMEM((8, DEAL, BLK), bf16),
        pltpu.VMEM((4, DEAL, BLK), bf16),
        pltpu.VMEM((2, DEAL, BLK), bf16),
        pltpu.VMEM((2, DEAL, BLK), bf16),
        pltpu.VMEM((2, DEAL, BLK), bf16),
        pltpu.VMEM((2, DEAL, BLK), bf16),
        pltpu.VMEM((DEAL, BLK), bf16),
    ]
    return pl.pallas_call(
        layer_kernel,
        name="layer",
        out_shape=jax.ShapeDtypeStruct((8, 8, 16, BLK), bf16),
        in_specs=[pl.BlockSpec(memory_space=pltpu.SMEM), vmem, vmem] + [hbm] * 10,
        out_specs=vmem,
        scratch_shapes=[
            pltpu.VMEM((LMAX, 2048), bf16),
            pltpu.VMEM((LMAX, 128), f32),
            pltpu.VMEM((2048, 768), bf16),
            pltpu.VMEM((LMAX, 768), f32),
            pltpu.VMEM((2, LMAX, 256), bf16),
            pltpu.VMEM((2, LMAX, 256), bf16),

            pltpu.VMEM((LMAX, 256), f32),
            pltpu.VMEM((256, 256), f32),
            pltpu.VMEM((3, SPAN, SPAN), f32),
            pltpu.VMEM((2, 4, SPAN, 128), f32),
            pltpu.VMEM((8, 8, 16, 256), bf16),
            pltpu.VMEM((32, 12288), f32),
            pltpu.VMEM((2, 128, 1536), f32),
            pltpu.VMEM((16, 32, 768), bf16),
            pltpu.VMEM((3, 128, 768), bf16),
            pltpu.VMEM((32, 8192), f32),
            pltpu.VMEM((2, 128, 1024), f32),
            pltpu.VMEM((16, 32, 512), bf16),
            pltpu.VMEM((3, 128, 512), bf16),
            pltpu.VMEM((2048, 512), bf16),
            pltpu.VMEM((2, 256, 2048), f32),
            pltpu.VMEM((2, 512, 1024), bf16),
            pltpu.VMEM((2, 256, 1024), bf16),
            pltpu.VMEM((8, 8, 16, 256), bf16),
            pltpu.VMEM((8, 8, 16, BLK), bf16),
            pltpu.VMEM((DEAL, LMAX), bf16),
            pltpu.VMEM((8, 128, DEAL), bf16),
            pltpu.VMEM((DEAL, BLK), bf16),
            pltpu.VMEM((2, DEAL, 512), bf16),
            pltpu.VMEM((DEAL, 2048), bf16),
            pltpu.VMEM((DEAL, 2048), bf16),
            pltpu.VMEM((DEAL, BLK), bf16),
            pltpu.VMEM((8, 8, 16, BLK), bf16),
        ] + sums + sums + [
            pltpu.SemaphoreType.DMA((12,)),
            pltpu.SemaphoreType.DMA((6,)),
            pltpu.SemaphoreType.DMA((4,)),
            pltpu.SemaphoreType.DMA((LAYER_COPIES,)),
            pltpu.SemaphoreType.DMA((LAYER_COPIES,)),
        ],
        compiler_params=pltpu.CompilerParams(
            collective_id=0, has_side_effects=True, vmem_limit_bytes=63 * 2**20
        ),
    )(*operands)


def body(
    tokens,
    lengths,
    retention_gain,
    forward_gain,
    query_weight,
    key_weight,
    value_weight,
    gate_weight,
    output_weight,
    swish_weight,
    up_weight,
    down_weight,
):
    rows = tokens.reshape(8, 8, 16, BLK)
    finished = layer(
        lengths, retention_gain.reshape(1, 2048), forward_gain.reshape(1, 2048), tokens[0], rows,
        query_weight, key_weight, value_weight, gate_weight, output_weight, swish_weight, up_weight, down_weight
    )
    return finished.reshape(1, LMAX, BLK)


def solution(mesh):
    placed = (
        P("req", None, "mlp"),
        P(),
        P(),
        P(),
        P("mlp", None),
        P("mlp", None),
        P("mlp", None),
        P("mlp", None),
        P("mlp", None),
        P("mlp", None),
        P("mlp", None),
        P("mlp", None),
    )
    return jax.shard_map(
        body, mesh=mesh, in_specs=placed, out_specs=P("req", None, "mlp"), check_vma=False
    )
```

```python
import math
import jax
import jax.numpy as jnp
from jax import lax
from jax.experimental import pallas as pl
from jax.experimental.pallas import tpu as pltpu
from jax.sharding import PartitionSpec as P

H = 8
DK = 256
DV = 512
SPAN = 256
LMAX = 1024
BLK = 128
REST = [(1, 0), (3, 0), (1, 1), (3, 1), (2, 0), (2, 1)]
DIRECT = [(0, 0, 1), (0, 1, 0), (0, 1, 1)]

epsilon = 1e-05
bf16 = jnp.bfloat16
f32 = jnp.float32


class Cut:
    def __init__(self, rows, cut, base=0):
        first, mid, rest, end = base + cut // 2, base + cut, base + (rows + cut) // 2, base + rows
        self.all = (base, end)
        self.ALLA, self.LOA, self.HIA = (base, mid), (base, first), (first, mid)
        self.ALLB, self.LOB, self.HIB = (mid, end), (mid, rest), (rest, end)


WIDE_CUT = Cut(1024, 480)
DEAL = 448
DEAL_CUTS = (Cut(224, 96), Cut(224, 96, 224))


def rows_of(span):
    return pl.ds(span[0], span[1] - span[0])


class Place:
    def __init__(self):
        self.req = lax.axis_index("req")
        self.me = lax.axis_index("mlp")
        self.x = self.req // 2
        self.zh = self.req % 2
        self.y = self.me // 4
        self.z = (self.me // 2) % 2
        self.c = self.me % 2

    def member(self, dy, zr, cc):
        return ((self.y + dy + 4) % 4) * 4 + ((self.z + zr) % 2) * 2 + (self.c + cc) % 2

    def near(self, dy, zr, cc):
        return (self.req, self.member(dy, zr, cc))

    def beside(self, zr, cc):
        return (self.x * 2 + (self.zh + zr) % 2, self.member(0, zr, cc))

    def across(self, dx):
        return (((self.x + dx + 4) % 4) * 2 + self.zh, self.me)


class Mover:
    def __init__(self, send, recv):
        self.send, self.recv, self.count, self.sent = send, recv, 0, []

    def plan(self, src, dst, device):
        i = self.count
        self.count += 1
        return pltpu.make_async_remote_copy(
            src_ref=src, dst_ref=dst, send_sem=self.send.at[i], recv_sem=self.recv.at[i],
            device_id=device, device_id_type=pl.DeviceIdType.MESH,
        )

    def go(self, src, dst, device):
        copy = self.plan(src, dst, device)
        copy.start()
        self.sent.append(copy)
        return copy

    def drain(self):
        for copy in self.sent:
            copy.wait_send()
        self.sent = []


def greet(devices):
    barrier = pltpu.get_barrier_semaphore()
    for device in devices:
        pl.semaphore_signal(barrier, inc=1, device_id=device, device_id_type=pl.DeviceIdType.MESH)


def await_greetings(devices):
    pl.semaphore_wait(pltpu.get_barrier_semaphore(), len(devices))


def column(member):
    return pl.ds(pl.multiple_of(member * BLK, BLK), BLK)


class Gather:
    def __init__(self, place, mover, full, cut):
        self.p, self.m, self.full, self.s = place, mover, full, cut
        self.need = {}

    def at(self, span, dy, zr):
        return self.full.at[rows_of(span), column(self.p.member(dy, zr, 0))]

    def pass_on(self, span, dy, zr, targets):
        place = self.p
        ref = self.at(span, dy, zr)
        out = []
        for step in targets:
            device = {"r": place.near(1, 0, 0), "l": place.near(-1, 0, 0),
                      "z": place.near(0, 1, 0), "c": place.near(0, 0, 1)}[step]
            copy = self.m.go(ref, ref, device)
            if step == "c":
                self.need.setdefault((dy % 4, zr), []).append(copy)
            else:
                out.append(copy)
        return out

    def start_a(self):
        self.a = self.pass_on(self.s.ALLA, 0, 0, "rlzc")

    def start_b(self):
        self.b = self.pass_on(self.s.ALLB, 0, 0, "zrlc")

    def first(self):
        ar, al, az = self.a
        bz, br, bl = self.b
        bz.wait_recv()
        self.zb = self.pass_on(self.s.ALLB, 0, 1, "rlc")
        ar.wait_recv()
        self.al1 = self.pass_on(self.s.LOA, -1, 0, "r") + self.pass_on(self.s.ALLA, -1, 0, "zc")
        al.wait_recv()
        self.ar1 = self.pass_on(self.s.HIA, 1, 0, "l") + self.pass_on(self.s.ALLA, 1, 0, "zc")
        br.wait_recv()
        self.bl1 = self.pass_on(self.s.LOB, -1, 0, "r") + self.pass_on(self.s.ALLB, -1, 0, "c")
        bl.wait_recv()
        self.br1 = self.pass_on(self.s.HIB, 1, 0, "l") + self.pass_on(self.s.ALLB, 1, 0, "c")
        az.wait_recv()
        self.pass_on(self.s.ALLA, 0, 1, "c")

    def second(self):
        lo, az = self.al1
        hi, az2 = self.ar1
        lo.wait_recv()
        self.o1 = self.pass_on(self.s.LOA, -2, 0, "zc")
        hi.wait_recv()
        self.o2 = self.pass_on(self.s.HIA, 2, 0, "zc")
        zr, zl = self.zb
        zr.wait_recv()
        self.zlo = self.pass_on(self.s.LOB, -1, 1, "r") + self.pass_on(self.s.ALLB, -1, 1, "c")
        zl.wait_recv()
        self.zhi = self.pass_on(self.s.HIB, 1, 1, "l") + self.pass_on(self.s.ALLB, 1, 1, "c")
        az.wait_recv()
        self.pass_on(self.s.ALLA, -1, 1, "c")
        az2.wait_recv()
        self.pass_on(self.s.ALLA, 1, 1, "c")

    def third(self):
        self.bl1[0].wait_recv()
        self.pass_on(self.s.LOB, -2, 0, "c")
        self.br1[0].wait_recv()
        self.pass_on(self.s.HIB, 2, 0, "c")
        self.o1[0].wait_recv()
        self.pass_on(self.s.LOA, -2, 1, "c")
        self.o2[0].wait_recv()
        self.pass_on(self.s.HIA, 2, 1, "c")
        self.zlo[0].wait_recv()
        self.pass_on(self.s.LOB, -2, 1, "c")
        self.zhi[0].wait_recv()
        self.pass_on(self.s.HIB, 2, 1, "c")

    def ready(self, dy, zr):
        for copy in self.need.pop((dy % 4, zr), ()):
            copy.wait_recv()

    def finish(self):
        for key in list(self.need):
            self.ready(*key)


GATHER_COPIES = 38


class Handout:
    def __init__(self, place, mover, refs, out, quarter, whole, pack, mate, local):
        self.p, self.m, self.refs, self.out = place, mover, refs, out
        self.quarter, self.whole, self.pack, self.mate, self.local = quarter, whole, pack, mate, local
        self.rel = [(dy, zr, cc) for dy, zr in REST for cc in (0, 1)]
        self.cols = out.shape[1]

    def load(self):
        place = self.p
        part = pl.ds(pl.multiple_of(place.x * 32, 32), 32)
        self.loads, at = [], 0
        for ref in self.refs:
            self.one(ref.at[part, :], self.quarter.at[:, pl.ds(at, ref.shape[1])])
            at += ref.shape[1]
        for zr in (0, 1):
            chip = place.member(0, zr, 0) // 2
            at = 0
            for ref in self.refs:
                wide = ref.shape[1] // 8
                self.one(ref.at[:, pl.ds(pl.multiple_of(chip * wide, 128), wide)], self.whole.at[zr, :, pl.ds(at, wide)])
                at += wide

    def one(self, src, dst):
        copy = pltpu.make_async_copy(src, dst, self.local.at[len(self.loads)])
        copy.start()
        self.loads.append(copy)

    def lot(self, member, slot, low=0, high=32):
        return pl.ds(pl.multiple_of(member * 128 + slot * 32 + low, 16), high - low)

    def prepare(self):
        for copy in self.loads[:len(self.refs)]:
            copy.wait()
        for d in range(16):
            for i in range(self.cols // 256):
                self.pack[d, :, i * 256:(i + 1) * 256] = self.quarter[:, i * 4096 + self.spot(d, i):][:, :256].astype(bf16)

    def share(self):
        place = self.p
        self.first = [
            self.m.go(self.pack.at[place.member(*r)], self.out.at[self.lot(place.me, place.x), :], place.near(*r))
            for r in self.rel
        ]

    def spot(self, d, i):
        if i == 0 and len(self.refs) * 256 > self.cols:
            return (d % 2) * 2048 + (d // 2) * 256
        return d * 256

    def share_whole(self):
        place = self.p
        for copy in self.loads[len(self.refs):]:
            copy.wait()
        rows = pl.ds(pl.multiple_of(place.me * 128, 128), 128)
        self.whole_sent = []
        for i in range(self.cols // 256):
            mine = self.whole[0, :, pl.ds(pl.multiple_of(i * 512 + place.c * 256, 128), 256)]
            self.out[rows, i * 256:(i + 1) * 256] = mine.astype(bf16)
        for at, (dy, zr, cc) in enumerate(DIRECT):
            core = (place.c + cc) % 2
            for i in range(self.cols // 256):
                other = self.whole[zr, :, pl.ds(pl.multiple_of(i * 512 + core * 256, 128), 256)]
                self.mate[at, :, i * 256:(i + 1) * 256] = other.astype(bf16)
            self.whole_sent.append(self.m.go(self.mate.at[at], self.out.at[rows, :], place.beside(zr, cc)))

    def origin(self, r):
        return self.p.member(-r[0], r[1], r[2])

    def spread(self, which):
        place = self.p
        got = []
        for i in which:
            self.first[i].wait_recv()
            ref = self.out.at[self.lot(self.origin(self.rel[i]), place.x), :]
            got.append((i, self.m.go(ref, ref, place.across(1)), self.m.go(ref, ref, place.across(-1))))
        return got

    def onward(self, got):
        place = self.p
        halves = []
        for i, right, left in got:
            origin = self.origin(self.rel[i])
            right.wait_recv()
            ref = self.out.at[self.lot(origin, (place.x + 3) % 4, 0, 16), :]
            halves.append(self.m.go(ref, ref, place.across(1)))
            left.wait_recv()
            ref = self.out.at[self.lot(origin, (place.x + 1) % 4, 16, 32), :]
            halves.append(self.m.go(ref, ref, place.across(-1)))
        return halves


HANDOUT_COPIES = 12 * 5 + 3


def group_peers(place):
    return [place.near(dy, zr, cc) for dy, zr in REST for cc in (0, 1)] + [place.near(*r) for r in DIRECT] + [
        place.beside(1, 0), place.beside(1, 1)]


def await_all(copies):
    for copy in copies:
        copy.wait_recv()


class Scatter:
    def __init__(self, place, mover, wide, wpar, bufs, cut):
        self.p, self.m, self.wide, self.wpar, self.cut = place, mover, wide, wpar, cut
        self.S, self.RA, self.RLO, self.RHI, self.RL, self.RR, self.RZ = bufs
        self.right, self.left, self.over = place.near(1, 0, 0), place.near(-1, 0, 0), place.near(0, 1, 0)

    def multiply(self):
        rows = rows_of(self.cut.all)
        for i in range(4):
            part = jnp.dot(self.wide[rows, :], self.wpar[:, i * 256:(i + 1) * 256], preferred_element_type=f32)
            part = part.astype(bf16)
            self.S[2 * i, rows, :] = part[:, :128]
            self.S[2 * i + 1, rows, :] = part[:, 128:]

    def piece(self, zr, dy, span):
        return self.S.at[zr * 4 + dy, rows_of(span), :]

    def add(self, zr, dy, span, *others):
        rows = rows_of(span)
        total = self.S[zr * 4 + dy, rows, :].astype(f32)
        for other in others:
            total = total + other[rows, :].astype(f32)
        self.S[zr * 4 + dy, rows, :] = total.astype(bf16)

    def start_a(self):
        s = self.cut
        self.za = {dy: self.m.go(self.piece(1, dy, s.ALLA), self.RA.at[dy, rows_of(s.ALLA), :], self.over)
                   for dy in (2, 1, 3, 0)}

    def start_b(self):
        s = self.cut
        self.lo, self.hi = {}, {}
        for zr in (1, 0):
            self.lo[zr] = self.m.go(self.piece(zr, 2, s.LOB), self.RLO.at[zr, rows_of(s.LOB), :], self.right)
            self.hi[zr] = self.m.go(self.piece(zr, 2, s.HIB), self.RHI.at[zr, rows_of(s.HIB), :], self.left)

    def middle(self):
        s, m = self.cut, self.m
        lo, hi, za = self.lo, self.hi, self.za
        right, left, over = self.right, self.left, self.over
        RA, RLO, RHI, RL, RR, RZ = self.RA, self.RLO, self.RHI, self.RL, self.RR, self.RZ
        toR, toL = {}, {}
        for zr in (1, 0):
            lo[zr].wait_recv()
            self.add(zr, 1, s.LOB, RLO.at[zr])
            toR[zr] = m.go(self.piece(zr, 1, s.ALLB), RL.at[zr, rows_of(s.ALLB), :], right)
            hi[zr].wait_recv()
            self.add(zr, 3, s.HIB, RHI.at[zr])
            toL[zr] = m.go(self.piece(zr, 3, s.ALLB), RR.at[zr, rows_of(s.ALLB), :], left)
            if zr == 1:
                za[2].wait_recv()
                self.add(0, 2, s.ALLA, RA.at[2])
                loA = m.go(self.piece(0, 2, s.LOA), RLO.at[0, rows_of(s.LOA), :], right)
                hiA = m.go(self.piece(0, 2, s.HIA), RHI.at[0, rows_of(s.HIA), :], left)
        za[1].wait_recv()
        self.add(0, 1, s.ALLA, RA.at[1])
        za[3].wait_recv()
        self.add(0, 3, s.ALLA, RA.at[3])
        loA.wait_recv()
        self.add(0, 1, s.LOA, RLO.at[0])
        toRA = m.go(self.piece(0, 1, s.ALLA), RL.at[0, rows_of(s.ALLA), :], right)
        hiA.wait_recv()
        self.add(0, 3, s.HIA, RHI.at[0])
        toLA = m.go(self.piece(0, 3, s.ALLA), RR.at[0, rows_of(s.ALLA), :], left)
        toR[1].wait_recv()
        toL[1].wait_recv()
        self.add(1, 0, s.ALLB, RL.at[1], RR.at[1])
        zb = m.go(self.piece(1, 0, s.ALLB), RZ.at[rows_of(s.ALLB), :], over)
        self.last = (za[0], toRA, toLA), (toR[0], toL[0], zb)

    def total(self, span, which, extra):
        for copy in self.last[which]:
            copy.wait_recv()
        rows = rows_of(span)
        total = self.S[0, rows, :].astype(f32) + self.RL[0, rows, :].astype(f32)
        return total + self.RR[0, rows, :].astype(f32) + extra[rows, :].astype(f32)

    def total_a(self):
        return self.total(self.cut.ALLA, 0, self.RA.at[0])

    def total_b(self):
        return self.total(self.cut.ALLB, 1, self.RZ)


SCATTER_COPIES = 4 + 4 + 4 + 2 + 2 + 1
OTHERS = [(dx, dz) for dx in (2, 1, 3, 0) for dz in (1, 0) if (dx, dz) != (0, 0)]


def layer_kernel(lengths, gain1, gain2, tokens, token_lots_in, query, key, value, gate, out_weight, swish, up,
                 down_weight, out,
                 full1, squares, first, acc, qk, vg, retained, memory, decay, stats, gated,
                 quarter1, whole1, pack1, mate1, quarter2, whole2, pack2, mate2, second,
                 stage, wpar, wmate, lots, token_lots, pick, unpick, base, wide, full2, normed2, result, spare,
                 S1, RA1, RLO1, RHI1, RL1, RR1, RZ1, S2, RA2, RLO2, RHI2, RL2, RR2, RZ2,
                 local1, local2, load_sem, send, recv):
    place = Place()
    mover = Mover(send, recv)
    req = place.req
    hand1 = Handout(place, mover, (query, key, value, gate), first, quarter1, whole1, pack1, mate1, local1)
    hand2 = Handout(place, mover, (swish, up), second, quarter2, whole2, pack2, mate2, local2)
    mine = column(place.me)

    def group(dx, dz):
        return ((place.x + dx + 4) % 4) * 2 + (place.zh + dz) % 2

    peers = group_peers(place) + [(group(dx, dz), place.me) for dx, dz in OTHERS]
    greet(peers)
    hand1.load()
    loads = [pltpu.make_async_copy(tokens, full1.at[:, mine], load_sem.at[0]),
             pltpu.make_async_copy(out_weight, stage.at[0], load_sem.at[1]),
             pltpu.make_async_copy(down_weight, stage.at[1], load_sem.at[2]),
             pltpu.make_async_copy(token_lots_in.at[:, 0], token_lots.at[req], load_sem.at[3])]
    loads[0].start()
    mate_core = place.near(0, 0, 1)
    hand1.prepare()
    await_greetings(peers)
    hand1.share()
    loads[0].wait()
    gather = Gather(place, mover, full1, WIDE_CUT)
    gather.start_a()
    gather.start_b()
    hand1.share_whole()
    for copy in loads[1:]:
        copy.start()
    hand2.load()

    head = place.me // 2
    log_decay, span_decay = jnp.float32(0.0), jnp.float32(0.0)
    for h in range(H):
        rate = 1.0 - 2.0 ** (-5 - h)
        log_decay = jnp.where(head == h, jnp.float32(math.log(rate)), log_decay)
        span_decay = jnp.where(head == h, jnp.float32(rate ** SPAN), span_decay)
    order = [(dy, zr) for zr in (0, 1) for dy in range(4)]

    def set_weight(which):
        loads[1 + which].wait()
        for i, (dy, zr) in enumerate(order):
            wpar[which, 0:256, i * 128:(i + 1) * 128] = stage[which, :, column(place.member(dy, zr, 0))].astype(bf16)
            wmate[which, :, i * 128:(i + 1) * 128] = stage[which, :, column(place.member(dy, zr, 1))].astype(bf16)
        return mover.go(wmate.at[which], wpar.at[which, pl.ds(256, 256), :], mate_core)

    starts, counts = [], []
    start = jnp.int32(0)
    for r in range(8):
        length = lengths[r]
        turn = (req - r + 8) % 8
        count = 16 * (length // 128) + jnp.clip(length % 128 - 16 * turn, 0, 16)
        starts.append(start)
        counts.append(count)
        start = start + count

    def select():
        row = lax.broadcasted_iota(jnp.int32, (DEAL, 128), 0)
        lane = lax.broadcasted_iota(jnp.int32, (DEAL, 128), 1)
        slot = lax.broadcasted_iota(jnp.int32, (128, DEAL), 0)
        at = lax.broadcasted_iota(jnp.int32, (128, DEAL), 1)
        for r in range(8):
            chosen = (lane == row - starts[r]) & (lane < counts[r])
            pick[:, r * 128:(r + 1) * 128] = jnp.where(chosen, 1.0, 0.0).astype(bf16)
            chosen = (at == slot + starts[r]) & (slot < counts[r])
            unpick[r] = jnp.where(chosen, 1.0, 0.0).astype(bf16)

    def gained(rows, chips):
        total, square = None, None
        for chip in chips:
            depth = pl.ds(pl.multiple_of(chip * 256, 256), 256)
            values = full1[rows, depth].astype(f32)
            part = jnp.dot((values * gain1[:, depth]).astype(bf16), first[depth, :], preferred_element_type=f32)
            values = values * values
            values = values[:, :128] + values[:, 128:]
            total = part if total is None else total + part
            square = values if square is None else square + values
        return total, square

    def gather_product(rels, fresh=False):
        chips = [place.member(-dy, zr, 0) // 2 for dy, zr in rels]
        for dy, zr in rels:
            gather.ready(-dy, zr)

        def step(i, carry):
            rows = pl.ds(pl.multiple_of(i * SPAN, SPAN), SPAN)
            part, square = gained(rows, chips)
            acc[rows, :] = part if fresh else acc[rows, :] + part
            squares[rows, :] = square if fresh else squares[rows, :] + square
            return carry

        lax.fori_loop(0, LMAX // SPAN, step, 0)

    got1 = hand1.spread(range(12))
    i = lax.broadcasted_iota(jnp.int32, (SPAN, SPAN), 0)
    j = lax.broadcasted_iota(jnp.int32, (SPAN, SPAN), 1)
    decay[0] = jnp.where(i >= j, jnp.exp((i - j).astype(f32) * log_decay), 0.0)
    decay[1] = jnp.exp((i + 1).astype(f32) * log_decay)
    decay[2] = jnp.exp((SPAN - 1 - i).astype(f32) * log_decay)
    weights = [set_weight(0)]
    gather.first()
    halves1 = hand1.onward(got1[:4])
    gather.second()
    halves1 += hand1.onward(got1[4:8])
    gather.third()
    halves1 += hand1.onward(got1[8:])
    await_all(hand1.whole_sent[:1])
    gather_product([(0, 0)], True)
    hand2.prepare()
    hand2.share()
    hand2.share_whole()
    await_all(hand1.whole_sent[1:])
    gather_product([(0, 1)])
    await_all(halves1[:8])
    gather_product([(1, 0), (3, 0)])
    await_all(halves1[8:16])
    gather_product([(1, 1), (3, 1)])
    await_all(halves1[16:20])
    gather_product([(2, 0)])
    gather.finish()
    await_all(halves1[20:])
    dealt_tokens = []
    for dx, dz in OTHERS:
        target = group(dx, dz)
        turn = (target - req + 8) % 8
        dealt_tokens.append(mover.go(token_lots_in.at[:, turn], token_lots.at[req], (target, place.me)))
    last_chip = [place.member(-2, 1, 0) // 2]
    key_scale = jnp.where(place.c == 0, 1.0, DK ** (-0.5))
    swapped = []

    def project(b):
        rows = pl.ds(b * SPAN, SPAN)
        total, square = gained(rows, last_chip)
        square = jnp.sum(squares[rows, :] + square, axis=1, keepdims=True)
        total = (acc[rows, :] + total) * lax.rsqrt(square * (1.0 / 2048) + epsilon)
        qk[place.c, rows, :] = (total[:, :256] * key_scale).astype(bf16)
        ref = qk.at[place.c, rows, :]
        swapped.append(mover.go(ref, ref, mate_core))
        vg[0, rows, :] = total[:, 256:512].astype(bf16)
        vg[1, rows, :] = total[:, 512:].astype(bf16)

    def attend(b):
        rows = pl.ds(b * SPAN, SPAN)
        swapped[b].wait_recv()
        query_block, key_block, value_block = qk[0, rows, :], qk[1, rows, :], vg[0, rows, :]
        scores = lax.dot_general(query_block, key_block, (((1,), (1,)), ((), ())), preferred_element_type=f32)
        total = jnp.dot((scores * decay[0]).astype(bf16), value_block, preferred_element_type=f32)
        if b > 0:
            across = jnp.dot(query_block, memory[...].astype(bf16), preferred_element_type=f32)
            total = total + across * decay[1]
        if b < 3:
            decayed = (key_block.astype(f32) * decay[2]).astype(bf16)
            update = lax.dot_general(decayed, value_block, (((0,), (0,)), ((), ())), preferred_element_type=f32)
            memory[...] = update if b == 0 else memory[...] * span_decay + update
        retained[rows, :] = total
        mean = jnp.sum(total, axis=1, keepdims=True) * (1.0 / 256)
        spread = total - mean
        square = jnp.sum(spread * spread, axis=1, keepdims=True)
        lanes = lax.broadcasted_iota(jnp.int32, (SPAN, 128), 1)
        stats[0, b] = jnp.where(lanes < 64, mean, square)
        return mover.go(stats.at[0, b], stats.at[1, b], mate_core)

    def finish(b, told):
        rows = pl.ds(b * SPAN, SPAN)
        told.wait_recv()
        mean, square = stats[0, b, :, 0:1], stats[0, b, :, 64:65]
        mean2, square2 = stats[1, b, :, 0:1], stats[1, b, :, 64:65]
        gap = (mean - mean2) * 0.5
        middle = (mean + mean2) * 0.5
        var = (square + square2) * (1.0 / DV) + gap * gap
        grouped = (retained[rows, :] - middle) * lax.rsqrt(var + epsilon)
        gates = vg[1, rows, :].astype(f32)
        done = (gates / (1.0 + jnp.exp(-gates)) * grouped).astype(bf16)
        gated[2 * b:2 * b + 2] = done.reshape(2, 8, 16, 256)
        two = pl.ds(2 * b, 2)
        sent = []
        for dx, dz in OTHERS:
            target = group(dx, dz)
            turn = (target - req + 8) % 8
            sent.append(mover.go(gated.at[two, turn], lots.at[req, two], (target, place.me)))
        lots[req, 2 * b:2 * b + 2] = gated[2 * b:2 * b + 2, 0]
        return sent

    dealt, told = [], []
    project(0)
    for b in range(4):
        if b < 3:
            project(b + 1)
        told.append(attend(b))
        if b > 0:
            dealt += finish(b - 1, told[b - 1])
    dealt += finish(3, told[3])
    loads[3].wait()
    select()
    await_all(dealt)
    got2 = hand2.spread(range(12))
    def pass_core(which, cut, part):
        rows = rows_of(cut.all)
        wide[which, rows, 0:256] = part.astype(bf16)
        ref = wide.at[which, rows, pl.ds(0, 256)]
        return mover.go(ref, wide.at[which, rows, pl.ds(256, 256)], mate_core)

    def scatters(which, bufs):
        return [Scatter(place, mover, wide.at[which], wpar.at[which], bufs, cut) for cut in DEAL_CUTS]

    def begin(scatter, copy):
        copy.wait_recv()
        scatter.multiply()
        scatter.start_a()
        scatter.start_b()

    sent = []
    for cut in DEAL_CUTS:
        part = jnp.dot(pick[rows_of(cut.all), :], lots[...].reshape(LMAX, 256), preferred_element_type=f32)
        sent.append(pass_core(0, cut, part))
    weights[0].wait_recv()
    sums = scatters(0, (S1, RA1, RLO1, RHI1, RL1, RR1, RZ1))
    for scatter, copy in zip(sums, sent):
        begin(scatter, copy)
    weights.append(set_weight(1))
    await_all(dealt_tokens)
    base[...] = jnp.dot(pick[...], token_lots[...].reshape(LMAX, BLK), preferred_element_type=f32).astype(bf16)
    for scatter in sums:
        scatter.middle()
    gathers = []
    for scatter in sums:
        cut = scatter.cut
        gather = Gather(place, mover, full2, cut)
        gathers.append(gather)
        full2[rows_of(cut.ALLA), mine] = (base[rows_of(cut.ALLA), :].astype(f32) + scatter.total_a()).astype(bf16)
        gather.start_a()
        full2[rows_of(cut.ALLB), mine] = (base[rows_of(cut.ALLB), :].astype(f32) + scatter.total_b()).astype(bf16)
        gather.start_b()
    halves2 = hand2.onward(got2[:6])
    for gather in gathers:
        gather.first()
    for gather in gathers:
        gather.second()
    halves2 += hand2.onward(got2[6:])
    gathers[0].third()
    gathers[0].finish()
    await_all(halves2 + hand2.whole_sent)

    def forward(cut):
        def normalize(i, carry):
            rows = pl.ds(pl.multiple_of(cut.all[0] + i * 32, 32), 32)
            values = full2[rows, :].astype(f32)
            scale = lax.rsqrt(jnp.mean(values * values, axis=-1, keepdims=True) + epsilon)
            normed2[rows, :] = (values * scale * gain2[...]).astype(bf16)
            return carry

        lax.fori_loop(0, 7, normalize, 0)
        part = jnp.dot(normed2[rows_of(cut.all), :], second[...], preferred_element_type=f32)
        swished = part[:, :256]
        return pass_core(1, cut, swished / (1.0 + jnp.exp(-swished)) * part[:, 256:])

    sent = [forward(DEAL_CUTS[0])]
    gathers[1].third()
    gathers[1].finish()
    weights[1].wait_recv()
    sums = scatters(1, (S2, RA2, RLO2, RHI2, RL2, RR2, RZ2))
    begin(sums[0], sent[0])
    sent.append(forward(DEAL_CUTS[1]))
    begin(sums[1], sent[1])
    for scatter in sums:
        scatter.middle()
    for scatter in sums:
        for span, total in ((scatter.cut.ALLA, scatter.total_a), (scatter.cut.ALLB, scatter.total_b)):
            rows = rows_of(span)
            result[rows, :] = (full2[rows, mine].astype(f32) + total()).astype(bf16)
    for r in range(8):
        spare[r] = jnp.dot(unpick[r], result[...], preferred_element_type=f32).astype(bf16).reshape(8, 16, BLK)
    returned = []
    for dx, dz in OTHERS:
        target = group(dx, dz)
        returned.append(mover.go(spare.at[target], out.at[:, (req - target + 8) % 8], (target, place.me)))
    out[:, 0] = spare[req]
    await_all(returned)
    mover.drain()


LAYER_COPIES = 2 * HANDOUT_COPIES + 3 * GATHER_COPIES + 4 * SCATTER_COPIES + 7 * 6 + 2 + 4 + 4 + 4


def layer(*operands):
    vmem = pl.BlockSpec(memory_space=pltpu.VMEM)
    hbm = pl.BlockSpec(memory_space=pl.ANY)
    sums = [
        pltpu.VMEM((8, DEAL, BLK), bf16),
        pltpu.VMEM((4, DEAL, BLK), bf16),
        pltpu.VMEM((2, DEAL, BLK), bf16),
        pltpu.VMEM((2, DEAL, BLK), bf16),
        pltpu.VMEM((2, DEAL, BLK), bf16),
        pltpu.VMEM((2, DEAL, BLK), bf16),
        pltpu.VMEM((DEAL, BLK), bf16),
    ]
    return pl.pallas_call(
        layer_kernel,
        name="layer",
        out_shape=jax.ShapeDtypeStruct((8, 8, 16, BLK), bf16),
        in_specs=[pl.BlockSpec(memory_space=pltpu.SMEM), vmem, vmem] + [hbm] * 10,
        out_specs=vmem,
        scratch_shapes=[
            pltpu.VMEM((LMAX, 2048), bf16),
            pltpu.VMEM((LMAX, 128), f32),
            pltpu.VMEM((2048, 768), bf16),
            pltpu.VMEM((LMAX, 768), f32),
            pltpu.VMEM((2, LMAX, 256), bf16),
            pltpu.VMEM((2, LMAX, 256), bf16),

            pltpu.VMEM((LMAX, 256), f32),
            pltpu.VMEM((256, 256), f32),
            pltpu.VMEM((3, SPAN, SPAN), f32),
            pltpu.VMEM((2, 4, SPAN, 128), f32),
            pltpu.VMEM((8, 8, 16, 256), bf16),
            pltpu.VMEM((32, 12288), f32),
            pltpu.VMEM((2, 128, 1536), f32),
            pltpu.VMEM((16, 32, 768), bf16),
            pltpu.VMEM((3, 128, 768), bf16),
            pltpu.VMEM((32, 8192), f32),
            pltpu.VMEM((2, 128, 1024), f32),
            pltpu.VMEM((16, 32, 512), bf16),
            pltpu.VMEM((3, 128, 512), bf16),
            pltpu.VMEM((2048, 512), bf16),
            pltpu.VMEM((2, 256, 2048), f32),
            pltpu.VMEM((2, 512, 1024), bf16),
            pltpu.VMEM((2, 256, 1024), bf16),
            pltpu.VMEM((8, 8, 16, 256), bf16),
            pltpu.VMEM((8, 8, 16, BLK), bf16),
            pltpu.VMEM((DEAL, LMAX), bf16),
            pltpu.VMEM((8, 128, DEAL), bf16),
            pltpu.VMEM((DEAL, BLK), bf16),
            pltpu.VMEM((2, DEAL, 512), bf16),
            pltpu.VMEM((DEAL, 2048), bf16),
            pltpu.VMEM((DEAL, 2048), bf16),
            pltpu.VMEM((DEAL, BLK), bf16),
            pltpu.VMEM((8, 8, 16, BLK), bf16),
        ] + sums + sums + [
            pltpu.SemaphoreType.DMA((12,)),
            pltpu.SemaphoreType.DMA((6,)),
            pltpu.SemaphoreType.DMA((4,)),
            pltpu.SemaphoreType.DMA((LAYER_COPIES,)),
            pltpu.SemaphoreType.DMA((LAYER_COPIES,)),
        ],
        compiler_params=pltpu.CompilerParams(
            collective_id=0, has_side_effects=True, vmem_limit_bytes=63 * 2**20
        ),
    )(*operands)


def body(
    tokens,
    lengths,
    retention_gain,
    forward_gain,
    query_weight,
    key_weight,
    value_weight,
    gate_weight,
    output_weight,
    swish_weight,
    up_weight,
    down_weight,
):
    rows = tokens.reshape(8, 8, 16, BLK)
    finished = layer(
        lengths, retention_gain.reshape(1, 2048), forward_gain.reshape(1, 2048), tokens[0], rows,
        query_weight, key_weight, value_weight, gate_weight, output_weight, swish_weight, up_weight, down_weight
    )
    return finished.reshape(1, LMAX, BLK)


def solution(mesh):
    placed = (
        P("req", None, "mlp"),
        P(),
        P(),
        P(),
        P("mlp", None),
        P("mlp", None),
        P("mlp", None),
        P("mlp", None),
        P("mlp", None),
        P("mlp", None),
        P("mlp", None),
        P("mlp", None),
    )
    return jax.shard_map(
        body, mesh=mesh, in_specs=placed, out_specs=P("req", None, "mlp"), check_vma=False
    )
```

```python
import math
import jax
import jax.numpy as jnp
from jax import lax
from jax.experimental import pallas as pl
from jax.experimental.pallas import tpu as pltpu
from jax.sharding import PartitionSpec as P

H = 8
DK = 256
DV = 512
SPAN = 256
LMAX = 1024
BLK = 128
REST = [(1, 0), (3, 0), (1, 1), (3, 1), (2, 0), (2, 1)]
DIRECT = [(0, 0, 1), (0, 1, 0), (0, 1, 1)]

epsilon = 1e-05
bf16 = jnp.bfloat16
f32 = jnp.float32


class Cut:
    def __init__(self, rows, cut):
        half, rest = cut // 2, (rows + cut) // 2
        self.ALLA, self.LOA, self.HIA = (0, cut), (0, half), (half, cut)
        self.ALLB, self.LOB, self.HIB = (cut, rows), (cut, rest), (rest, rows)


WIDE_CUT = Cut(1024, 480)
DEAL = 448
DEAL_CUT = Cut(DEAL, 256)


def rows_of(span):
    return pl.ds(span[0], span[1] - span[0])


class Place:
    def __init__(self):
        self.req = lax.axis_index("req")
        self.me = lax.axis_index("mlp")
        self.x = self.req // 2
        self.zh = self.req % 2
        self.y = self.me // 4
        self.z = (self.me // 2) % 2
        self.c = self.me % 2

    def member(self, dy, zr, cc):
        return ((self.y + dy + 4) % 4) * 4 + ((self.z + zr) % 2) * 2 + (self.c + cc) % 2

    def near(self, dy, zr, cc):
        return (self.req, self.member(dy, zr, cc))

    def beside(self, zr, cc):
        return (self.x * 2 + (self.zh + zr) % 2, self.member(0, zr, cc))

    def across(self, dx):
        return (((self.x + dx + 4) % 4) * 2 + self.zh, self.me)


class Mover:
    def __init__(self, send, recv):
        self.send, self.recv, self.count, self.sent = send, recv, 0, []

    def plan(self, src, dst, device):
        i = self.count
        self.count += 1
        return pltpu.make_async_remote_copy(
            src_ref=src, dst_ref=dst, send_sem=self.send.at[i], recv_sem=self.recv.at[i],
            device_id=device, device_id_type=pl.DeviceIdType.MESH,
        )

    def go(self, src, dst, device):
        copy = self.plan(src, dst, device)
        copy.start()
        self.sent.append(copy)
        return copy

    def drain(self):
        for copy in self.sent:
            copy.wait_send()
        self.sent = []


def greet(devices):
    barrier = pltpu.get_barrier_semaphore()
    for device in devices:
        pl.semaphore_signal(barrier, inc=1, device_id=device, device_id_type=pl.DeviceIdType.MESH)


def await_greetings(devices):
    pl.semaphore_wait(pltpu.get_barrier_semaphore(), len(devices))


def column(member):
    return pl.ds(pl.multiple_of(member * BLK, BLK), BLK)


class Gather:
    def __init__(self, place, mover, full, cut):
        self.p, self.m, self.full, self.s = place, mover, full, cut
        self.need = {}

    def at(self, span, dy, zr):
        return self.full.at[rows_of(span), column(self.p.member(dy, zr, 0))]

    def pass_on(self, span, dy, zr, targets):
        place = self.p
        ref = self.at(span, dy, zr)
        out = []
        for step in targets:
            device = {"r": place.near(1, 0, 0), "l": place.near(-1, 0, 0),
                      "z": place.near(0, 1, 0), "c": place.near(0, 0, 1)}[step]
            copy = self.m.go(ref, ref, device)
            if step == "c":
                self.need.setdefault((dy % 4, zr), []).append(copy)
            else:
                out.append(copy)
        return out

    def start_a(self):
        self.a = self.pass_on(self.s.ALLA, 0, 0, "rlzc")

    def start_b(self):
        self.b = self.pass_on(self.s.ALLB, 0, 0, "zrlc")

    def first(self):
        ar, al, az = self.a
        bz, br, bl = self.b
        bz.wait_recv()
        self.zb = self.pass_on(self.s.ALLB, 0, 1, "rlc")
        ar.wait_recv()
        self.al1 = self.pass_on(self.s.LOA, -1, 0, "r") + self.pass_on(self.s.ALLA, -1, 0, "zc")
        al.wait_recv()
        self.ar1 = self.pass_on(self.s.HIA, 1, 0, "l") + self.pass_on(self.s.ALLA, 1, 0, "zc")
        br.wait_recv()
        self.bl1 = self.pass_on(self.s.LOB, -1, 0, "r") + self.pass_on(self.s.ALLB, -1, 0, "c")
        bl.wait_recv()
        self.br1 = self.pass_on(self.s.HIB, 1, 0, "l") + self.pass_on(self.s.ALLB, 1, 0, "c")
        az.wait_recv()
        self.pass_on(self.s.ALLA, 0, 1, "c")

    def second(self):
        lo, az = self.al1
        hi, az2 = self.ar1
        lo.wait_recv()
        self.o1 = self.pass_on(self.s.LOA, -2, 0, "zc")
        hi.wait_recv()
        self.o2 = self.pass_on(self.s.HIA, 2, 0, "zc")
        zr, zl = self.zb
        zr.wait_recv()
        self.zlo = self.pass_on(self.s.LOB, -1, 1, "r") + self.pass_on(self.s.ALLB, -1, 1, "c")
        zl.wait_recv()
        self.zhi = self.pass_on(self.s.HIB, 1, 1, "l") + self.pass_on(self.s.ALLB, 1, 1, "c")
        az.wait_recv()
        self.pass_on(self.s.ALLA, -1, 1, "c")
        az2.wait_recv()
        self.pass_on(self.s.ALLA, 1, 1, "c")

    def third(self):
        self.bl1[0].wait_recv()
        self.pass_on(self.s.LOB, -2, 0, "c")
        self.br1[0].wait_recv()
        self.pass_on(self.s.HIB, 2, 0, "c")
        self.o1[0].wait_recv()
        self.pass_on(self.s.LOA, -2, 1, "c")
        self.o2[0].wait_recv()
        self.pass_on(self.s.HIA, 2, 1, "c")
        self.zlo[0].wait_recv()
        self.pass_on(self.s.LOB, -2, 1, "c")
        self.zhi[0].wait_recv()
        self.pass_on(self.s.HIB, 2, 1, "c")

    def ready(self, dy, zr):
        for copy in self.need.pop((dy % 4, zr), ()):
            copy.wait_recv()

    def finish(self):
        for key in list(self.need):
            self.ready(*key)


GATHER_COPIES = 38


class Handout:
    def __init__(self, place, mover, refs, out, quarter, whole, pack, mate, local):
        self.p, self.m, self.refs, self.out = place, mover, refs, out
        self.quarter, self.whole, self.pack, self.mate, self.local = quarter, whole, pack, mate, local
        self.rel = [(dy, zr, cc) for dy, zr in REST for cc in (0, 1)]
        self.cols = out.shape[1]

    def load(self):
        place = self.p
        part = pl.ds(pl.multiple_of(place.x * 32, 32), 32)
        self.loads, at = [], 0
        for ref in self.refs:
            self.one(ref.at[part, :], self.quarter.at[:, pl.ds(at, ref.shape[1])])
            at += ref.shape[1]
        for zr in (0, 1):
            chip = place.member(0, zr, 0) // 2
            at = 0
            for ref in self.refs:
                wide = ref.shape[1] // 8
                self.one(ref.at[:, pl.ds(pl.multiple_of(chip * wide, 128), wide)], self.whole.at[zr, :, pl.ds(at, wide)])
                at += wide

    def one(self, src, dst):
        copy = pltpu.make_async_copy(src, dst, self.local.at[len(self.loads)])
        copy.start()
        self.loads.append(copy)

    def lot(self, member, slot, low=0, high=32):
        return pl.ds(pl.multiple_of(member * 128 + slot * 32 + low, 16), high - low)

    def prepare(self):
        for copy in self.loads[:len(self.refs)]:
            copy.wait()
        for d in range(16):
            for i in range(self.cols // 256):
                self.pack[d, :, i * 256:(i + 1) * 256] = self.quarter[:, i * 4096 + self.spot(d, i):][:, :256].astype(bf16)

    def prepare_whole(self):
        place = self.p
        for copy in self.loads[len(self.refs):]:
            copy.wait()
        rows = pl.ds(pl.multiple_of(place.me * 128, 128), 128)
        for i in range(self.cols // 256):
            mine = self.whole[0, :, pl.ds(pl.multiple_of(i * 512 + place.c * 256, 128), 256)]
            self.out[rows, i * 256:(i + 1) * 256] = mine.astype(bf16)
        for at, (dy, zr, cc) in enumerate(DIRECT):
            core = (place.c + cc) % 2
            for i in range(self.cols // 256):
                other = self.whole[zr, :, pl.ds(pl.multiple_of(i * 512 + core * 256, 128), 256)]
                self.mate[at, :, i * 256:(i + 1) * 256] = other.astype(bf16)

    def share(self):
        place = self.p
        self.first = [
            self.m.go(self.pack.at[place.member(*r)], self.out.at[self.lot(place.me, place.x), :], place.near(*r))
            for r in self.rel
        ]

    def spot(self, d, i):
        if i == 0 and len(self.refs) * 256 > self.cols:
            return (d % 2) * 2048 + (d // 2) * 256
        return d * 256

    def share_whole(self):
        place = self.p
        rows = pl.ds(pl.multiple_of(place.me * 128, 128), 128)
        self.whole_sent = [
            self.m.go(self.mate.at[at], self.out.at[rows, :], place.beside(zr, cc))
            for at, (dy, zr, cc) in enumerate(DIRECT)
        ]

    def origin(self, r):
        return self.p.member(-r[0], r[1], r[2])

    def spread(self, which):
        place = self.p
        got = []
        for i in which:
            self.first[i].wait_recv()
            ref = self.out.at[self.lot(self.origin(self.rel[i]), place.x), :]
            got.append((i, self.m.go(ref, ref, place.across(1)), self.m.go(ref, ref, place.across(-1))))
        return got

    def onward(self, got):
        place = self.p
        halves = []
        for i, right, left in got:
            origin = self.origin(self.rel[i])
            right.wait_recv()
            ref = self.out.at[self.lot(origin, (place.x + 3) % 4, 0, 16), :]
            halves.append(self.m.go(ref, ref, place.across(1)))
            left.wait_recv()
            ref = self.out.at[self.lot(origin, (place.x + 1) % 4, 16, 32), :]
            halves.append(self.m.go(ref, ref, place.across(-1)))
        return halves


HANDOUT_COPIES = 12 * 5 + 3


def group_peers(place):
    return [place.near(dy, zr, cc) for dy, zr in REST for cc in (0, 1)] + [place.near(*r) for r in DIRECT] + [
        place.beside(1, 0), place.beside(1, 1)]


def await_all(copies):
    for copy in copies:
        copy.wait_recv()


class DirectGather:
    def __init__(self, place, mover, full, cut):
        self.p, self.m, self.full, self.s = place, mover, full, cut
        self.cores = []

    def send(self, span, dy, zr, device):
        ref = self.full.at[rows_of(span), column(self.p.member(dy, zr, 0))]
        return self.m.go(ref, ref, device)

    def share(self, span, dy, zr):
        self.cores.append(self.send(span, dy, zr, self.p.near(0, 0, 1)))

    def ring(self, span, zr):
        return {dy: self.send(span, 0, zr, self.p.near(dy, 0, 0)) for dy in (2, 1, 3)}

    def start_a(self):
        self.a = self.ring(self.s.ALLA, 0)
        self.za = {0: self.send(self.s.ALLA, 0, 0, self.p.near(0, 1, 0))}
        self.share(self.s.ALLA, 0, 0)

    def start_b(self):
        self.zb = self.send(self.s.ALLB, 0, 0, self.p.near(0, 1, 0))
        self.b0 = self.ring(self.s.ALLB, 0)
        self.share(self.s.ALLB, 0, 0)

    def run(self):
        s = self.s
        self.zb.wait_recv()
        b1 = self.ring(s.ALLB, 1)
        self.share(s.ALLB, 0, 1)
        for dy in (1, 3, 2):
            self.a[dy].wait_recv()
            self.za[dy] = self.send(s.ALLA, -dy, 0, self.p.near(0, 1, 0))
            self.share(s.ALLA, -dy, 0)
        self.za[0].wait_recv()
        self.share(s.ALLA, 0, 1)
        for dy in (1, 3, 2):
            self.b0[dy].wait_recv()
            self.share(s.ALLB, -dy, 0)
        for dy in (1, 3, 2):
            b1[dy].wait_recv()
            self.share(s.ALLB, -dy, 1)
            self.za[dy].wait_recv()
            self.share(s.ALLA, -dy, 1)
        for copy in self.cores:
            copy.wait_recv()


DIRECT_COPIES = 30


class Scatter:
    def __init__(self, place, mover, wide, wpar, bufs):
        self.p, self.m, self.wide, self.wpar = place, mover, wide, wpar
        self.S, self.RA, self.RY, self.RZ = bufs
        self.over = place.near(0, 1, 0)

    def multiply(self, span):
        rows = rows_of(span)
        for i in range(4):
            part = jnp.dot(self.wide[rows, :], self.wpar[:, i * 256:(i + 1) * 256], preferred_element_type=f32)
            part = part.astype(bf16)
            self.S[2 * i, rows, :] = part[:, :128]
            self.S[2 * i + 1, rows, :] = part[:, 128:]

    def ring(self, span, zr, dy):
        rows = rows_of(span)
        return self.m.go(self.S.at[zr * 4 + dy, rows, :], self.RY.at[zr, dy, rows, :], self.p.near(dy, 0, 0))

    def total(self, span, zr, *others):
        rows = rows_of(span)
        total = self.S[zr * 4, rows, :].astype(f32)
        for dy in (1, 3, 2):
            total = total + self.RY[zr, dy, rows, :].astype(f32)
        for other in others:
            total = total + other[rows, :].astype(f32)
        return total

    def start_a(self):
        rows = rows_of(DEAL_CUT.ALLA)
        self.za = {dy: self.m.go(self.S.at[4 + dy, rows, :], self.RA.at[dy, rows, :], self.over)
                   for dy in (2, 1, 3, 0)}

    def start_b(self):
        self.b = {zr: [self.ring(DEAL_CUT.ALLB, zr, dy) for dy in (2, 1, 3)] for zr in (1, 0)}

    def middle(self):
        rows = rows_of(DEAL_CUT.ALLA)
        self.a = []
        for dy in (2, 1, 3):
            self.za[dy].wait_recv()
            total = self.S[dy, rows, :].astype(f32) + self.RA[dy, rows, :].astype(f32)
            self.S[dy, rows, :] = total.astype(bf16)
            self.a.append(self.ring(DEAL_CUT.ALLA, 0, dy))
        await_all(self.b[1])
        rows = rows_of(DEAL_CUT.ALLB)
        self.S[4, rows, :] = self.total(DEAL_CUT.ALLB, 1).astype(bf16)
        self.zb = self.m.go(self.S.at[4, rows, :], self.RZ.at[rows, :], self.over)

    def total_a(self):
        await_all([self.za[0]] + self.a)
        return self.total(DEAL_CUT.ALLA, 0, self.RA.at[0])

    def total_b(self):
        await_all(self.b[0] + [self.zb])
        return self.total(DEAL_CUT.ALLB, 0, self.RZ)


SCATTER_COPIES = 4 + 6 + 3 + 1
OTHERS = [(dx, dz) for dx in (2, 1, 3, 0) for dz in (1, 0) if (dx, dz) != (0, 0)]


def layer_kernel(lengths, gain1, gain2, tokens, token_lots_in, query, key, value, gate, out_weight, swish, up,
                 down_weight, out,
                 full1, squares, first, acc, qk, vg, retained, memory, decay, stats, gated,
                 quarter1, whole1, pack1, mate1, quarter2, whole2, pack2, mate2, second,
                 stage, wpar, wmate, lots, token_lots, pick, unpick, base, wide, full2, normed2, result, spare,
                 S1, RA1, RY1, RZ1, S2, RA2, RY2, RZ2,
                 local1, local2, load_sem, send, recv):
    place = Place()
    mover = Mover(send, recv)
    req = place.req
    cut = DEAL_CUT
    hand1 = Handout(place, mover, (query, key, value, gate), first, quarter1, whole1, pack1, mate1, local1)
    hand2 = Handout(place, mover, (swish, up), second, quarter2, whole2, pack2, mate2, local2)
    mine = column(place.me)

    def group(dx, dz):
        return ((place.x + dx + 4) % 4) * 2 + (place.zh + dz) % 2

    peers = group_peers(place) + [(group(dx, dz), place.me) for dx, dz in OTHERS]
    greet(peers)
    hand1.load()
    loads = [pltpu.make_async_copy(tokens, full1.at[:, mine], load_sem.at[0]),
             pltpu.make_async_copy(out_weight, stage.at[0], load_sem.at[1]),
             pltpu.make_async_copy(down_weight, stage.at[1], load_sem.at[2]),
             pltpu.make_async_copy(token_lots_in.at[:, 0], token_lots.at[req], load_sem.at[3])]
    for copy in loads:
        copy.start()
    hand2.load()
    mate_core = place.near(0, 0, 1)
    hand1.prepare()
    await_greetings(peers)
    hand1.share()
    loads[0].wait()
    gather = Gather(place, mover, full1, WIDE_CUT)
    hand1.prepare_whole()
    hand1.share_whole()

    head = place.me // 2
    log_decay, span_decay = jnp.float32(0.0), jnp.float32(0.0)
    for h in range(H):
        rate = 1.0 - 2.0 ** (-5 - h)
        log_decay = jnp.where(head == h, jnp.float32(math.log(rate)), log_decay)
        span_decay = jnp.where(head == h, jnp.float32(rate ** SPAN), span_decay)
    i = lax.broadcasted_iota(jnp.int32, (SPAN, SPAN), 0)
    j = lax.broadcasted_iota(jnp.int32, (SPAN, SPAN), 1)
    decay[0] = jnp.where(i >= j, jnp.exp((i - j).astype(f32) * log_decay), 0.0)
    decay[1] = jnp.exp((i + 1).astype(f32) * log_decay)
    decay[2] = jnp.exp((SPAN - 1 - i).astype(f32) * log_decay)

    order = [(dy, zr) for zr in (0, 1) for dy in range(4)]

    def set_weight(which):
        loads[1 + which].wait()
        for i, (dy, zr) in enumerate(order):
            wpar[which, 0:256, i * 128:(i + 1) * 128] = stage[which, :, column(place.member(dy, zr, 0))].astype(bf16)
            wmate[which, :, i * 128:(i + 1) * 128] = stage[which, :, column(place.member(dy, zr, 1))].astype(bf16)
        return mover.go(wmate.at[which], wpar.at[which, pl.ds(256, 256), :], mate_core)

    starts, counts = [], []
    start = jnp.int32(0)
    for r in range(8):
        length = lengths[r]
        turn = (req - r + 8) % 8
        count = 16 * (length // 128) + jnp.clip(length % 128 - 16 * turn, 0, 16)
        starts.append(start)
        counts.append(count)
        start = start + count

    def select():
        row = lax.broadcasted_iota(jnp.int32, (DEAL, 128), 0)
        lane = lax.broadcasted_iota(jnp.int32, (DEAL, 128), 1)
        slot = lax.broadcasted_iota(jnp.int32, (128, DEAL), 0)
        at = lax.broadcasted_iota(jnp.int32, (128, DEAL), 1)
        for r in range(8):
            chosen = (lane == row - starts[r]) & (lane < counts[r])
            pick[:, r * 128:(r + 1) * 128] = jnp.where(chosen, 1.0, 0.0).astype(bf16)
            chosen = (at == slot + starts[r]) & (slot < counts[r])
            unpick[r] = jnp.where(chosen, 1.0, 0.0).astype(bf16)

    def gained(rows, chips):
        total, square = None, None
        for chip in chips:
            depth = pl.ds(pl.multiple_of(chip * 256, 256), 256)
            values = full1[rows, depth].astype(f32)
            part = jnp.dot((values * gain1[:, depth]).astype(bf16), first[depth, :], preferred_element_type=f32)
            values = values * values
            values = values[:, :128] + values[:, 128:]
            total = part if total is None else total + part
            square = values if square is None else square + values
        return total, square

    def gather_product(rels, fresh=False):
        chips = [place.member(-dy, zr, 0) // 2 for dy, zr in rels]
        for dy, zr in rels:
            gather.ready(-dy, zr)

        def step(i, carry):
            rows = pl.ds(pl.multiple_of(i * SPAN, SPAN), SPAN)
            part, square = gained(rows, chips)
            acc[rows, :] = part if fresh else acc[rows, :] + part
            squares[rows, :] = square if fresh else squares[rows, :] + square
            return carry

        lax.fori_loop(0, LMAX // SPAN, step, 0)

    got1 = hand1.spread(range(4))
    gather.start_a()
    gather.start_b()
    hand2.prepare()
    got1 += hand1.spread(range(4, 12))
    hand2.prepare_whole()
    weights = [set_weight(0)]
    gather.first()
    halves1 = hand1.onward(got1[:4])
    await_all(hand1.whole_sent[:1])
    gather_product([(0, 0)], True)
    gather.second()
    halves1 += hand1.onward(got1[4:8])
    await_all(hand1.whole_sent[1:])
    gather_product([(0, 1)])
    gather.third()
    halves1 += hand1.onward(got1[8:])
    hand2.share()
    hand2.share_whole()
    await_all(halves1[:8])
    gather_product([(1, 0), (3, 0)])
    await_all(halves1[8:16])
    gather_product([(1, 1), (3, 1)])
    await_all(halves1[16:20])
    gather_product([(2, 0)])
    gather.finish()
    await_all(halves1[20:])
    dealt_tokens = []
    for dx, dz in OTHERS:
        target = group(dx, dz)
        turn = (target - req + 8) % 8
        dealt_tokens.append(mover.go(token_lots_in.at[:, turn], token_lots.at[req], (target, place.me)))
    last_chip = [place.member(-2, 1, 0) // 2]
    key_scale = jnp.where(place.c == 0, 1.0, DK ** (-0.5))
    swapped = []

    def project(b):
        rows = pl.ds(b * SPAN, SPAN)
        total, square = gained(rows, last_chip)
        square = jnp.sum(squares[rows, :] + square, axis=1, keepdims=True)
        total = (acc[rows, :] + total) * lax.rsqrt(square * (1.0 / 2048) + epsilon)
        qk[place.c, rows, :] = (total[:, :256] * key_scale).astype(bf16)
        ref = qk.at[place.c, rows, :]
        swapped.append(mover.go(ref, ref, mate_core))
        vg[0, rows, :] = total[:, 256:512].astype(bf16)
        vg[1, rows, :] = total[:, 512:].astype(bf16)

    def attend(b):
        rows = pl.ds(b * SPAN, SPAN)
        swapped[b].wait_recv()
        query_block, key_block, value_block = qk[0, rows, :], qk[1, rows, :], vg[0, rows, :]
        scores = lax.dot_general(query_block, key_block, (((1,), (1,)), ((), ())), preferred_element_type=f32)
        total = jnp.dot((scores * decay[0]).astype(bf16), value_block, preferred_element_type=f32)
        if b > 0:
            across = jnp.dot(query_block, memory[...].astype(bf16), preferred_element_type=f32)
            total = total + across * decay[1]
        if b < 3:
            decayed = (key_block.astype(f32) * decay[2]).astype(bf16)
            update = lax.dot_general(decayed, value_block, (((0,), (0,)), ((), ())), preferred_element_type=f32)
            memory[...] = update if b == 0 else memory[...] * span_decay + update
        retained[rows, :] = total
        mean = jnp.sum(total, axis=1, keepdims=True) * (1.0 / 256)
        spread = total - mean
        square = jnp.sum(spread * spread, axis=1, keepdims=True)
        lanes = lax.broadcasted_iota(jnp.int32, (SPAN, 128), 1)
        stats[0, b] = jnp.where(lanes < 64, mean, square)
        return mover.go(stats.at[0, b], stats.at[1, b], mate_core)

    def finish(b, told):
        rows = pl.ds(b * SPAN, SPAN)
        told.wait_recv()
        mean, square = stats[0, b, :, 0:1], stats[0, b, :, 64:65]
        mean2, square2 = stats[1, b, :, 0:1], stats[1, b, :, 64:65]
        gap = (mean - mean2) * 0.5
        middle = (mean + mean2) * 0.5
        var = (square + square2) * (1.0 / DV) + gap * gap
        grouped = (retained[rows, :] - middle) * lax.rsqrt(var + epsilon)
        gates = vg[1, rows, :].astype(f32)
        done = (gates / (1.0 + jnp.exp(-gates)) * grouped).astype(bf16)
        gated[2 * b:2 * b + 2] = done.reshape(2, 8, 16, 256)
        two = pl.ds(2 * b, 2)
        sent = []
        for dx, dz in OTHERS:
            target = group(dx, dz)
            turn = (target - req + 8) % 8
            sent.append(mover.go(gated.at[two, turn], lots.at[req, two], (target, place.me)))
        lots[req, 2 * b:2 * b + 2] = gated[2 * b:2 * b + 2, 0]
        return sent

    dealt, told = [], []
    project(0)
    for b in range(4):
        if b < 3:
            project(b + 1)
        told.append(attend(b))
        if b > 0:
            dealt += finish(b - 1, told[b - 1])
    dealt += finish(3, told[3])
    loads[3].wait()
    select()
    await_all(dealt)
    got2 = hand2.spread(range(12))
    sent = []
    for span in (cut.ALLA, cut.ALLB):
        rows = rows_of(span)
        part = jnp.dot(pick[rows, :], lots[...].reshape(LMAX, 256), preferred_element_type=f32)
        wide[0, rows, 0:256] = part.astype(bf16)
        ref = wide.at[0, rows, pl.ds(0, 256)]
        sent.append(mover.go(ref, wide.at[0, rows, pl.ds(256, 256)], mate_core))

    scatter = Scatter(place, mover, wide.at[0], wpar.at[0], (S1, RA1, RY1, RZ1))
    weights[0].wait_recv()
    sent[0].wait_recv()
    scatter.multiply(cut.ALLA)
    scatter.start_a()
    sent[1].wait_recv()
    scatter.multiply(cut.ALLB)
    scatter.start_b()
    weights.append(set_weight(1))
    await_all(dealt_tokens)
    base[...] = jnp.dot(pick[...], token_lots[...].reshape(LMAX, BLK), preferred_element_type=f32).astype(bf16)
    scatter.middle()
    gather = DirectGather(place, mover, full2, cut)
    full2[rows_of(cut.ALLA), mine] = (base[rows_of(cut.ALLA), :].astype(f32) + scatter.total_a()).astype(bf16)
    gather.start_a()
    full2[rows_of(cut.ALLB), mine] = (base[rows_of(cut.ALLB), :].astype(f32) + scatter.total_b()).astype(bf16)
    gather.start_b()
    halves2 = hand2.onward(got2)
    gather.run()
    await_all(halves2 + hand2.whole_sent)
    def normalize(i, carry):
        rows = pl.ds(pl.multiple_of(i * 32, 32), 32)
        values = full2[rows, :].astype(f32)
        scale = lax.rsqrt(jnp.mean(values * values, axis=-1, keepdims=True) + epsilon)
        normed2[rows, :] = (values * scale * gain2[...]).astype(bf16)
        return carry

    lax.fori_loop(0, DEAL // 32, normalize, 0)
    sent = []
    for span in (cut.ALLA, cut.ALLB):
        rows = rows_of(span)
        part = jnp.dot(normed2[rows, :], second[...], preferred_element_type=f32)
        swished = part[:, :256]
        wide[1, rows, 0:256] = (swished / (1.0 + jnp.exp(-swished)) * part[:, 256:]).astype(bf16)
        ref = wide.at[1, rows, pl.ds(0, 256)]
        sent.append(mover.go(ref, wide.at[1, rows, pl.ds(256, 256)], mate_core))
    scatter = Scatter(place, mover, wide.at[1], wpar.at[1], (S2, RA2, RY2, RZ2))
    weights[1].wait_recv()
    sent[0].wait_recv()
    scatter.multiply(cut.ALLA)
    scatter.start_a()
    sent[1].wait_recv()
    scatter.multiply(cut.ALLB)
    scatter.start_b()
    scatter.middle()
    for span, total in ((cut.ALLA, scatter.total_a), (cut.ALLB, scatter.total_b)):
        rows = rows_of(span)
        result[rows, :] = (full2[rows, mine].astype(f32) + total()).astype(bf16)
    for r in range(8):
        spare[r] = jnp.dot(unpick[r], result[...], preferred_element_type=f32).astype(bf16).reshape(8, 16, BLK)
    returned = []
    for dx, dz in OTHERS:
        target = group(dx, dz)
        returned.append(mover.go(spare.at[target], out.at[:, (req - target + 8) % 8], (target, place.me)))
    out[:, 0] = spare[req]
    await_all(returned)
    mover.drain()


LAYER_COPIES = 2 * HANDOUT_COPIES + GATHER_COPIES + DIRECT_COPIES + 2 * SCATTER_COPIES + 7 * 6 + 2 + 4 + 4 + 4


def layer(*operands):
    vmem = pl.BlockSpec(memory_space=pltpu.VMEM)
    hbm = pl.BlockSpec(memory_space=pl.ANY)
    sums = [
        pltpu.VMEM((8, DEAL, BLK), bf16),
        pltpu.VMEM((4, DEAL, BLK), bf16),
        pltpu.VMEM((2, 4, DEAL, BLK), bf16),
        pltpu.VMEM((DEAL, BLK), bf16),
    ]
    return pl.pallas_call(
        layer_kernel,
        name="layer",
        out_shape=jax.ShapeDtypeStruct((8, 8, 16, BLK), bf16),
        in_specs=[pl.BlockSpec(memory_space=pltpu.SMEM), vmem, vmem] + [hbm] * 10,
        out_specs=vmem,
        scratch_shapes=[
            pltpu.VMEM((LMAX, 2048), bf16),
            pltpu.VMEM((LMAX, 128), f32),
            pltpu.VMEM((2048, 768), bf16),
            pltpu.VMEM((LMAX, 768), f32),
            pltpu.VMEM((2, LMAX, 256), bf16),
            pltpu.VMEM((2, LMAX, 256), bf16),

            pltpu.VMEM((LMAX, 256), f32),
            pltpu.VMEM((256, 256), f32),
            pltpu.VMEM((3, SPAN, SPAN), f32),
            pltpu.VMEM((2, 4, SPAN, 128), f32),
            pltpu.VMEM((8, 8, 16, 256), bf16),
            pltpu.VMEM((32, 12288), f32),
            pltpu.VMEM((2, 128, 1536), f32),
            pltpu.VMEM((16, 32, 768), bf16),
            pltpu.VMEM((3, 128, 768), bf16),
            pltpu.VMEM((32, 8192), f32),
            pltpu.VMEM((2, 128, 1024), f32),
            pltpu.VMEM((16, 32, 512), bf16),
            pltpu.VMEM((3, 128, 512), bf16),
            pltpu.VMEM((2048, 512), bf16),
            pltpu.VMEM((2, 256, 2048), f32),
            pltpu.VMEM((2, 512, 1024), bf16),
            pltpu.VMEM((2, 256, 1024), bf16),
            pltpu.VMEM((8, 8, 16, 256), bf16),
            pltpu.VMEM((8, 8, 16, BLK), bf16),
            pltpu.VMEM((DEAL, LMAX), bf16),
            pltpu.VMEM((8, 128, DEAL), bf16),
            pltpu.VMEM((DEAL, BLK), bf16),
            pltpu.VMEM((2, DEAL, 512), bf16),
            pltpu.VMEM((DEAL, 2048), bf16),
            pltpu.VMEM((DEAL, 2048), bf16),
            pltpu.VMEM((DEAL, BLK), bf16),
            pltpu.VMEM((8, 8, 16, BLK), bf16),
        ] + sums + sums + [
            pltpu.SemaphoreType.DMA((12,)),
            pltpu.SemaphoreType.DMA((6,)),
            pltpu.SemaphoreType.DMA((4,)),
            pltpu.SemaphoreType.DMA((LAYER_COPIES,)),
            pltpu.SemaphoreType.DMA((LAYER_COPIES,)),
        ],
        compiler_params=pltpu.CompilerParams(
            collective_id=0, has_side_effects=True, vmem_limit_bytes=63 * 2**20
        ),
    )(*operands)


def body(
    tokens,
    lengths,
    retention_gain,
    forward_gain,
    query_weight,
    key_weight,
    value_weight,
    gate_weight,
    output_weight,
    swish_weight,
    up_weight,
    down_weight,
):
    rows = tokens.reshape(8, 8, 16, BLK)
    finished = layer(
        lengths, retention_gain.reshape(1, 2048), forward_gain.reshape(1, 2048), tokens[0], rows,
        query_weight, key_weight, value_weight, gate_weight, output_weight, swish_weight, up_weight, down_weight
    )
    return finished.reshape(1, LMAX, BLK)


def solution(mesh):
    placed = (
        P("req", None, "mlp"),
        P(),
        P(),
        P(),
        P("mlp", None),
        P("mlp", None),
        P("mlp", None),
        P("mlp", None),
        P("mlp", None),
        P("mlp", None),
        P("mlp", None),
        P("mlp", None),
    )
    return jax.shard_map(
        body, mesh=mesh, in_specs=placed, out_specs=P("req", None, "mlp"), check_vma=False
    )
```

```python
import math
import jax
import jax.numpy as jnp
from jax import lax
from jax.experimental import pallas as pl
from jax.experimental.pallas import tpu as pltpu
from jax.sharding import PartitionSpec as P

H = 8
DK = 256
DV = 512
SPAN = 256
LMAX = 1024
BLK = 128
REST = [(1, 0), (3, 0), (1, 1), (3, 1), (2, 0), (2, 1)]
DIRECT = [(0, 0, 1), (0, 1, 0), (0, 1, 1)]

epsilon = 1e-05
bf16 = jnp.bfloat16
f32 = jnp.float32


class Cut:
    def __init__(self, rows, cut):
        half, rest = cut // 2, (rows + cut) // 2
        self.ALLA, self.LOA, self.HIA = (0, cut), (0, half), (half, cut)
        self.ALLB, self.LOB, self.HIB = (cut, rows), (cut, rest), (rest, rows)


WIDE_CUT = Cut(1024, 480)
DEAL = 448
DEAL_CUT = Cut(DEAL, 256)


def rows_of(span):
    return pl.ds(span[0], span[1] - span[0])


class Place:
    def __init__(self):
        self.req = lax.axis_index("req")
        self.me = lax.axis_index("mlp")
        self.x = self.req // 2
        self.zh = self.req % 2
        self.y = self.me // 4
        self.z = (self.me // 2) % 2
        self.c = self.me % 2

    def member(self, dy, zr, cc):
        return ((self.y + dy + 4) % 4) * 4 + ((self.z + zr) % 2) * 2 + (self.c + cc) % 2

    def near(self, dy, zr, cc):
        return (self.req, self.member(dy, zr, cc))

    def beside(self, zr, cc):
        return (self.x * 2 + (self.zh + zr) % 2, self.member(0, zr, cc))

    def across(self, dx):
        return (((self.x + dx + 4) % 4) * 2 + self.zh, self.me)


class Mover:
    def __init__(self, send, recv):
        self.send, self.recv, self.count, self.sent = send, recv, 0, []

    def plan(self, src, dst, device):
        i = self.count
        self.count += 1
        return pltpu.make_async_remote_copy(
            src_ref=src, dst_ref=dst, send_sem=self.send.at[i], recv_sem=self.recv.at[i],
            device_id=device, device_id_type=pl.DeviceIdType.MESH,
        )

    def go(self, src, dst, device):
        copy = self.plan(src, dst, device)
        copy.start()
        self.sent.append(copy)
        return copy

    def drain(self):
        for copy in self.sent:
            copy.wait_send()
        self.sent = []


def greet(devices):
    barrier = pltpu.get_barrier_semaphore()
    for device in devices:
        pl.semaphore_signal(barrier, inc=1, device_id=device, device_id_type=pl.DeviceIdType.MESH)


def await_greetings(devices):
    pl.semaphore_wait(pltpu.get_barrier_semaphore(), len(devices))


def column(member):
    return pl.ds(pl.multiple_of(member * BLK, BLK), BLK)


class Gather:
    def __init__(self, place, mover, full, cut):
        self.p, self.m, self.full, self.s = place, mover, full, cut
        self.need = {}

    def at(self, span, dy, zr):
        return self.full.at[rows_of(span), column(self.p.member(dy, zr, 0))]

    def pass_on(self, span, dy, zr, targets):
        place = self.p
        ref = self.at(span, dy, zr)
        out = []
        for step in targets:
            device = {"r": place.near(1, 0, 0), "l": place.near(-1, 0, 0),
                      "z": place.near(0, 1, 0), "c": place.near(0, 0, 1)}[step]
            copy = self.m.go(ref, ref, device)
            if step == "c":
                self.need.setdefault((dy % 4, zr), []).append(copy)
            else:
                out.append(copy)
        return out

    def start_a(self):
        self.a = self.pass_on(self.s.ALLA, 0, 0, "rlzc")

    def start_b(self):
        self.b = self.pass_on(self.s.ALLB, 0, 0, "zrlc")

    def first(self):
        ar, al, az = self.a
        bz, br, bl = self.b
        bz.wait_recv()
        self.zb = self.pass_on(self.s.ALLB, 0, 1, "rlc")
        ar.wait_recv()
        self.al1 = self.pass_on(self.s.LOA, -1, 0, "r") + self.pass_on(self.s.ALLA, -1, 0, "zc")
        al.wait_recv()
        self.ar1 = self.pass_on(self.s.HIA, 1, 0, "l") + self.pass_on(self.s.ALLA, 1, 0, "zc")
        br.wait_recv()
        self.bl1 = self.pass_on(self.s.LOB, -1, 0, "r") + self.pass_on(self.s.ALLB, -1, 0, "c")
        bl.wait_recv()
        self.br1 = self.pass_on(self.s.HIB, 1, 0, "l") + self.pass_on(self.s.ALLB, 1, 0, "c")
        az.wait_recv()
        self.pass_on(self.s.ALLA, 0, 1, "c")

    def second(self):
        lo, az = self.al1
        hi, az2 = self.ar1
        lo.wait_recv()
        self.o1 = self.pass_on(self.s.LOA, -2, 0, "zc")
        hi.wait_recv()
        self.o2 = self.pass_on(self.s.HIA, 2, 0, "zc")
        zr, zl = self.zb
        zr.wait_recv()
        self.zlo = self.pass_on(self.s.LOB, -1, 1, "r") + self.pass_on(self.s.ALLB, -1, 1, "c")
        zl.wait_recv()
        self.zhi = self.pass_on(self.s.HIB, 1, 1, "l") + self.pass_on(self.s.ALLB, 1, 1, "c")
        az.wait_recv()
        self.pass_on(self.s.ALLA, -1, 1, "c")
        az2.wait_recv()
        self.pass_on(self.s.ALLA, 1, 1, "c")

    def third(self):
        self.bl1[0].wait_recv()
        self.pass_on(self.s.LOB, -2, 0, "c")
        self.br1[0].wait_recv()
        self.pass_on(self.s.HIB, 2, 0, "c")
        self.o1[0].wait_recv()
        self.pass_on(self.s.LOA, -2, 1, "c")
        self.o2[0].wait_recv()
        self.pass_on(self.s.HIA, 2, 1, "c")
        self.zlo[0].wait_recv()
        self.pass_on(self.s.LOB, -2, 1, "c")
        self.zhi[0].wait_recv()
        self.pass_on(self.s.HIB, 2, 1, "c")

    def ready(self, dy, zr):
        for copy in self.need.pop((dy % 4, zr), ()):
            copy.wait_recv()

    def finish(self):
        for key in list(self.need):
            self.ready(*key)


GATHER_COPIES = 38


class Handout:
    def __init__(self, place, mover, refs, out, quarter, whole, pack, mate, local):
        self.p, self.m, self.refs, self.out = place, mover, refs, out
        self.quarter, self.whole, self.pack, self.mate, self.local = quarter, whole, pack, mate, local
        self.rel = [(dy, zr, cc) for dy, zr in REST for cc in (0, 1)]
        self.cols = out.shape[1]

    def load(self):
        place = self.p
        part = pl.ds(pl.multiple_of(place.x * 32, 32), 32)
        self.loads, at = [], 0
        for ref in self.refs:
            self.one(ref.at[part, :], self.quarter.at[:, pl.ds(at, ref.shape[1])])
            at += ref.shape[1]
        for zr in (0, 1):
            chip = place.member(0, zr, 0) // 2
            at = 0
            for ref in self.refs:
                wide = ref.shape[1] // 8
                self.one(ref.at[:, pl.ds(pl.multiple_of(chip * wide, 128), wide)], self.whole.at[zr, :, pl.ds(at, wide)])
                at += wide

    def one(self, src, dst):
        copy = pltpu.make_async_copy(src, dst, self.local.at[len(self.loads)])
        copy.start()
        self.loads.append(copy)

    def lot(self, member, slot, low=0, high=32):
        return pl.ds(pl.multiple_of(member * 128 + slot * 32 + low, 16), high - low)

    def prepare(self):
        for copy in self.loads[:len(self.refs)]:
            copy.wait()
        for d in range(16):
            for i in range(self.cols // 256):
                self.pack[d, :, i * 256:(i + 1) * 256] = self.quarter[:, i * 4096 + self.spot(d, i):][:, :256].astype(bf16)

    def prepare_whole(self):
        place = self.p
        for copy in self.loads[len(self.refs):]:
            copy.wait()
        rows = pl.ds(pl.multiple_of(place.me * 128, 128), 128)
        for i in range(self.cols // 256):
            mine = self.whole[0, :, pl.ds(pl.multiple_of(i * 512 + place.c * 256, 128), 256)]
            self.out[rows, i * 256:(i + 1) * 256] = mine.astype(bf16)
        for at, (dy, zr, cc) in enumerate(DIRECT):
            core = (place.c + cc) % 2
            for i in range(self.cols // 256):
                other = self.whole[zr, :, pl.ds(pl.multiple_of(i * 512 + core * 256, 128), 256)]
                self.mate[at, :, i * 256:(i + 1) * 256] = other.astype(bf16)

    def share(self):
        place = self.p
        self.first = [
            self.m.go(self.pack.at[place.member(*r)], self.out.at[self.lot(place.me, place.x), :], place.near(*r))
            for r in self.rel
        ]

    def spot(self, d, i):
        if i == 0 and len(self.refs) * 256 > self.cols:
            return (d % 2) * 2048 + (d // 2) * 256
        return d * 256

    def share_whole(self):
        place = self.p
        rows = pl.ds(pl.multiple_of(place.me * 128, 128), 128)
        self.whole_sent = [
            self.m.go(self.mate.at[at], self.out.at[rows, :], place.beside(zr, cc))
            for at, (dy, zr, cc) in enumerate(DIRECT)
        ]

    def origin(self, r):
        return self.p.member(-r[0], r[1], r[2])

    def spread(self, which):
        place = self.p
        got = []
        for i in which:
            self.first[i].wait_recv()
            ref = self.out.at[self.lot(self.origin(self.rel[i]), place.x), :]
            got.append((i, self.m.go(ref, ref, place.across(1)), self.m.go(ref, ref, place.across(-1))))
        return got

    def onward(self, got):
        place = self.p
        halves = []
        for i, right, left in got:
            origin = self.origin(self.rel[i])
            right.wait_recv()
            ref = self.out.at[self.lot(origin, (place.x + 3) % 4, 0, 16), :]
            halves.append(self.m.go(ref, ref, place.across(1)))
            left.wait_recv()
            ref = self.out.at[self.lot(origin, (place.x + 1) % 4, 16, 32), :]
            halves.append(self.m.go(ref, ref, place.across(-1)))
        return halves


HANDOUT_COPIES = 12 * 5 + 3


def group_peers(place):
    return [place.near(dy, zr, cc) for dy, zr in REST for cc in (0, 1)] + [place.near(*r) for r in DIRECT] + [
        place.beside(1, 0), place.beside(1, 1)]


def await_all(copies):
    for copy in copies:
        copy.wait_recv()


class DirectGather:
    def __init__(self, place, mover, full, cut):
        self.p, self.m, self.full, self.s = place, mover, full, cut
        self.cores = []

    def send(self, span, dy, zr, device):
        ref = self.full.at[rows_of(span), column(self.p.member(dy, zr, 0))]
        return self.m.go(ref, ref, device)

    def share(self, span, dy, zr):
        self.cores.append(self.send(span, dy, zr, self.p.near(0, 0, 1)))

    def ring(self, span, zr):
        return {dy: self.send(span, 0, zr, self.p.near(dy, 0, 0)) for dy in (2, 1, 3)}

    def start_a(self):
        self.a = self.ring(self.s.ALLA, 0)
        self.za = {0: self.send(self.s.ALLA, 0, 0, self.p.near(0, 1, 0))}
        self.share(self.s.ALLA, 0, 0)

    def start_b(self):
        self.zb = self.send(self.s.ALLB, 0, 0, self.p.near(0, 1, 0))
        self.b0 = self.ring(self.s.ALLB, 0)
        self.share(self.s.ALLB, 0, 0)

    def near_side(self):
        s = self.s
        self.zb.wait_recv()
        self.b1 = self.ring(s.ALLB, 1)
        late = len(self.cores)
        self.share(s.ALLB, 0, 1)
        for dy in (1, 3, 2):
            self.a[dy].wait_recv()
            self.za[dy] = self.send(s.ALLA, -dy, 0, self.p.near(0, 1, 0))
            self.share(s.ALLA, -dy, 0)
        for dy in (1, 3, 2):
            self.b0[dy].wait_recv()
            self.share(s.ALLB, -dy, 0)
        later = self.cores[late:late + 1]
        for copy in self.cores[:late] + self.cores[late + 1:]:
            copy.wait_recv()
        self.cores = later

    def far_side(self):
        s = self.s
        self.za[0].wait_recv()
        self.share(s.ALLA, 0, 1)
        for dy in (1, 3, 2):
            self.b1[dy].wait_recv()
            self.share(s.ALLB, -dy, 1)
            self.za[dy].wait_recv()
            self.share(s.ALLA, -dy, 1)
        await_all(self.cores)


DIRECT_COPIES = 30


class Scatter:
    def __init__(self, place, mover, wide, wpar, bufs):
        self.p, self.m, self.wide, self.wpar = place, mover, wide, wpar
        self.S, self.RA, self.RY, self.RZ = bufs
        self.over = place.near(0, 1, 0)

    def multiply(self, span):
        rows = rows_of(span)
        for i in range(4):
            part = jnp.dot(self.wide[rows, :], self.wpar[:, i * 256:(i + 1) * 256], preferred_element_type=f32)
            part = part.astype(bf16)
            self.S[2 * i, rows, :] = part[:, :128]
            self.S[2 * i + 1, rows, :] = part[:, 128:]

    def ring(self, span, zr, dy):
        rows = rows_of(span)
        return self.m.go(self.S.at[zr * 4 + dy, rows, :], self.RY.at[zr, dy, rows, :], self.p.near(dy, 0, 0))

    def total(self, span, zr, *others):
        rows = rows_of(span)
        total = self.S[zr * 4, rows, :].astype(f32)
        for dy in (1, 3, 2):
            total = total + self.RY[zr, dy, rows, :].astype(f32)
        for other in others:
            total = total + other[rows, :].astype(f32)
        return total

    def start_a(self):
        rows = rows_of(DEAL_CUT.ALLA)
        self.za = {dy: self.m.go(self.S.at[4 + dy, rows, :], self.RA.at[dy, rows, :], self.over)
                   for dy in (2, 1, 3, 0)}

    def start_b(self):
        self.b = {zr: [self.ring(DEAL_CUT.ALLB, zr, dy) for dy in (2, 1, 3)] for zr in (1, 0)}

    def middle(self):
        rows = rows_of(DEAL_CUT.ALLA)
        self.a = []
        for dy in (2, 1, 3):
            self.za[dy].wait_recv()
            total = self.S[dy, rows, :].astype(f32) + self.RA[dy, rows, :].astype(f32)
            self.S[dy, rows, :] = total.astype(bf16)
            self.a.append(self.ring(DEAL_CUT.ALLA, 0, dy))
        await_all(self.b[1])
        rows = rows_of(DEAL_CUT.ALLB)
        self.S[4, rows, :] = self.total(DEAL_CUT.ALLB, 1).astype(bf16)
        self.zb = self.m.go(self.S.at[4, rows, :], self.RZ.at[rows, :], self.over)

    def total_a(self):
        await_all([self.za[0]] + self.a)
        return self.total(DEAL_CUT.ALLA, 0, self.RA.at[0])

    def total_b(self):
        await_all(self.b[0] + [self.zb])
        return self.total(DEAL_CUT.ALLB, 0, self.RZ)


SCATTER_COPIES = 4 + 6 + 3 + 1
OTHERS = [(dx, dz) for dx in (2, 1, 3, 0) for dz in (1, 0) if (dx, dz) != (0, 0)]


def layer_kernel(lengths, gain1, gain2, tokens, token_lots_in, query, key, value, gate, out_weight, swish, up,
                 down_weight, out,
                 full1, squares, first, acc, qk, vg, retained, memory, decay, stats, gated,
                 quarter1, whole1, pack1, mate1, quarter2, whole2, pack2, mate2, second,
                 stage, wpar, wmate, lots, token_lots, pick, unpick, base, wide, full2, acc2, squares2, result, spare,
                 S1, RA1, RY1, RZ1, S2, RA2, RY2, RZ2,
                 local1, local2, load_sem, send, recv):
    place = Place()
    mover = Mover(send, recv)
    req = place.req
    cut = DEAL_CUT
    hand1 = Handout(place, mover, (query, key, value, gate), first, quarter1, whole1, pack1, mate1, local1)
    hand2 = Handout(place, mover, (swish, up), second, quarter2, whole2, pack2, mate2, local2)
    mine = column(place.me)

    def group(dx, dz):
        return ((place.x + dx + 4) % 4) * 2 + (place.zh + dz) % 2

    peers = group_peers(place) + [(group(dx, dz), place.me) for dx, dz in OTHERS]
    greet(peers)
    hand1.load()
    loads = [pltpu.make_async_copy(tokens, full1.at[:, mine], load_sem.at[0]),
             pltpu.make_async_copy(out_weight, stage.at[0], load_sem.at[1]),
             pltpu.make_async_copy(down_weight, stage.at[1], load_sem.at[2]),
             pltpu.make_async_copy(token_lots_in.at[:, 0], token_lots.at[req], load_sem.at[3])]
    for copy in loads:
        copy.start()
    hand2.load()
    mate_core = place.near(0, 0, 1)
    hand1.prepare()
    await_greetings(peers)
    hand1.share()
    loads[0].wait()
    gather = Gather(place, mover, full1, WIDE_CUT)
    hand1.prepare_whole()
    hand1.share_whole()

    head = place.me // 2
    log_decay, span_decay = jnp.float32(0.0), jnp.float32(0.0)
    for h in range(H):
        rate = 1.0 - 2.0 ** (-5 - h)
        log_decay = jnp.where(head == h, jnp.float32(math.log(rate)), log_decay)
        span_decay = jnp.where(head == h, jnp.float32(rate ** SPAN), span_decay)
    i = lax.broadcasted_iota(jnp.int32, (SPAN, SPAN), 0)
    j = lax.broadcasted_iota(jnp.int32, (SPAN, SPAN), 1)
    decay[0] = jnp.where(i >= j, jnp.exp((i - j).astype(f32) * log_decay), 0.0)
    decay[1] = jnp.exp((i + 1).astype(f32) * log_decay)
    decay[2] = jnp.exp((SPAN - 1 - i).astype(f32) * log_decay)

    order = [(dy, zr) for zr in (0, 1) for dy in range(4)]

    def set_weight(which):
        loads[1 + which].wait()
        for i, (dy, zr) in enumerate(order):
            wpar[which, 0:256, i * 128:(i + 1) * 128] = stage[which, :, column(place.member(dy, zr, 0))].astype(bf16)
            wmate[which, :, i * 128:(i + 1) * 128] = stage[which, :, column(place.member(dy, zr, 1))].astype(bf16)
        return mover.go(wmate.at[which], wpar.at[which, pl.ds(256, 256), :], mate_core)

    starts, counts = [], []
    start = jnp.int32(0)
    for r in range(8):
        length = lengths[r]
        turn = (req - r + 8) % 8
        count = 16 * (length // 128) + jnp.clip(length % 128 - 16 * turn, 0, 16)
        starts.append(start)
        counts.append(count)
        start = start + count

    def select():
        row = lax.broadcasted_iota(jnp.int32, (DEAL, 128), 0)
        lane = lax.broadcasted_iota(jnp.int32, (DEAL, 128), 1)
        slot = lax.broadcasted_iota(jnp.int32, (128, DEAL), 0)
        at = lax.broadcasted_iota(jnp.int32, (128, DEAL), 1)
        for r in range(8):
            chosen = (lane == row - starts[r]) & (lane < counts[r])
            pick[:, r * 128:(r + 1) * 128] = jnp.where(chosen, 1.0, 0.0).astype(bf16)
            chosen = (at == slot + starts[r]) & (slot < counts[r])
            unpick[r] = jnp.where(chosen, 1.0, 0.0).astype(bf16)

    def gained(rows, chips):
        total, square = None, None
        for chip in chips:
            depth = pl.ds(pl.multiple_of(chip * 256, 256), 256)
            values = full1[rows, depth].astype(f32)
            part = jnp.dot((values * gain1[:, depth]).astype(bf16), first[depth, :], preferred_element_type=f32)
            values = values * values
            values = values[:, :128] + values[:, 128:]
            total = part if total is None else total + part
            square = values if square is None else square + values
        return total, square

    def gather_product(rels, fresh=False):
        chips = [place.member(-dy, zr, 0) // 2 for dy, zr in rels]
        for dy, zr in rels:
            gather.ready(-dy, zr)

        def step(i, carry):
            rows = pl.ds(pl.multiple_of(i * SPAN, SPAN), SPAN)
            part, square = gained(rows, chips)
            acc[rows, :] = part if fresh else acc[rows, :] + part
            squares[rows, :] = square if fresh else squares[rows, :] + square
            return carry

        lax.fori_loop(0, LMAX // SPAN, step, 0)

    got1 = hand1.spread(range(4))
    gather.start_a()
    gather.start_b()
    hand2.prepare()
    got1 += hand1.spread(range(4, 12))
    hand2.prepare_whole()
    weights = [set_weight(0)]
    gather.first()
    halves1 = hand1.onward(got1[:4])
    await_all(hand1.whole_sent[:1])
    gather_product([(0, 0)], True)
    gather.second()
    halves1 += hand1.onward(got1[4:8])
    await_all(hand1.whole_sent[1:])
    gather_product([(0, 1)])
    gather.third()
    halves1 += hand1.onward(got1[8:])
    hand2.share()
    hand2.share_whole()
    await_all(halves1[:8])
    gather_product([(1, 0), (3, 0)])
    await_all(halves1[8:16])
    gather_product([(1, 1), (3, 1)])
    await_all(halves1[16:20])
    gather_product([(2, 0)])
    gather.finish()
    await_all(halves1[20:])
    dealt_tokens = []
    for dx, dz in OTHERS:
        target = group(dx, dz)
        turn = (target - req + 8) % 8
        dealt_tokens.append(mover.go(token_lots_in.at[:, turn], token_lots.at[req], (target, place.me)))
    last_chip = [place.member(-2, 1, 0) // 2]
    key_scale = jnp.where(place.c == 0, 1.0, DK ** (-0.5))
    swapped = []

    def project(b):
        rows = pl.ds(b * SPAN, SPAN)
        total, square = gained(rows, last_chip)
        square = jnp.sum(squares[rows, :] + square, axis=1, keepdims=True)
        total = (acc[rows, :] + total) * lax.rsqrt(square * (1.0 / 2048) + epsilon)
        qk[place.c, rows, :] = (total[:, :256] * key_scale).astype(bf16)
        ref = qk.at[place.c, rows, :]
        swapped.append(mover.go(ref, ref, mate_core))
        vg[0, rows, :] = total[:, 256:512].astype(bf16)
        vg[1, rows, :] = total[:, 512:].astype(bf16)

    def attend(b):
        rows = pl.ds(b * SPAN, SPAN)
        swapped[b].wait_recv()
        query_block, key_block, value_block = qk[0, rows, :], qk[1, rows, :], vg[0, rows, :]
        scores = lax.dot_general(query_block, key_block, (((1,), (1,)), ((), ())), preferred_element_type=f32)
        total = jnp.dot((scores * decay[0]).astype(bf16), value_block, preferred_element_type=f32)
        if b > 0:
            across = jnp.dot(query_block, memory[...].astype(bf16), preferred_element_type=f32)
            total = total + across * decay[1]
        if b < 3:
            decayed = (key_block.astype(f32) * decay[2]).astype(bf16)
            update = lax.dot_general(decayed, value_block, (((0,), (0,)), ((), ())), preferred_element_type=f32)
            memory[...] = update if b == 0 else memory[...] * span_decay + update
        retained[rows, :] = total
        mean = jnp.sum(total, axis=1, keepdims=True) * (1.0 / 256)
        spread = total - mean
        square = jnp.sum(spread * spread, axis=1, keepdims=True)
        lanes = lax.broadcasted_iota(jnp.int32, (SPAN, 128), 1)
        stats[0, b] = jnp.where(lanes < 64, mean, square)
        return mover.go(stats.at[0, b], stats.at[1, b], mate_core)

    def finish(b, told):
        rows = pl.ds(b * SPAN, SPAN)
        told.wait_recv()
        mean, square = stats[0, b, :, 0:1], stats[0, b, :, 64:65]
        mean2, square2 = stats[1, b, :, 0:1], stats[1, b, :, 64:65]
        gap = (mean - mean2) * 0.5
        middle = (mean + mean2) * 0.5
        var = (square + square2) * (1.0 / DV) + gap * gap
        grouped = (retained[rows, :] - middle) * lax.rsqrt(var + epsilon)
        gates = vg[1, rows, :].astype(f32)
        done = (gates / (1.0 + jnp.exp(-gates)) * grouped).astype(bf16)
        gated[2 * b:2 * b + 2] = done.reshape(2, 8, 16, 256)
        two = pl.ds(2 * b, 2)
        sent = []
        for dx, dz in OTHERS:
            target = group(dx, dz)
            turn = (target - req + 8) % 8
            sent.append(mover.go(gated.at[two, turn], lots.at[req, two], (target, place.me)))
        lots[req, 2 * b:2 * b + 2] = gated[2 * b:2 * b + 2, 0]
        return sent

    dealt, told = [], []
    project(0)
    for b in range(4):
        if b < 3:
            project(b + 1)
            if b == 0:
                got2 = hand2.spread(range(4))
        told.append(attend(b))
        if b > 0:
            dealt += finish(b - 1, told[b - 1])
    dealt += finish(3, told[3])
    loads[3].wait()
    select()
    await_all(dealt)
    got2 += hand2.spread(range(4, 12))
    sent = []
    for span in (cut.ALLA, cut.ALLB):
        rows = rows_of(span)
        part = jnp.dot(pick[rows, :], lots[...].reshape(LMAX, 256), preferred_element_type=f32)
        wide[0, rows, 0:256] = part.astype(bf16)
        ref = wide.at[0, rows, pl.ds(0, 256)]
        sent.append(mover.go(ref, wide.at[0, rows, pl.ds(256, 256)], mate_core))

    scatter = Scatter(place, mover, wide.at[0], wpar.at[0], (S1, RA1, RY1, RZ1))
    weights[0].wait_recv()
    sent[0].wait_recv()
    scatter.multiply(cut.ALLA)
    scatter.start_a()
    sent[1].wait_recv()
    scatter.multiply(cut.ALLB)
    scatter.start_b()
    weights.append(set_weight(1))
    await_all(dealt_tokens)
    base[...] = jnp.dot(pick[...], token_lots[...].reshape(LMAX, BLK), preferred_element_type=f32).astype(bf16)
    scatter.middle()
    halves2 = hand2.onward(got2)
    gather = DirectGather(place, mover, full2, cut)
    full2[rows_of(cut.ALLA), mine] = (base[rows_of(cut.ALLA), :].astype(f32) + scatter.total_a()).astype(bf16)
    gather.start_a()
    full2[rows_of(cut.ALLB), mine] = (base[rows_of(cut.ALLB), :].astype(f32) + scatter.total_b()).astype(bf16)
    gather.start_b()

    def forward(rows, zr):
        total, square = None, None
        for dy in range(4):
            depth = pl.ds(pl.multiple_of(place.member(dy, zr, 0) // 2 * 256, 256), 256)
            values = full2[rows, depth].astype(f32)
            part = jnp.dot((values * gain2[:, depth]).astype(bf16), second[depth, :], preferred_element_type=f32)
            values = values * values
            values = values[:, :128] + values[:, 128:]
            total = part if total is None else total + part
            square = values if square is None else square + values
        return total, square

    gather.near_side()
    await_all(halves2 + hand2.whole_sent)
    for span in (cut.ALLA, cut.ALLB):
        rows = rows_of(span)
        acc2[rows, :], squares2[rows, :] = forward(rows, 0)
    gather.far_side()
    sent = []
    for span in (cut.ALLA, cut.ALLB):
        rows = rows_of(span)
        part, square = forward(rows, 1)
        square = jnp.sum(squares2[rows, :] + square, axis=1, keepdims=True)
        part = (acc2[rows, :] + part) * lax.rsqrt(square * (1.0 / 2048) + epsilon)
        swished = part[:, :256]
        wide[1, rows, 0:256] = (swished / (1.0 + jnp.exp(-swished)) * part[:, 256:]).astype(bf16)
        ref = wide.at[1, rows, pl.ds(0, 256)]
        sent.append(mover.go(ref, wide.at[1, rows, pl.ds(256, 256)], mate_core))
    scatter = Scatter(place, mover, wide.at[1], wpar.at[1], (S2, RA2, RY2, RZ2))
    weights[1].wait_recv()
    sent[0].wait_recv()
    scatter.multiply(cut.ALLA)
    scatter.start_a()
    sent[1].wait_recv()
    scatter.multiply(cut.ALLB)
    scatter.start_b()
    scatter.middle()
    for span, total in ((cut.ALLA, scatter.total_a), (cut.ALLB, scatter.total_b)):
        rows = rows_of(span)
        result[rows, :] = (full2[rows, mine].astype(f32) + total()).astype(bf16)
    returned = []
    for dx, dz in OTHERS:
        target = group(dx, dz)
        back = jnp.dot(unpick[target], result[...], preferred_element_type=f32)
        spare[target] = back.astype(bf16).reshape(8, 16, BLK)
        returned.append(mover.go(spare.at[target], out.at[:, (req - target + 8) % 8], (target, place.me)))
    back = jnp.dot(unpick[req], result[...], preferred_element_type=f32)
    out[:, 0] = back.astype(bf16).reshape(8, 16, BLK)
    await_all(returned)
    mover.drain()


LAYER_COPIES = 2 * HANDOUT_COPIES + GATHER_COPIES + DIRECT_COPIES + 2 * SCATTER_COPIES + 7 * 6 + 2 + 4 + 4 + 4


def layer(*operands):
    vmem = pl.BlockSpec(memory_space=pltpu.VMEM)
    hbm = pl.BlockSpec(memory_space=pl.ANY)
    sums = [
        pltpu.VMEM((8, DEAL, BLK), bf16),
        pltpu.VMEM((4, DEAL, BLK), bf16),
        pltpu.VMEM((2, 4, DEAL, BLK), bf16),
        pltpu.VMEM((DEAL, BLK), bf16),
    ]
    return pl.pallas_call(
        layer_kernel,
        name="layer",
        out_shape=jax.ShapeDtypeStruct((8, 8, 16, BLK), bf16),
        in_specs=[pl.BlockSpec(memory_space=pltpu.SMEM), vmem, vmem] + [hbm] * 10,
        out_specs=vmem,
        scratch_shapes=[
            pltpu.VMEM((LMAX, 2048), bf16),
            pltpu.VMEM((LMAX, 128), f32),
            pltpu.VMEM((2048, 768), bf16),
            pltpu.VMEM((LMAX, 768), f32),
            pltpu.VMEM((2, LMAX, 256), bf16),
            pltpu.VMEM((2, LMAX, 256), bf16),

            pltpu.VMEM((LMAX, 256), f32),
            pltpu.VMEM((256, 256), f32),
            pltpu.VMEM((3, SPAN, SPAN), f32),
            pltpu.VMEM((2, 4, SPAN, 128), f32),
            pltpu.VMEM((8, 8, 16, 256), bf16),
            pltpu.VMEM((32, 12288), f32),
            pltpu.VMEM((2, 128, 1536), f32),
            pltpu.VMEM((16, 32, 768), bf16),
            pltpu.VMEM((3, 128, 768), bf16),
            pltpu.VMEM((32, 8192), f32),
            pltpu.VMEM((2, 128, 1024), f32),
            pltpu.VMEM((16, 32, 512), bf16),
            pltpu.VMEM((3, 128, 512), bf16),
            pltpu.VMEM((2048, 512), bf16),
            pltpu.VMEM((2, 256, 2048), f32),
            pltpu.VMEM((2, 512, 1024), bf16),
            pltpu.VMEM((2, 256, 1024), bf16),
            pltpu.VMEM((8, 8, 16, 256), bf16),
            pltpu.VMEM((8, 8, 16, BLK), bf16),
            pltpu.VMEM((DEAL, LMAX), bf16),
            pltpu.VMEM((8, 128, DEAL), bf16),
            pltpu.VMEM((DEAL, BLK), bf16),
            pltpu.VMEM((2, DEAL, 512), bf16),
            pltpu.VMEM((DEAL, 2048), bf16),
            pltpu.VMEM((DEAL, 512), f32),
            pltpu.VMEM((DEAL, 128), f32),
            pltpu.VMEM((DEAL, BLK), bf16),
            pltpu.VMEM((8, 8, 16, BLK), bf16),
        ] + sums + sums + [
            pltpu.SemaphoreType.DMA((12,)),
            pltpu.SemaphoreType.DMA((6,)),
            pltpu.SemaphoreType.DMA((4,)),
            pltpu.SemaphoreType.DMA((LAYER_COPIES,)),
            pltpu.SemaphoreType.DMA((LAYER_COPIES,)),
        ],
        compiler_params=pltpu.CompilerParams(
            collective_id=0, has_side_effects=True, vmem_limit_bytes=63 * 2**20
        ),
    )(*operands)


def body(
    tokens,
    lengths,
    retention_gain,
    forward_gain,
    query_weight,
    key_weight,
    value_weight,
    gate_weight,
    output_weight,
    swish_weight,
    up_weight,
    down_weight,
):
    rows = tokens.reshape(8, 8, 16, BLK)
    finished = layer(
        lengths, retention_gain.reshape(1, 2048), forward_gain.reshape(1, 2048), tokens[0], rows,
        query_weight, key_weight, value_weight, gate_weight, output_weight, swish_weight, up_weight, down_weight
    )
    return finished.reshape(1, LMAX, BLK)


def solution(mesh):
    placed = (
        P("req", None, "mlp"),
        P(),
        P(),
        P(),
        P("mlp", None),
        P("mlp", None),
        P("mlp", None),
        P("mlp", None),
        P("mlp", None),
        P("mlp", None),
        P("mlp", None),
        P("mlp", None),
    )
    return jax.shard_map(
        body, mesh=mesh, in_specs=placed, out_specs=P("req", None, "mlp"), check_vma=False
    )
```

```python
import math
import jax
import jax.numpy as jnp
from jax import lax
from jax.experimental import pallas as pl
from jax.experimental.pallas import tpu as pltpu
from jax.sharding import PartitionSpec as P

H = 8
DK = 256
DV = 512
SPAN = 256
LMAX = 1024
BLK = 128
REST = [(1, 0), (3, 0), (1, 1), (3, 1), (2, 0), (2, 1)]
DIRECT = [(0, 0, 1), (0, 1, 0), (0, 1, 1)]

epsilon = 1e-05
bf16 = jnp.bfloat16
f32 = jnp.float32


class Cut:
    def __init__(self, rows, cut):
        half, rest = cut // 2, (rows + cut) // 2
        self.ALLA, self.LOA, self.HIA = (0, cut), (0, half), (half, cut)
        self.ALLB, self.LOB, self.HIB = (cut, rows), (cut, rest), (rest, rows)


WIDE_CUT = Cut(1024, 512)
DEAL = 448
DEAL_CUT = Cut(DEAL, 256)


def rows_of(span):
    return pl.ds(span[0], span[1] - span[0])


class Place:
    def __init__(self):
        self.req = lax.axis_index("req")
        self.me = lax.axis_index("mlp")
        self.x = self.req // 2
        self.zh = self.req % 2
        self.y = self.me // 4
        self.z = (self.me // 2) % 2
        self.c = self.me % 2

    def member(self, dy, zr, cc):
        return ((self.y + dy + 4) % 4) * 4 + ((self.z + zr) % 2) * 2 + (self.c + cc) % 2

    def near(self, dy, zr, cc):
        return (self.req, self.member(dy, zr, cc))

    def beside(self, zr, cc):
        return (self.x * 2 + (self.zh + zr) % 2, self.member(0, zr, cc))

    def across(self, dx):
        return (((self.x + dx + 4) % 4) * 2 + self.zh, self.me)


class Mover:
    def __init__(self, send, recv):
        self.send, self.recv, self.count, self.sent = send, recv, 0, []

    def plan(self, src, dst, device):
        i = self.count
        self.count += 1
        return pltpu.make_async_remote_copy(
            src_ref=src, dst_ref=dst, send_sem=self.send.at[i], recv_sem=self.recv.at[i],
            device_id=device, device_id_type=pl.DeviceIdType.MESH,
        )

    def go(self, src, dst, device):
        copy = self.plan(src, dst, device)
        copy.start()
        self.sent.append(copy)
        return copy

    def drain(self):
        for copy in self.sent:
            copy.wait_send()
        self.sent = []


def greet(devices):
    barrier = pltpu.get_barrier_semaphore()
    for device in devices:
        pl.semaphore_signal(barrier, inc=1, device_id=device, device_id_type=pl.DeviceIdType.MESH)


def await_greetings(devices):
    pl.semaphore_wait(pltpu.get_barrier_semaphore(), len(devices))


def column(member):
    return pl.ds(pl.multiple_of(member * BLK, BLK), BLK)


class Gather:
    def __init__(self, place, mover, full, cut):
        self.p, self.m, self.full, self.s = place, mover, full, cut
        self.need = {}

    def at(self, span, dy, zr):
        return self.full.at[rows_of(span), column(self.p.member(dy, zr, 0))]

    def pass_on(self, span, dy, zr, targets):
        place = self.p
        ref = self.at(span, dy, zr)
        out = []
        for step in targets:
            device = {"r": place.near(1, 0, 0), "l": place.near(-1, 0, 0),
                      "z": place.near(0, 1, 0), "c": place.near(0, 0, 1)}[step]
            copy = self.m.go(ref, ref, device)
            if step == "c":
                self.need.setdefault((dy % 4, zr), []).append(copy)
            else:
                out.append(copy)
        return out

    def start_a(self):
        self.a = self.pass_on(self.s.ALLA, 0, 0, "rlzc")

    def start_b(self):
        self.b = self.pass_on(self.s.ALLB, 0, 0, "zrlc")

    def first(self):
        ar, al, az = self.a
        bz, br, bl = self.b
        bz.wait_recv()
        self.zb = self.pass_on(self.s.ALLB, 0, 1, "rlc")
        ar.wait_recv()
        self.al1 = self.pass_on(self.s.LOA, -1, 0, "r") + self.pass_on(self.s.ALLA, -1, 0, "zc")
        al.wait_recv()
        self.ar1 = self.pass_on(self.s.HIA, 1, 0, "l") + self.pass_on(self.s.ALLA, 1, 0, "zc")
        br.wait_recv()
        self.bl1 = self.pass_on(self.s.LOB, -1, 0, "r") + self.pass_on(self.s.ALLB, -1, 0, "c")
        bl.wait_recv()
        self.br1 = self.pass_on(self.s.HIB, 1, 0, "l") + self.pass_on(self.s.ALLB, 1, 0, "c")
        az.wait_recv()
        self.pass_on(self.s.ALLA, 0, 1, "c")

    def second(self):
        lo, az = self.al1
        hi, az2 = self.ar1
        lo.wait_recv()
        self.o1 = self.pass_on(self.s.LOA, -2, 0, "zc")
        hi.wait_recv()
        self.o2 = self.pass_on(self.s.HIA, 2, 0, "zc")
        zr, zl = self.zb
        zr.wait_recv()
        self.zlo = self.pass_on(self.s.LOB, -1, 1, "r") + self.pass_on(self.s.ALLB, -1, 1, "c")
        zl.wait_recv()
        self.zhi = self.pass_on(self.s.HIB, 1, 1, "l") + self.pass_on(self.s.ALLB, 1, 1, "c")
        az.wait_recv()
        self.pass_on(self.s.ALLA, -1, 1, "c")
        az2.wait_recv()
        self.pass_on(self.s.ALLA, 1, 1, "c")

    def third(self):
        self.bl1[0].wait_recv()
        self.pass_on(self.s.LOB, -2, 0, "c")
        self.br1[0].wait_recv()
        self.pass_on(self.s.HIB, 2, 0, "c")
        self.o1[0].wait_recv()
        self.pass_on(self.s.LOA, -2, 1, "c")
        self.o2[0].wait_recv()
        self.pass_on(self.s.HIA, 2, 1, "c")
        self.zlo[0].wait_recv()
        self.pass_on(self.s.LOB, -2, 1, "c")
        self.zhi[0].wait_recv()
        self.pass_on(self.s.HIB, 2, 1, "c")

    def ready(self, dy, zr):
        for copy in self.need.pop((dy % 4, zr), ()):
            copy.wait_recv()

    def finish(self):
        for key in list(self.need):
            self.ready(*key)


GATHER_COPIES = 38


class Handout:
    def __init__(self, place, mover, refs, out, quarter, whole, pack, mate, local):
        self.p, self.m, self.refs, self.out = place, mover, refs, out
        self.quarter, self.whole, self.pack, self.mate, self.local = quarter, whole, pack, mate, local
        self.rel = [(dy, zr, cc) for dy, zr in REST for cc in (0, 1)]
        self.cols = out.shape[1]

    def load(self):
        place = self.p
        part = pl.ds(pl.multiple_of(place.x * 32, 32), 32)
        self.loads, at = [], 0
        for ref in self.refs:
            self.one(ref.at[part, :], self.quarter.at[:, pl.ds(at, ref.shape[1])])
            at += ref.shape[1]
        for zr in (0, 1):
            chip = place.member(0, zr, 0) // 2
            at = 0
            for ref in self.refs:
                wide = ref.shape[1] // 8
                self.one(ref.at[:, pl.ds(pl.multiple_of(chip * wide, 128), wide)], self.whole.at[zr, :, pl.ds(at, wide)])
                at += wide

    def one(self, src, dst):
        copy = pltpu.make_async_copy(src, dst, self.local.at[len(self.loads)])
        copy.start()
        self.loads.append(copy)

    def lot(self, member, slot, low=0, high=32):
        return pl.ds(pl.multiple_of(member * 128 + slot * 32 + low, 16), high - low)

    def prepare(self):
        for copy in self.loads[:len(self.refs)]:
            copy.wait()
        for d in range(16):
            for i in range(self.cols // 256):
                self.pack[d, :, i * 256:(i + 1) * 256] = self.quarter[:, i * 4096 + self.spot(d, i):][:, :256].astype(bf16)

    def prepare_whole(self):
        place = self.p
        for copy in self.loads[len(self.refs):]:
            copy.wait()
        rows = pl.ds(pl.multiple_of(place.me * 128, 128), 128)
        for i in range(self.cols // 256):
            mine = self.whole[0, :, pl.ds(pl.multiple_of(i * 512 + place.c * 256, 128), 256)]
            self.out[rows, i * 256:(i + 1) * 256] = mine.astype(bf16)
        for at, (dy, zr, cc) in enumerate(DIRECT):
            core = (place.c + cc) % 2
            for i in range(self.cols // 256):
                other = self.whole[zr, :, pl.ds(pl.multiple_of(i * 512 + core * 256, 128), 256)]
                self.mate[at, :, i * 256:(i + 1) * 256] = other.astype(bf16)

    def share(self):
        place = self.p
        self.first = [
            self.m.go(self.pack.at[place.member(*r)], self.out.at[self.lot(place.me, place.x), :], place.near(*r))
            for r in self.rel
        ]

    def spot(self, d, i):
        if i == 0 and len(self.refs) * 256 > self.cols:
            return (d % 2) * 2048 + (d // 2) * 256
        return d * 256

    def share_whole(self):
        place = self.p
        rows = pl.ds(pl.multiple_of(place.me * 128, 128), 128)
        self.whole_sent = [
            self.m.go(self.mate.at[at], self.out.at[rows, :], place.beside(zr, cc))
            for at, (dy, zr, cc) in enumerate(DIRECT)
        ]

    def origin(self, r):
        return self.p.member(-r[0], r[1], r[2])

    def spread(self, which):
        place = self.p
        got = []
        for i in which:
            self.first[i].wait_recv()
            ref = self.out.at[self.lot(self.origin(self.rel[i]), place.x), :]
            got.append((i, self.m.go(ref, ref, place.across(1)), self.m.go(ref, ref, place.across(-1))))
        return got

    def onward(self, got):
        place = self.p
        halves = []
        for i, right, left in got:
            origin = self.origin(self.rel[i])
            right.wait_recv()
            ref = self.out.at[self.lot(origin, (place.x + 3) % 4, 0, 16), :]
            halves.append(self.m.go(ref, ref, place.across(1)))
            left.wait_recv()
            ref = self.out.at[self.lot(origin, (place.x + 1) % 4, 16, 32), :]
            halves.append(self.m.go(ref, ref, place.across(-1)))
        return halves


HANDOUT_COPIES = 12 * 5 + 3


def group_peers(place):
    return [place.near(dy, zr, cc) for dy, zr in REST for cc in (0, 1)] + [place.near(*r) for r in DIRECT] + [
        place.beside(1, 0), place.beside(1, 1)]


def await_all(copies):
    for copy in copies:
        copy.wait_recv()


class DirectGather:
    def __init__(self, place, mover, full, cut):
        self.p, self.m, self.full, self.s = place, mover, full, cut
        self.cores = []

    def send(self, span, dy, zr, device):
        ref = self.full.at[rows_of(span), column(self.p.member(dy, zr, 0))]
        return self.m.go(ref, ref, device)

    def share(self, span, dy, zr):
        self.cores.append(self.send(span, dy, zr, self.p.near(0, 0, 1)))

    def ring(self, span, zr):
        return {dy: self.send(span, 0, zr, self.p.near(dy, 0, 0)) for dy in (2, 1, 3)}

    def start_a(self):
        self.a = self.ring(self.s.ALLA, 0)
        self.za = {0: self.send(self.s.ALLA, 0, 0, self.p.near(0, 1, 0))}
        self.share(self.s.ALLA, 0, 0)

    def start_b(self):
        self.zb = self.send(self.s.ALLB, 0, 0, self.p.near(0, 1, 0))
        self.b0 = self.ring(self.s.ALLB, 0)
        self.share(self.s.ALLB, 0, 0)

    def near_side(self):
        s = self.s
        self.zb.wait_recv()
        self.b1 = self.ring(s.ALLB, 1)
        late = len(self.cores)
        self.share(s.ALLB, 0, 1)
        for dy in (1, 3, 2):
            self.a[dy].wait_recv()
            self.za[dy] = self.send(s.ALLA, -dy, 0, self.p.near(0, 1, 0))
            self.share(s.ALLA, -dy, 0)
        for dy in (1, 3, 2):
            self.b0[dy].wait_recv()
            self.share(s.ALLB, -dy, 0)
        later = self.cores[late:late + 1]
        for copy in self.cores[:late] + self.cores[late + 1:]:
            copy.wait_recv()
        self.cores = later

    def far_side(self):
        s = self.s
        self.za[0].wait_recv()
        self.share(s.ALLA, 0, 1)
        for dy in (1, 3, 2):
            self.b1[dy].wait_recv()
            self.share(s.ALLB, -dy, 1)
            self.za[dy].wait_recv()
            self.share(s.ALLA, -dy, 1)
        await_all(self.cores)


DIRECT_COPIES = 30


class Scatter:
    def __init__(self, place, mover, wide, wpar, bufs):
        self.p, self.m, self.wide, self.wpar = place, mover, wide, wpar
        self.S, self.RA, self.RY, self.RZ = bufs
        self.over = place.near(0, 1, 0)

    def multiply(self, span, zr):
        rows = rows_of(span)
        for i in (2 * zr + 1, 2 * zr):
            part = jnp.dot(self.wide[rows, :], self.wpar[:, i * 256:(i + 1) * 256], preferred_element_type=f32)
            part = part.astype(bf16)
            self.S[2 * i, rows, :] = part[:, :128]
            self.S[2 * i + 1, rows, :] = part[:, 128:]

    def ring(self, span, zr, dy):
        rows = rows_of(span)
        return self.m.go(self.S.at[zr * 4 + dy, rows, :], self.RY.at[zr, dy, rows, :], self.p.near(dy, 0, 0))

    def total(self, span, zr, *others):
        rows = rows_of(span)
        total = self.S[zr * 4, rows, :].astype(f32)
        for dy in (1, 3, 2):
            total = total + self.RY[zr, dy, rows, :].astype(f32)
        for other in others:
            total = total + other[rows, :].astype(f32)
        return total

    def start_a(self):
        rows = rows_of(DEAL_CUT.ALLA)
        self.za = {dy: self.m.go(self.S.at[4 + dy, rows, :], self.RA.at[dy, rows, :], self.over)
                   for dy in (2, 1, 3, 0)}

    def start_b(self, zr):
        self.b[zr] = [self.ring(DEAL_CUT.ALLB, zr, dy) for dy in (2, 1, 3)]

    def start(self, sent):
        self.b = {}
        sent[0].wait_recv()
        self.multiply(DEAL_CUT.ALLA, 1)
        self.start_a()
        sent[1].wait_recv()
        self.multiply(DEAL_CUT.ALLB, 1)
        self.start_b(1)
        self.multiply(DEAL_CUT.ALLB, 0)
        self.start_b(0)
        self.multiply(DEAL_CUT.ALLA, 0)

    def middle(self):
        rows = rows_of(DEAL_CUT.ALLA)
        self.a = []
        for dy in (2, 1, 3):
            self.za[dy].wait_recv()
            total = self.S[dy, rows, :].astype(f32) + self.RA[dy, rows, :].astype(f32)
            self.S[dy, rows, :] = total.astype(bf16)
            self.a.append(self.ring(DEAL_CUT.ALLA, 0, dy))
        await_all(self.b[1])
        rows = rows_of(DEAL_CUT.ALLB)
        self.S[4, rows, :] = self.total(DEAL_CUT.ALLB, 1).astype(bf16)
        self.zb = self.m.go(self.S.at[4, rows, :], self.RZ.at[rows, :], self.over)

    def total_a(self):
        await_all([self.za[0]] + self.a)
        return self.total(DEAL_CUT.ALLA, 0, self.RA.at[0])

    def total_b(self):
        await_all(self.b[0] + [self.zb])
        return self.total(DEAL_CUT.ALLB, 0, self.RZ)


SCATTER_COPIES = 4 + 6 + 3 + 1
OTHERS = [(dx, dz) for dx in (2, 1, 3, 0) for dz in (1, 0) if (dx, dz) != (0, 0)]


def layer_kernel(lengths, gain1, gain2, tokens, token_lots_in, query, key, value, gate, out_weight, swish, up,
                 down_weight, out,
                 full1, squares, first, acc, qk, vg, retained, memory, decay, stats, gated,
                 quarter1, whole1, pack1, mate1, quarter2, whole2, pack2, mate2, second,
                 stage, wpar, wmate, lots, token_lots, pick, unpick, base, wide, full2, acc2, squares2, result, spare,
                 S1, RA1, RY1, RZ1, S2, RA2, RY2, RZ2,
                 local1, local2, load_sem, send, recv):
    place = Place()
    mover = Mover(send, recv)
    req = place.req
    cut = DEAL_CUT
    hand1 = Handout(place, mover, (query, key, value, gate), first, quarter1, whole1, pack1, mate1, local1)
    hand2 = Handout(place, mover, (swish, up), second, quarter2, whole2, pack2, mate2, local2)
    mine = column(place.me)

    def group(dx, dz):
        return ((place.x + dx + 4) % 4) * 2 + (place.zh + dz) % 2

    peers = group_peers(place) + [(group(dx, dz), place.me) for dx, dz in OTHERS]
    greet(peers)
    hand1.load()
    loads = [pltpu.make_async_copy(tokens, full1.at[:, mine], load_sem.at[0]),
             pltpu.make_async_copy(out_weight, stage.at[0], load_sem.at[1]),
             pltpu.make_async_copy(down_weight, stage.at[1], load_sem.at[2]),
             pltpu.make_async_copy(token_lots_in.at[:, 0], token_lots.at[req], load_sem.at[3])]
    for copy in loads:
        copy.start()
    hand2.load()
    mate_core = place.near(0, 0, 1)
    hand1.prepare()
    await_greetings(peers)
    hand1.share()
    loads[0].wait()
    gather = Gather(place, mover, full1, WIDE_CUT)
    hand1.prepare_whole()
    hand1.share_whole()

    head = place.me // 2
    log_decay, span_decay = jnp.float32(0.0), jnp.float32(0.0)
    for h in range(H):
        rate = 1.0 - 2.0 ** (-5 - h)
        log_decay = jnp.where(head == h, jnp.float32(math.log(rate)), log_decay)
        span_decay = jnp.where(head == h, jnp.float32(rate ** SPAN), span_decay)
    i = lax.broadcasted_iota(jnp.int32, (SPAN, SPAN), 0)
    j = lax.broadcasted_iota(jnp.int32, (SPAN, SPAN), 1)
    decay[0] = jnp.where(i >= j, jnp.exp((i - j).astype(f32) * log_decay), 0.0)
    decay[1] = jnp.exp((i + 1).astype(f32) * log_decay)
    decay[2] = jnp.exp((SPAN - 1 - i).astype(f32) * log_decay)

    order = [(dy, zr) for zr in (0, 1) for dy in range(4)]

    def set_weight(which):
        loads[1 + which].wait()
        for i, (dy, zr) in enumerate(order):
            wpar[which, 0:256, i * 128:(i + 1) * 128] = stage[which, :, column(place.member(dy, zr, 0))].astype(bf16)
            wmate[which, :, i * 128:(i + 1) * 128] = stage[which, :, column(place.member(dy, zr, 1))].astype(bf16)
        return mover.go(wmate.at[which], wpar.at[which, pl.ds(256, 256), :], mate_core)

    starts, counts = [], []
    start = jnp.int32(0)
    for r in range(8):
        length = lengths[r]
        turn = (req - r + 8) % 8
        count = 16 * (length // 128) + jnp.clip(length % 128 - 16 * turn, 0, 16)
        starts.append(start)
        counts.append(count)
        start = start + count

    def select():
        row = lax.broadcasted_iota(jnp.int32, (DEAL, 128), 0)
        lane = lax.broadcasted_iota(jnp.int32, (DEAL, 128), 1)
        slot = lax.broadcasted_iota(jnp.int32, (128, DEAL), 0)
        at = lax.broadcasted_iota(jnp.int32, (128, DEAL), 1)
        for r in range(8):
            chosen = (lane == row - starts[r]) & (lane < counts[r])
            pick[:, r * 128:(r + 1) * 128] = jnp.where(chosen, 1.0, 0.0).astype(bf16)
            chosen = (at == slot + starts[r]) & (slot < counts[r])
            unpick[r] = jnp.where(chosen, 1.0, 0.0).astype(bf16)

    def gained(rows, chips):
        total, square = None, None
        for chip in chips:
            depth = pl.ds(pl.multiple_of(chip * 256, 256), 256)
            values = full1[rows, depth].astype(f32)
            part = jnp.dot((values * gain1[:, depth]).astype(bf16), first[depth, :], preferred_element_type=f32)
            values = values * values
            values = values[:, :128] + values[:, 128:]
            total = part if total is None else total + part
            square = values if square is None else square + values
        return total, square

    def gather_product(rels, fresh=False):
        chips = [place.member(-dy, zr, 0) // 2 for dy, zr in rels]
        for dy, zr in rels:
            gather.ready(-dy, zr)

        def step(i, carry):
            rows = pl.ds(pl.multiple_of(i * SPAN, SPAN), SPAN)
            part, square = gained(rows, chips)
            acc[rows, :] = part if fresh else acc[rows, :] + part
            squares[rows, :] = square if fresh else squares[rows, :] + square
            return carry

        lax.fori_loop(0, LMAX // SPAN, step, 0)

    got1 = hand1.spread(range(4))
    gather.start_a()
    gather.start_b()
    hand2.prepare()
    got1 += hand1.spread(range(4, 12))
    hand2.prepare_whole()
    weights = [set_weight(0)]
    gather.first()
    halves1 = hand1.onward(got1[:4])
    await_all(hand1.whole_sent[:1])
    gather_product([(0, 0)], True)
    gather.second()
    halves1 += hand1.onward(got1[4:8])
    await_all(hand1.whole_sent[1:])
    gather_product([(0, 1)])
    gather.third()
    halves1 += hand1.onward(got1[8:])
    hand2.share()
    hand2.share_whole()
    await_all(halves1[:8])
    gather_product([(1, 0), (3, 0)])
    await_all(halves1[8:16])
    gather_product([(1, 1), (3, 1)])
    await_all(halves1[16:20])
    gather_product([(2, 0)])
    gather.finish()
    await_all(halves1[20:])
    dealt_tokens = []
    for dx, dz in OTHERS:
        target = group(dx, dz)
        turn = (target - req + 8) % 8
        dealt_tokens.append(mover.go(token_lots_in.at[:, turn], token_lots.at[req], (target, place.me)))
    last_chip = [place.member(-2, 1, 0) // 2]
    key_scale = jnp.where(place.c == 0, 1.0, DK ** (-0.5))
    swapped = []

    def project(b):
        rows = pl.ds(b * SPAN, SPAN)
        total, square = gained(rows, last_chip)
        square = jnp.sum(squares[rows, :] + square, axis=1, keepdims=True)
        total = (acc[rows, :] + total) * lax.rsqrt(square * (1.0 / 2048) + epsilon)
        qk[place.c, rows, :] = (total[:, :256] * key_scale).astype(bf16)
        ref = qk.at[place.c, rows, :]
        swapped.append(mover.go(ref, ref, mate_core))
        vg[0, rows, :] = total[:, 256:512].astype(bf16)
        vg[1, rows, :] = total[:, 512:].astype(bf16)

    def attend(b):
        rows = pl.ds(b * SPAN, SPAN)
        swapped[b].wait_recv()
        query_block, key_block, value_block = qk[0, rows, :], qk[1, rows, :], vg[0, rows, :]
        scores = lax.dot_general(query_block, key_block, (((1,), (1,)), ((), ())), preferred_element_type=f32)
        total = jnp.dot((scores * decay[0]).astype(bf16), value_block, preferred_element_type=f32)
        if b > 0:
            across = jnp.dot(query_block, memory[...].astype(bf16), preferred_element_type=f32)
            total = total + across * decay[1]
        retained[rows, :] = total
        mean = jnp.sum(total, axis=1, keepdims=True) * (1.0 / 256)
        spread = total - mean
        square = jnp.sum(spread * spread, axis=1, keepdims=True)
        lanes = lax.broadcasted_iota(jnp.int32, (SPAN, 128), 1)
        stats[0, b] = jnp.where(lanes < 64, mean, square)
        told = mover.go(stats.at[0, b], stats.at[1, b], mate_core)
        if b < 3:
            decayed = (key_block.astype(f32) * decay[2]).astype(bf16)
            update = lax.dot_general(decayed, value_block, (((0,), (0,)), ((), ())), preferred_element_type=f32)
            memory[...] = update if b == 0 else memory[...] * span_decay + update
        return told

    def finish(b, told):
        rows = pl.ds(b * SPAN, SPAN)
        told.wait_recv()
        mean, square = stats[0, b, :, 0:1], stats[0, b, :, 64:65]
        mean2, square2 = stats[1, b, :, 0:1], stats[1, b, :, 64:65]
        gap = (mean - mean2) * 0.5
        middle = (mean + mean2) * 0.5
        var = (square + square2) * (1.0 / DV) + gap * gap
        grouped = (retained[rows, :] - middle) * lax.rsqrt(var + epsilon)
        gates = vg[1, rows, :].astype(f32)
        done = (gates / (1.0 + jnp.exp(-gates)) * grouped).astype(bf16)
        gated[2 * b:2 * b + 2] = done.reshape(2, 8, 16, 256)
        two = pl.ds(2 * b, 2)
        sent = []
        for dx, dz in OTHERS:
            target = group(dx, dz)
            turn = (target - req + 8) % 8
            sent.append(mover.go(gated.at[two, turn], lots.at[req, two], (target, place.me)))
        lots[req, 2 * b:2 * b + 2] = gated[2 * b:2 * b + 2, 0]
        return sent

    dealt, told = [], []
    project(0)
    for b in range(4):
        if b < 3:
            project(b + 1)
            if b == 0:
                got2 = hand2.spread(range(4))
        told.append(attend(b))
        if b > 0:
            dealt += finish(b - 1, told[b - 1])
    dealt += finish(3, told[3])
    loads[3].wait()
    select()
    await_all(dealt)
    got2 += hand2.spread(range(4, 12))
    sent = []
    for span in (cut.ALLA, cut.ALLB):
        rows = rows_of(span)
        part = jnp.dot(pick[rows, :], lots[...].reshape(LMAX, 256), preferred_element_type=f32)
        wide[0, rows, 0:256] = part.astype(bf16)
        ref = wide.at[0, rows, pl.ds(0, 256)]
        sent.append(mover.go(ref, wide.at[0, rows, pl.ds(256, 256)], mate_core))

    scatter = Scatter(place, mover, wide.at[0], wpar.at[0], (S1, RA1, RY1, RZ1))
    weights[0].wait_recv()
    scatter.start(sent)
    weights.append(set_weight(1))
    await_all(dealt_tokens)
    base[...] = jnp.dot(pick[...], token_lots[...].reshape(LMAX, BLK), preferred_element_type=f32).astype(bf16)
    scatter.middle()
    halves2 = hand2.onward(got2)
    gather = DirectGather(place, mover, full2, cut)
    full2[rows_of(cut.ALLA), mine] = (base[rows_of(cut.ALLA), :].astype(f32) + scatter.total_a()).astype(bf16)
    gather.start_a()
    full2[rows_of(cut.ALLB), mine] = (base[rows_of(cut.ALLB), :].astype(f32) + scatter.total_b()).astype(bf16)
    gather.start_b()

    def forward(rows, zr):
        total, square = None, None
        for dy in range(4):
            depth = pl.ds(pl.multiple_of(place.member(dy, zr, 0) // 2 * 256, 256), 256)
            values = full2[rows, depth].astype(f32)
            part = jnp.dot((values * gain2[:, depth]).astype(bf16), second[depth, :], preferred_element_type=f32)
            values = values * values
            values = values[:, :128] + values[:, 128:]
            total = part if total is None else total + part
            square = values if square is None else square + values
        return total, square

    gather.near_side()
    await_all(halves2 + hand2.whole_sent)
    for span in (cut.ALLA, cut.ALLB):
        rows = rows_of(span)
        acc2[rows, :], squares2[rows, :] = forward(rows, 0)
    gather.far_side()
    sent = []
    for span in (cut.ALLA, cut.ALLB):
        rows = rows_of(span)
        part, square = forward(rows, 1)
        square = jnp.sum(squares2[rows, :] + square, axis=1, keepdims=True)
        part = (acc2[rows, :] + part) * lax.rsqrt(square * (1.0 / 2048) + epsilon)
        swished = part[:, :256]
        wide[1, rows, 0:256] = (swished / (1.0 + jnp.exp(-swished)) * part[:, 256:]).astype(bf16)
        ref = wide.at[1, rows, pl.ds(0, 256)]
        sent.append(mover.go(ref, wide.at[1, rows, pl.ds(256, 256)], mate_core))
    scatter = Scatter(place, mover, wide.at[1], wpar.at[1], (S2, RA2, RY2, RZ2))
    weights[1].wait_recv()
    scatter.start(sent)
    scatter.middle()
    for span, total in ((cut.ALLA, scatter.total_a), (cut.ALLB, scatter.total_b)):
        rows = rows_of(span)
        result[rows, :] = (full2[rows, mine].astype(f32) + total()).astype(bf16)
    returned = []
    for dx, dz in OTHERS:
        target = group(dx, dz)
        back = jnp.dot(unpick[target], result[...], preferred_element_type=f32)
        spare[target] = back.astype(bf16).reshape(8, 16, BLK)
        returned.append(mover.go(spare.at[target], out.at[:, (req - target + 8) % 8], (target, place.me)))
    back = jnp.dot(unpick[req], result[...], preferred_element_type=f32)
    out[:, 0] = back.astype(bf16).reshape(8, 16, BLK)
    await_all(returned)
    mover.drain()


LAYER_COPIES = 2 * HANDOUT_COPIES + GATHER_COPIES + DIRECT_COPIES + 2 * SCATTER_COPIES + 7 * 6 + 2 + 4 + 4 + 4


def layer(*operands):
    vmem = pl.BlockSpec(memory_space=pltpu.VMEM)
    hbm = pl.BlockSpec(memory_space=pl.ANY)
    sums = [
        pltpu.VMEM((8, DEAL, BLK), bf16),
        pltpu.VMEM((4, DEAL, BLK), bf16),
        pltpu.VMEM((2, 4, DEAL, BLK), bf16),
        pltpu.VMEM((DEAL, BLK), bf16),
    ]
    return pl.pallas_call(
        layer_kernel,
        name="layer",
        out_shape=jax.ShapeDtypeStruct((8, 8, 16, BLK), bf16),
        in_specs=[pl.BlockSpec(memory_space=pltpu.SMEM), vmem, vmem] + [hbm] * 10,
        out_specs=vmem,
        scratch_shapes=[
            pltpu.VMEM((LMAX, 2048), bf16),
            pltpu.VMEM((LMAX, 128), f32),
            pltpu.VMEM((2048, 768), bf16),
            pltpu.VMEM((LMAX, 768), f32),
            pltpu.VMEM((2, LMAX, 256), bf16),
            pltpu.VMEM((2, LMAX, 256), bf16),

            pltpu.VMEM((LMAX, 256), f32),
            pltpu.VMEM((256, 256), f32),
            pltpu.VMEM((3, SPAN, SPAN), f32),
            pltpu.VMEM((2, 4, SPAN, 128), f32),
            pltpu.VMEM((8, 8, 16, 256), bf16),
            pltpu.VMEM((32, 12288), f32),
            pltpu.VMEM((2, 128, 1536), f32),
            pltpu.VMEM((16, 32, 768), bf16),
            pltpu.VMEM((3, 128, 768), bf16),
            pltpu.VMEM((32, 8192), f32),
            pltpu.VMEM((2, 128, 1024), f32),
            pltpu.VMEM((16, 32, 512), bf16),
            pltpu.VMEM((3, 128, 512), bf16),
            pltpu.VMEM((2048, 512), bf16),
            pltpu.VMEM((2, 256, 2048), f32),
            pltpu.VMEM((2, 512, 1024), bf16),
            pltpu.VMEM((2, 256, 1024), bf16),
            pltpu.VMEM((8, 8, 16, 256), bf16),
            pltpu.VMEM((8, 8, 16, BLK), bf16),
            pltpu.VMEM((DEAL, LMAX), bf16),
            pltpu.VMEM((8, 128, DEAL), bf16),
            pltpu.VMEM((DEAL, BLK), bf16),
            pltpu.VMEM((2, DEAL, 512), bf16),
            pltpu.VMEM((DEAL, 2048), bf16),
            pltpu.VMEM((DEAL, 512), f32),
            pltpu.VMEM((DEAL, 128), f32),
            pltpu.VMEM((DEAL, BLK), bf16),
            pltpu.VMEM((8, 8, 16, BLK), bf16),
        ] + sums + sums + [
            pltpu.SemaphoreType.DMA((12,)),
            pltpu.SemaphoreType.DMA((6,)),
            pltpu.SemaphoreType.DMA((4,)),
            pltpu.SemaphoreType.DMA((LAYER_COPIES,)),
            pltpu.SemaphoreType.DMA((LAYER_COPIES,)),
        ],
        compiler_params=pltpu.CompilerParams(
            collective_id=0, has_side_effects=True, vmem_limit_bytes=63 * 2**20
        ),
    )(*operands)


def body(
    tokens,
    lengths,
    retention_gain,
    forward_gain,
    query_weight,
    key_weight,
    value_weight,
    gate_weight,
    output_weight,
    swish_weight,
    up_weight,
    down_weight,
):
    rows = tokens.reshape(8, 8, 16, BLK)
    finished = layer(
        lengths, retention_gain.reshape(1, 2048), forward_gain.reshape(1, 2048), tokens[0], rows,
        query_weight, key_weight, value_weight, gate_weight, output_weight, swish_weight, up_weight, down_weight
    )
    return finished.reshape(1, LMAX, BLK)


def solution(mesh):
    placed = (
        P("req", None, "mlp"),
        P(),
        P(),
        P(),
        P("mlp", None),
        P("mlp", None),
        P("mlp", None),
        P("mlp", None),
        P("mlp", None),
        P("mlp", None),
        P("mlp", None),
        P("mlp", None),
    )
    return jax.shard_map(
        body, mesh=mesh, in_specs=placed, out_specs=P("req", None, "mlp"), check_vma=False
    )
```

```python
import math
import jax
import jax.numpy as jnp
from jax import lax
from jax.experimental import pallas as pl
from jax.experimental.pallas import tpu as pltpu
from jax.sharding import PartitionSpec as P

H = 8
DK = 256
DV = 512
SPAN = 256
LMAX = 1024
BLK = 128
REST = [(1, 0), (3, 0), (1, 1), (3, 1), (2, 0), (2, 1)]
DIRECT = [(0, 0, 1), (0, 1, 0), (0, 1, 1)]

epsilon = 1e-05
bf16 = jnp.bfloat16
f32 = jnp.float32


class Cut:
    def __init__(self, rows, cut):
        half, rest = cut // 2, (rows + cut) // 2
        self.ALLA, self.LOA, self.HIA = (0, cut), (0, half), (half, cut)
        self.ALLB, self.LOB, self.HIB = (cut, rows), (cut, rest), (rest, rows)


WIDE_CUT = Cut(1024, 512)
DEAL = 448
DEAL_CUT = Cut(DEAL, 256)


def rows_of(span):
    return pl.ds(span[0], span[1] - span[0])


class Place:
    def __init__(self):
        self.req = lax.axis_index("req")
        self.me = lax.axis_index("mlp")
        self.x = self.req // 2
        self.zh = self.req % 2
        self.y = self.me // 4
        self.z = (self.me // 2) % 2
        self.c = self.me % 2

    def member(self, dy, zr, cc):
        return ((self.y + dy + 4) % 4) * 4 + ((self.z + zr) % 2) * 2 + (self.c + cc) % 2

    def near(self, dy, zr, cc):
        return (self.req, self.member(dy, zr, cc))

    def beside(self, zr, cc):
        return (self.x * 2 + (self.zh + zr) % 2, self.member(0, zr, cc))

    def across(self, dx):
        return (((self.x + dx + 4) % 4) * 2 + self.zh, self.me)


class Mover:
    def __init__(self, send, recv):
        self.send, self.recv, self.count, self.sent = send, recv, 0, []

    def plan(self, src, dst, device):
        i = self.count
        self.count += 1
        return pltpu.make_async_remote_copy(
            src_ref=src, dst_ref=dst, send_sem=self.send.at[i], recv_sem=self.recv.at[i],
            device_id=device, device_id_type=pl.DeviceIdType.MESH,
        )

    def go(self, src, dst, device):
        copy = self.plan(src, dst, device)
        copy.start()
        self.sent.append(copy)
        return copy

    def drain(self):
        for copy in self.sent:
            copy.wait_send()
        self.sent = []


def greet(devices):
    barrier = pltpu.get_barrier_semaphore()
    for device in devices:
        pl.semaphore_signal(barrier, inc=1, device_id=device, device_id_type=pl.DeviceIdType.MESH)


def await_greetings(devices):
    pl.semaphore_wait(pltpu.get_barrier_semaphore(), len(devices))


def column(member):
    return pl.ds(pl.multiple_of(member * BLK, BLK), BLK)


class Gather:
    def __init__(self, place, mover, full, cut):
        self.p, self.m, self.full, self.s = place, mover, full, cut
        self.need = {}

    def at(self, span, dy, zr):
        return self.full.at[rows_of(span), column(self.p.member(dy, zr, 0))]

    def pass_on(self, span, dy, zr, targets):
        place = self.p
        ref = self.at(span, dy, zr)
        out = []
        for step in targets:
            device = {"r": place.near(1, 0, 0), "l": place.near(-1, 0, 0),
                      "z": place.near(0, 1, 0), "c": place.near(0, 0, 1)}[step]
            copy = self.m.go(ref, ref, device)
            if step == "c":
                self.need.setdefault((dy % 4, zr), []).append(copy)
            else:
                out.append(copy)
        return out

    def start_a(self):
        self.a = self.pass_on(self.s.ALLA, 0, 0, "rlzc")

    def start_b(self):
        self.b = self.pass_on(self.s.ALLB, 0, 0, "zrlc")

    def first(self):
        ar, al, az = self.a
        bz, br, bl = self.b
        bz.wait_recv()
        self.zb = self.pass_on(self.s.ALLB, 0, 1, "rlc")
        ar.wait_recv()
        self.al1 = self.pass_on(self.s.LOA, -1, 0, "r") + self.pass_on(self.s.ALLA, -1, 0, "zc")
        al.wait_recv()
        self.ar1 = self.pass_on(self.s.HIA, 1, 0, "l") + self.pass_on(self.s.ALLA, 1, 0, "zc")
        br.wait_recv()
        self.bl1 = self.pass_on(self.s.LOB, -1, 0, "r") + self.pass_on(self.s.ALLB, -1, 0, "c")
        bl.wait_recv()
        self.br1 = self.pass_on(self.s.HIB, 1, 0, "l") + self.pass_on(self.s.ALLB, 1, 0, "c")
        az.wait_recv()
        self.pass_on(self.s.ALLA, 0, 1, "c")

    def second(self):
        lo, az = self.al1
        hi, az2 = self.ar1
        lo.wait_recv()
        self.o1 = self.pass_on(self.s.LOA, -2, 0, "zc")
        hi.wait_recv()
        self.o2 = self.pass_on(self.s.HIA, 2, 0, "zc")
        zr, zl = self.zb
        zr.wait_recv()
        self.zlo = self.pass_on(self.s.LOB, -1, 1, "r") + self.pass_on(self.s.ALLB, -1, 1, "c")
        zl.wait_recv()
        self.zhi = self.pass_on(self.s.HIB, 1, 1, "l") + self.pass_on(self.s.ALLB, 1, 1, "c")
        az.wait_recv()
        self.pass_on(self.s.ALLA, -1, 1, "c")
        az2.wait_recv()
        self.pass_on(self.s.ALLA, 1, 1, "c")

    def third(self):
        self.bl1[0].wait_recv()
        self.pass_on(self.s.LOB, -2, 0, "c")
        self.br1[0].wait_recv()
        self.pass_on(self.s.HIB, 2, 0, "c")
        self.o1[0].wait_recv()
        self.pass_on(self.s.LOA, -2, 1, "c")
        self.o2[0].wait_recv()
        self.pass_on(self.s.HIA, 2, 1, "c")
        self.zlo[0].wait_recv()
        self.pass_on(self.s.LOB, -2, 1, "c")
        self.zhi[0].wait_recv()
        self.pass_on(self.s.HIB, 2, 1, "c")

    def ready(self, dy, zr):
        for copy in self.need.pop((dy % 4, zr), ()):
            copy.wait_recv()

    def finish(self):
        for key in list(self.need):
            self.ready(*key)


GATHER_COPIES = 38


class Handout:
    def __init__(self, place, mover, refs, out, quarter, whole, pack, mate, local):
        self.p, self.m, self.refs, self.out = place, mover, refs, out
        self.quarter, self.whole, self.pack, self.mate, self.local = quarter, whole, pack, mate, local
        self.rel = [(dy, zr, cc) for dy, zr in REST for cc in (0, 1)]
        self.cols = out.shape[1]

    def load(self):
        place = self.p
        part = pl.ds(pl.multiple_of(place.x * 32, 32), 32)
        self.loads, at = [], 0
        for ref in self.refs:
            self.one(ref.at[part, :], self.quarter.at[:, pl.ds(at, ref.shape[1])])
            at += ref.shape[1]
        for zr in (0, 1):
            chip = place.member(0, zr, 0) // 2
            at = 0
            for ref in self.refs:
                wide = ref.shape[1] // 8
                self.one(ref.at[:, pl.ds(pl.multiple_of(chip * wide, 128), wide)], self.whole.at[zr, :, pl.ds(at, wide)])
                at += wide

    def one(self, src, dst):
        copy = pltpu.make_async_copy(src, dst, self.local.at[len(self.loads)])
        copy.start()
        self.loads.append(copy)

    def lot(self, member, slot, low=0, high=32):
        return pl.ds(pl.multiple_of(member * 128 + slot * 32 + low, 16), high - low)

    def prepare(self):
        for copy in self.loads[:len(self.refs)]:
            copy.wait()
        for d in range(16):
            for i in range(self.cols // 256):
                self.pack[d, :, i * 256:(i + 1) * 256] = self.quarter[:, i * 4096 + self.spot(d, i):][:, :256].astype(bf16)

    def prepare_whole(self):
        place = self.p
        for copy in self.loads[len(self.refs):]:
            copy.wait()
        rows = pl.ds(pl.multiple_of(place.me * 128, 128), 128)
        for i in range(self.cols // 256):
            mine = self.whole[0, :, pl.ds(pl.multiple_of(i * 512 + place.c * 256, 128), 256)]
            self.out[rows, i * 256:(i + 1) * 256] = mine.astype(bf16)
        for at, (dy, zr, cc) in enumerate(DIRECT):
            core = (place.c + cc) % 2
            for i in range(self.cols // 256):
                other = self.whole[zr, :, pl.ds(pl.multiple_of(i * 512 + core * 256, 128), 256)]
                self.mate[at, :, i * 256:(i + 1) * 256] = other.astype(bf16)

    def share(self):
        place = self.p
        self.first = [
            self.m.go(self.pack.at[place.member(*r)], self.out.at[self.lot(place.me, place.x), :], place.near(*r))
            for r in self.rel
        ]

    def spot(self, d, i):
        if i == 0 and len(self.refs) * 256 > self.cols:
            return (d % 2) * 2048 + (d // 2) * 256
        return d * 256

    def share_whole(self):
        place = self.p
        rows = pl.ds(pl.multiple_of(place.me * 128, 128), 128)
        self.whole_sent = [
            self.m.go(self.mate.at[at], self.out.at[rows, :], place.beside(zr, cc))
            for at, (dy, zr, cc) in enumerate(DIRECT)
        ]

    def origin(self, r):
        return self.p.member(-r[0], r[1], r[2])

    def spread(self, which):
        place = self.p
        got = []
        for i in which:
            self.first[i].wait_recv()
            ref = self.out.at[self.lot(self.origin(self.rel[i]), place.x), :]
            got.append((i, self.m.go(ref, ref, place.across(1)), self.m.go(ref, ref, place.across(-1))))
        return got

    def onward(self, got):
        place = self.p
        halves = []
        for i, right, left in got:
            origin = self.origin(self.rel[i])
            right.wait_recv()
            ref = self.out.at[self.lot(origin, (place.x + 3) % 4, 0, 16), :]
            halves.append(self.m.go(ref, ref, place.across(1)))
            left.wait_recv()
            ref = self.out.at[self.lot(origin, (place.x + 1) % 4, 16, 32), :]
            halves.append(self.m.go(ref, ref, place.across(-1)))
        return halves


HANDOUT_COPIES = 12 * 5 + 3


def group_peers(place):
    return [place.near(dy, zr, cc) for dy, zr in REST for cc in (0, 1)] + [place.near(*r) for r in DIRECT] + [
        place.beside(1, 0), place.beside(1, 1)]


def await_all(copies):
    for copy in copies:
        copy.wait_recv()


class DirectGather:
    def __init__(self, place, mover, full, cut):
        self.p, self.m, self.full, self.s = place, mover, full, cut
        self.cores = []

    def send(self, span, dy, zr, device):
        ref = self.full.at[rows_of(span), column(self.p.member(dy, zr, 0))]
        return self.m.go(ref, ref, device)

    def share(self, span, dy, zr):
        self.cores.append(self.send(span, dy, zr, self.p.near(0, 0, 1)))

    def ring(self, span, zr):
        return {dy: self.send(span, 0, zr, self.p.near(dy, 0, 0)) for dy in (2, 1, 3)}

    def start_a(self):
        self.a = self.ring(self.s.ALLA, 0)
        self.za = {0: self.send(self.s.ALLA, 0, 0, self.p.near(0, 1, 0))}
        self.share(self.s.ALLA, 0, 0)

    def start_b(self):
        self.zb = self.send(self.s.ALLB, 0, 0, self.p.near(0, 1, 0))
        self.b0 = self.ring(self.s.ALLB, 0)
        self.share(self.s.ALLB, 0, 0)

    def near_side(self):
        s = self.s
        self.zb.wait_recv()
        self.b1 = self.ring(s.ALLB, 1)
        late = len(self.cores)
        self.share(s.ALLB, 0, 1)
        for dy in (1, 3, 2):
            self.a[dy].wait_recv()
            self.za[dy] = self.send(s.ALLA, -dy, 0, self.p.near(0, 1, 0))
            self.share(s.ALLA, -dy, 0)
        for dy in (1, 3, 2):
            self.b0[dy].wait_recv()
            self.share(s.ALLB, -dy, 0)
        later = self.cores[late:late + 1]
        for copy in self.cores[:late] + self.cores[late + 1:]:
            copy.wait_recv()
        self.cores = later

    def far_side(self):
        s = self.s
        self.za[0].wait_recv()
        self.share(s.ALLA, 0, 1)
        for dy in (1, 3, 2):
            self.b1[dy].wait_recv()
            self.share(s.ALLB, -dy, 1)
            self.za[dy].wait_recv()
            self.share(s.ALLA, -dy, 1)
        await_all(self.cores)


DIRECT_COPIES = 30


class Scatter:
    def __init__(self, place, mover, wide, wpar, bufs):
        self.p, self.m, self.wide, self.wpar = place, mover, wide, wpar
        self.S, self.RA, self.RY, self.RZ = bufs
        self.over = place.near(0, 1, 0)

    def multiply(self, span, zr):
        rows = rows_of(span)
        for i in (2 * zr + 1, 2 * zr):
            part = jnp.dot(self.wide[rows, :], self.wpar[:, i * 256:(i + 1) * 256], preferred_element_type=f32)
            part = part.astype(bf16)
            self.S[2 * i, rows, :] = part[:, :128]
            self.S[2 * i + 1, rows, :] = part[:, 128:]

    def ring(self, span, zr, dy):
        rows = rows_of(span)
        return self.m.go(self.S.at[zr * 4 + dy, rows, :], self.RY.at[zr, dy, rows, :], self.p.near(dy, 0, 0))

    def total(self, span, zr, *others):
        rows = rows_of(span)
        total = self.S[zr * 4, rows, :].astype(f32)
        for dy in (1, 3, 2):
            total = total + self.RY[zr, dy, rows, :].astype(f32)
        for other in others:
            total = total + other[rows, :].astype(f32)
        return total

    def start_a(self):
        rows = rows_of(DEAL_CUT.ALLA)
        self.za = {dy: self.m.go(self.S.at[4 + dy, rows, :], self.RA.at[dy, rows, :], self.over)
                   for dy in (2, 1, 3, 0)}

    def start_b(self, zr):
        self.b[zr] = [self.ring(DEAL_CUT.ALLB, zr, dy) for dy in (2, 1, 3)]

    def start(self, sent):
        self.b = {}
        sent[0].wait_recv()
        self.multiply(DEAL_CUT.ALLA, 1)
        self.start_a()
        sent[1].wait_recv()
        self.multiply(DEAL_CUT.ALLB, 1)
        self.start_b(1)
        self.multiply(DEAL_CUT.ALLB, 0)
        self.start_b(0)
        self.multiply(DEAL_CUT.ALLA, 0)

    def middle(self):
        rows = rows_of(DEAL_CUT.ALLA)
        self.a = []
        for dy in (2, 1, 3):
            self.za[dy].wait_recv()
            total = self.S[dy, rows, :].astype(f32) + self.RA[dy, rows, :].astype(f32)
            self.S[dy, rows, :] = total.astype(bf16)
            self.a.append(self.ring(DEAL_CUT.ALLA, 0, dy))
        await_all(self.b[1])
        rows = rows_of(DEAL_CUT.ALLB)
        self.S[4, rows, :] = self.total(DEAL_CUT.ALLB, 1).astype(bf16)
        self.zb = self.m.go(self.S.at[4, rows, :], self.RZ.at[rows, :], self.over)

    def total_a(self):
        await_all([self.za[0]] + self.a)
        return self.total(DEAL_CUT.ALLA, 0, self.RA.at[0])

    def total_b(self):
        await_all(self.b[0] + [self.zb])
        return self.total(DEAL_CUT.ALLB, 0, self.RZ)


SCATTER_COPIES = 4 + 6 + 3 + 1
OTHERS = [(dx, dz) for dx in (2, 1, 3, 0) for dz in (1, 0) if (dx, dz) != (0, 0)]


def layer_kernel(lengths, gain1, gain2, tokens, token_lots_in, query, key, value, gate, out_weight, swish, up,
                 down_weight, out,
                 full1, squares, first, acc, qk, vg, retained, memory, decay, stats, gated,
                 quarter1, whole1, pack1, mate1, quarter2, whole2, pack2, mate2, second,
                 stage, wpar, wmate, lots, token_lots, pick, unpick, base, wide, full2, acc2, squares2, result, spare,
                 S1, RA1, RY1, RZ1, S2, RA2, RY2, RZ2,
                 local1, local2, load_sem, send, recv):
    place = Place()
    mover = Mover(send, recv)
    req = place.req
    cut = DEAL_CUT
    hand1 = Handout(place, mover, (query, key, value, gate), first, quarter1, whole1, pack1, mate1, local1)
    hand2 = Handout(place, mover, (swish, up), second, quarter2, whole2, pack2, mate2, local2)
    mine = column(place.me)

    def group(dx, dz):
        return ((place.x + dx + 4) % 4) * 2 + (place.zh + dz) % 2

    peers = group_peers(place) + [(group(dx, dz), place.me) for dx, dz in OTHERS]
    greet(peers)
    hand1.load()
    loads = [pltpu.make_async_copy(tokens, full1.at[:, mine], load_sem.at[0]),
             pltpu.make_async_copy(out_weight, stage.at[0], load_sem.at[1]),
             pltpu.make_async_copy(down_weight, stage.at[1], load_sem.at[2]),
             pltpu.make_async_copy(token_lots_in.at[:, 0], token_lots.at[req], load_sem.at[3])]
    for copy in loads:
        copy.start()
    hand2.load()
    mate_core = place.near(0, 0, 1)
    hand1.prepare()
    await_greetings(peers)
    hand1.share()
    loads[0].wait()
    gather = Gather(place, mover, full1, WIDE_CUT)
    hand1.prepare_whole()
    hand1.share_whole()

    head = place.me // 2
    log_decay, span_decay = jnp.float32(0.0), jnp.float32(0.0)
    for h in range(H):
        rate = 1.0 - 2.0 ** (-5 - h)
        log_decay = jnp.where(head == h, jnp.float32(math.log(rate)), log_decay)
        span_decay = jnp.where(head == h, jnp.float32(rate ** SPAN), span_decay)
    i = lax.broadcasted_iota(jnp.int32, (SPAN, SPAN), 0)
    j = lax.broadcasted_iota(jnp.int32, (SPAN, SPAN), 1)
    decay[0] = jnp.where(i >= j, jnp.exp((i - j).astype(f32) * log_decay), 0.0)
    decay[1] = jnp.exp((i + 1).astype(f32) * log_decay)
    decay[2] = jnp.exp((SPAN - 1 - i).astype(f32) * log_decay)

    order = [(dy, zr) for zr in (0, 1) for dy in range(4)]

    def set_weight(which):
        loads[1 + which].wait()
        for i, (dy, zr) in enumerate(order):
            wpar[which, 0:256, i * 128:(i + 1) * 128] = stage[which, :, column(place.member(dy, zr, 0))].astype(bf16)
            wmate[which, :, i * 128:(i + 1) * 128] = stage[which, :, column(place.member(dy, zr, 1))].astype(bf16)
        return mover.go(wmate.at[which], wpar.at[which, pl.ds(256, 256), :], mate_core)

    starts, counts = [], []
    start = jnp.int32(0)
    for r in range(8):
        length = lengths[r]
        turn = (req - r + 8) % 8
        count = 16 * (length // 128) + jnp.clip(length % 128 - 16 * turn, 0, 16)
        starts.append(start)
        counts.append(count)
        start = start + count

    def select():
        row = lax.broadcasted_iota(jnp.int32, (DEAL, 128), 0)
        lane = lax.broadcasted_iota(jnp.int32, (DEAL, 128), 1)
        slot = lax.broadcasted_iota(jnp.int32, (128, DEAL), 0)
        at = lax.broadcasted_iota(jnp.int32, (128, DEAL), 1)
        for r in range(8):
            chosen = (lane == row - starts[r]) & (lane < counts[r])
            pick[:, r * 128:(r + 1) * 128] = jnp.where(chosen, 1.0, 0.0).astype(bf16)
            chosen = (at == slot + starts[r]) & (slot < counts[r])
            unpick[r] = jnp.where(chosen, 1.0, 0.0).astype(bf16)

    def gained(rows, chips):
        total, square = None, None
        for chip in chips:
            depth = pl.ds(pl.multiple_of(chip * 256, 256), 256)
            values = full1[rows, depth].astype(f32)
            part = jnp.dot((values * gain1[:, depth]).astype(bf16), first[depth, :], preferred_element_type=f32)
            values = values * values
            values = values[:, :128] + values[:, 128:]
            total = part if total is None else total + part
            square = values if square is None else square + values
        return total, square

    def gather_product(rels, fresh=False):
        chips = [place.member(-dy, zr, 0) // 2 for dy, zr in rels]
        for dy, zr in rels:
            gather.ready(-dy, zr)

        def step(i, carry):
            rows = pl.ds(pl.multiple_of(i * SPAN, SPAN), SPAN)
            part, square = gained(rows, chips)
            acc[rows, :] = part if fresh else acc[rows, :] + part
            squares[rows, :] = square if fresh else squares[rows, :] + square
            return carry

        lax.fori_loop(0, LMAX // SPAN, step, 0)

    got1 = hand1.spread(range(4))
    gather.start_a()
    gather.start_b()
    hand2.prepare()
    got1 += hand1.spread(range(4, 12))
    hand2.prepare_whole()
    weights = [set_weight(0), set_weight(1)]
    gather.first()
    halves1 = hand1.onward(got1[:4])
    await_all(hand1.whole_sent[:1])
    gather_product([(0, 0)], True)
    gather.second()
    halves1 += hand1.onward(got1[4:8])
    await_all(hand1.whole_sent[1:])
    gather_product([(0, 1)])
    gather.third()
    halves1 += hand1.onward(got1[8:])
    hand2.share()
    hand2.share_whole()
    await_all(halves1[:8])
    gather_product([(1, 0), (3, 0)])
    await_all(halves1[8:16])
    gather_product([(1, 1), (3, 1)])
    await_all(halves1[16:20])
    gather_product([(2, 0)])
    gather.finish()
    await_all(halves1[20:])
    dealt_tokens = []
    for dx, dz in OTHERS:
        target = group(dx, dz)
        turn = (target - req + 8) % 8
        dealt_tokens.append(mover.go(token_lots_in.at[:, turn], token_lots.at[req], (target, place.me)))
    last_chip = [place.member(-2, 1, 0) // 2]
    key_scale = jnp.where(place.c == 0, 1.0, DK ** (-0.5))
    swapped = []

    def project(b):
        rows = pl.ds(b * SPAN, SPAN)
        total, square = gained(rows, last_chip)
        square = jnp.sum(squares[rows, :] + square, axis=1, keepdims=True)
        total = (acc[rows, :] + total) * lax.rsqrt(square * (1.0 / 2048) + epsilon)
        qk[place.c, rows, :] = (total[:, :256] * key_scale).astype(bf16)
        ref = qk.at[place.c, rows, :]
        swapped.append(mover.go(ref, ref, mate_core))
        vg[0, rows, :] = total[:, 256:512].astype(bf16)
        vg[1, rows, :] = total[:, 512:].astype(bf16)

    def attend(b):
        rows = pl.ds(b * SPAN, SPAN)
        swapped[b].wait_recv()
        query_block, key_block, value_block = qk[0, rows, :], qk[1, rows, :], vg[0, rows, :]
        scores = lax.dot_general(query_block, key_block, (((1,), (1,)), ((), ())), preferred_element_type=f32)
        total = jnp.dot((scores * decay[0]).astype(bf16), value_block, preferred_element_type=f32)
        if b > 0:
            across = jnp.dot(query_block, memory[...].astype(bf16), preferred_element_type=f32)
            total = total + across * decay[1]
        retained[rows, :] = total
        mean = jnp.sum(total, axis=1, keepdims=True) * (1.0 / 256)
        spread = total - mean
        square = jnp.sum(spread * spread, axis=1, keepdims=True)
        lanes = lax.broadcasted_iota(jnp.int32, (SPAN, 128), 1)
        stats[0, b] = jnp.where(lanes < 64, mean, square)
        told = mover.go(stats.at[0, b], stats.at[1, b], mate_core)
        if b < 3:
            decayed = (key_block.astype(f32) * decay[2]).astype(bf16)
            update = lax.dot_general(decayed, value_block, (((0,), (0,)), ((), ())), preferred_element_type=f32)
            memory[...] = update if b == 0 else memory[...] * span_decay + update
        return told

    def finish(b, told):
        rows = pl.ds(b * SPAN, SPAN)
        told.wait_recv()
        mean, square = stats[0, b, :, 0:1], stats[0, b, :, 64:65]
        mean2, square2 = stats[1, b, :, 0:1], stats[1, b, :, 64:65]
        gap = (mean - mean2) * 0.5
        middle = (mean + mean2) * 0.5
        var = (square + square2) * (1.0 / DV) + gap * gap
        grouped = (retained[rows, :] - middle) * lax.rsqrt(var + epsilon)
        gates = vg[1, rows, :].astype(f32)
        done = (gates / (1.0 + jnp.exp(-gates)) * grouped).astype(bf16)
        gated[2 * b:2 * b + 2] = done.reshape(2, 8, 16, 256)
        two = pl.ds(2 * b, 2)
        sent = []
        for dx, dz in OTHERS:
            target = group(dx, dz)
            turn = (target - req + 8) % 8
            sent.append(mover.go(gated.at[two, turn], lots.at[req, two], (target, place.me)))
        lots[req, 2 * b:2 * b + 2] = gated[2 * b:2 * b + 2, 0]
        return sent

    dealt, told = [], []
    project(0)
    for b in range(4):
        if b < 3:
            project(b + 1)
            if b == 0:
                got2 = hand2.spread(range(4))
        told.append(attend(b))
        if b > 0:
            dealt += finish(b - 1, told[b - 1])
    dealt += finish(3, told[3])
    loads[3].wait()
    select()
    got2 += hand2.spread(range(4, 12))
    await_all(dealt)
    sent = []
    for span in (cut.ALLA, cut.ALLB):
        rows = rows_of(span)
        part = jnp.dot(pick[rows, :], lots[...].reshape(LMAX, 256), preferred_element_type=f32)
        wide[0, rows, 0:256] = part.astype(bf16)
        ref = wide.at[0, rows, pl.ds(0, 256)]
        sent.append(mover.go(ref, wide.at[0, rows, pl.ds(256, 256)], mate_core))

    scatter = Scatter(place, mover, wide.at[0], wpar.at[0], (S1, RA1, RY1, RZ1))
    weights[0].wait_recv()
    scatter.start(sent)
    await_all(dealt_tokens)
    base[...] = jnp.dot(pick[...], token_lots[...].reshape(LMAX, BLK), preferred_element_type=f32).astype(bf16)
    halves2 = hand2.onward(got2[:8])
    scatter.middle()
    gather = DirectGather(place, mover, full2, cut)
    full2[rows_of(cut.ALLA), mine] = (base[rows_of(cut.ALLA), :].astype(f32) + scatter.total_a()).astype(bf16)
    gather.start_a()
    full2[rows_of(cut.ALLB), mine] = (base[rows_of(cut.ALLB), :].astype(f32) + scatter.total_b()).astype(bf16)
    gather.start_b()
    halves2 += hand2.onward(got2[8:])

    def forward(rows, zr):
        total, square = None, None
        for dy in range(4):
            depth = pl.ds(pl.multiple_of(place.member(dy, zr, 0) // 2 * 256, 256), 256)
            values = full2[rows, depth].astype(f32)
            part = jnp.dot((values * gain2[:, depth]).astype(bf16), second[depth, :], preferred_element_type=f32)
            values = values * values
            values = values[:, :128] + values[:, 128:]
            total = part if total is None else total + part
            square = values if square is None else square + values
        return total, square

    gather.near_side()
    await_all(halves2 + hand2.whole_sent)
    for span in (cut.ALLA, cut.ALLB):
        rows = rows_of(span)
        acc2[rows, :], squares2[rows, :] = forward(rows, 0)
    gather.far_side()
    sent = []
    for span in (cut.ALLA, cut.ALLB):
        rows = rows_of(span)
        part, square = forward(rows, 1)
        square = jnp.sum(squares2[rows, :] + square, axis=1, keepdims=True)
        part = (acc2[rows, :] + part) * lax.rsqrt(square * (1.0 / 2048) + epsilon)
        swished = part[:, :256]
        wide[1, rows, 0:256] = (swished / (1.0 + jnp.exp(-swished)) * part[:, 256:]).astype(bf16)
        ref = wide.at[1, rows, pl.ds(0, 256)]
        sent.append(mover.go(ref, wide.at[1, rows, pl.ds(256, 256)], mate_core))
    scatter = Scatter(place, mover, wide.at[1], wpar.at[1], (S2, RA2, RY2, RZ2))
    weights[1].wait_recv()
    scatter.start(sent)
    scatter.middle()
    for span, total in ((cut.ALLA, scatter.total_a), (cut.ALLB, scatter.total_b)):
        rows = rows_of(span)
        result[rows, :] = (full2[rows, mine].astype(f32) + total()).astype(bf16)
    returned = []
    for dx, dz in OTHERS:
        target = group(dx, dz)
        back = jnp.dot(unpick[target], result[...], preferred_element_type=f32)
        spare[target] = back.astype(bf16).reshape(8, 16, BLK)
        returned.append(mover.go(spare.at[target], out.at[:, (req - target + 8) % 8], (target, place.me)))
    back = jnp.dot(unpick[req], result[...], preferred_element_type=f32)
    out[:, 0] = back.astype(bf16).reshape(8, 16, BLK)
    await_all(returned)
    mover.drain()


LAYER_COPIES = 2 * HANDOUT_COPIES + GATHER_COPIES + DIRECT_COPIES + 2 * SCATTER_COPIES + 7 * 6 + 2 + 4 + 4 + 4


def layer(*operands):
    vmem = pl.BlockSpec(memory_space=pltpu.VMEM)
    hbm = pl.BlockSpec(memory_space=pl.ANY)
    sums = [
        pltpu.VMEM((8, DEAL, BLK), bf16),
        pltpu.VMEM((4, DEAL, BLK), bf16),
        pltpu.VMEM((2, 4, DEAL, BLK), bf16),
        pltpu.VMEM((DEAL, BLK), bf16),
    ]
    return pl.pallas_call(
        layer_kernel,
        name="layer",
        out_shape=jax.ShapeDtypeStruct((8, 8, 16, BLK), bf16),
        in_specs=[pl.BlockSpec(memory_space=pltpu.SMEM), vmem, vmem] + [hbm] * 10,
        out_specs=vmem,
        scratch_shapes=[
            pltpu.VMEM((LMAX, 2048), bf16),
            pltpu.VMEM((LMAX, 128), f32),
            pltpu.VMEM((2048, 768), bf16),
            pltpu.VMEM((LMAX, 768), f32),
            pltpu.VMEM((2, LMAX, 256), bf16),
            pltpu.VMEM((2, LMAX, 256), bf16),

            pltpu.VMEM((LMAX, 256), f32),
            pltpu.VMEM((256, 256), f32),
            pltpu.VMEM((3, SPAN, SPAN), f32),
            pltpu.VMEM((2, 4, SPAN, 128), f32),
            pltpu.VMEM((8, 8, 16, 256), bf16),
            pltpu.VMEM((32, 12288), f32),
            pltpu.VMEM((2, 128, 1536), f32),
            pltpu.VMEM((16, 32, 768), bf16),
            pltpu.VMEM((3, 128, 768), bf16),
            pltpu.VMEM((32, 8192), f32),
            pltpu.VMEM((2, 128, 1024), f32),
            pltpu.VMEM((16, 32, 512), bf16),
            pltpu.VMEM((3, 128, 512), bf16),
            pltpu.VMEM((2048, 512), bf16),
            pltpu.VMEM((2, 256, 2048), f32),
            pltpu.VMEM((2, 512, 1024), bf16),
            pltpu.VMEM((2, 256, 1024), bf16),
            pltpu.VMEM((8, 8, 16, 256), bf16),
            pltpu.VMEM((8, 8, 16, BLK), bf16),
            pltpu.VMEM((DEAL, LMAX), bf16),
            pltpu.VMEM((8, 128, DEAL), bf16),
            pltpu.VMEM((DEAL, BLK), bf16),
            pltpu.VMEM((2, DEAL, 512), bf16),
            pltpu.VMEM((DEAL, 2048), bf16),
            pltpu.VMEM((DEAL, 512), f32),
            pltpu.VMEM((DEAL, 128), f32),
            pltpu.VMEM((DEAL, BLK), bf16),
            pltpu.VMEM((8, 8, 16, BLK), bf16),
        ] + sums + sums + [
            pltpu.SemaphoreType.DMA((12,)),
            pltpu.SemaphoreType.DMA((6,)),
            pltpu.SemaphoreType.DMA((4,)),
            pltpu.SemaphoreType.DMA((LAYER_COPIES,)),
            pltpu.SemaphoreType.DMA((LAYER_COPIES,)),
        ],
        compiler_params=pltpu.CompilerParams(
            collective_id=0, has_side_effects=True, vmem_limit_bytes=63 * 2**20
        ),
    )(*operands)


def body(
    tokens,
    lengths,
    retention_gain,
    forward_gain,
    query_weight,
    key_weight,
    value_weight,
    gate_weight,
    output_weight,
    swish_weight,
    up_weight,
    down_weight,
):
    rows = tokens.reshape(8, 8, 16, BLK)
    finished = layer(
        lengths, retention_gain.reshape(1, 2048), forward_gain.reshape(1, 2048), tokens[0], rows,
        query_weight, key_weight, value_weight, gate_weight, output_weight, swish_weight, up_weight, down_weight
    )
    return finished.reshape(1, LMAX, BLK)


def solution(mesh):
    placed = (
        P("req", None, "mlp"),
        P(),
        P(),
        P(),
        P("mlp", None),
        P("mlp", None),
        P("mlp", None),
        P("mlp", None),
        P("mlp", None),
        P("mlp", None),
        P("mlp", None),
        P("mlp", None),
    )
    return jax.shard_map(
        body, mesh=mesh, in_specs=placed, out_specs=P("req", None, "mlp"), check_vma=False
    )
```
